32 devices in a mesh: tok: 8 (over z, x), mdl: 4 (over y, core).
Axes of the slice: x: 2, y: 2, z: 4, core: 2. Of those that a mesh axis runs over, the one named last changes fastest.
Arguments:
- tokens: bfloat16 [4, 4096, 768], P('mdl', 'tok'), may hold values from -6 to 6
- cotangent: bfloat16 [4, 4096, 768], P('mdl', 'tok'), may hold values from -6 to 6
- starts: int32 [4, 4], P('mdl'), may hold values from 0 to 3840, as said below
- w_qkv: float32 [768, 2304], P(('tok', 'mdl')), may hold values from -0.21875 to 0.21875
- b_query: float32 [768], P(('tok', 'mdl')), may hold values from -3 to 3
- b_value: float32 [768], P(('tok', 'mdl')), may hold values from -3 to 3
- w_out: float32 [768, 768], P(('tok', 'mdl')), may hold values from -6 to 6
- b_out: float32 [768], P(('tok', 'mdl')), may hold values from -2 to 2
- gain_one: float32 [768], P(('tok', 'mdl')), may hold values from 0.5 to 1.5
- shift_one: float32 [768], P(('tok', 'mdl')), may hold values from -2 to 2
- gain_two: float32 [768], P(('tok', 'mdl')), may hold values from 0.5 to 1.5
- shift_two: float32 [768], P(('tok', 'mdl')), may hold values from -2 to 2
- w_expand: float32 [768, 3072], P(('tok', 'mdl')), may hold values from -0.21875 to 0.21875
- b_expand: float32 [3072], P(('tok', 'mdl')), may hold values from -3 to 3
- w_shrink: float32 [3072, 768], P(('tok', 'mdl')), may hold values from -0.109375 to 0.109375
- b_shrink: float32 [768], P(('tok', 'mdl')), may hold values from -2 to 2
Outputs:
- layer_out: bfloat16 [4, 4096, 768], P('mdl', 'tok')
- dtokens: float32 [4, 4096, 768], P('mdl', 'tok')
- dw_qkv: float32 [768, 2304], P(('tok', 'mdl'))
- db_query: float32 [768], P(('tok', 'mdl'))
- db_value: float32 [768], P(('tok', 'mdl'))
- dw_out: float32 [768, 768], P(('tok', 'mdl'))
- db_out: float32 [768], P(('tok', 'mdl'))
- dgain_one: float32 [768], P(('tok', 'mdl'))
- dshift_one: float32 [768], P(('tok', 'mdl'))
- dgain_two: float32 [768], P(('tok', 'mdl'))
- dshift_two: float32 [768], P(('tok', 'mdl'))
- dw_expand: float32 [768, 3072], P(('tok', 'mdl'))
- db_expand: float32 [3072], P(('tok', 'mdl'))
- dw_shrink: float32 [3072, 768], P(('tok', 'mdl'))
- db_shrink: float32 [768], P(('tok', 'mdl'))
The draws below stay inside these ranges and needn't reach their ends.
Inputs may be any that keep to these rules, and one draw needn't show every extreme that they name: Piece p of a sequence starts within the p-th of 4 equal parts of the sequence (parts of 1024 positions) and ends inside that part, so pieces of a sequence never intersect; each sequence has 4 pieces.
All inputs are finite; a program needn't handle non-finite values.
Results may differ from the reference program's by a relative error of at most 0.013.
The reference program's roundings to bfloat16 on the way count: a program that leaves them out, or rounds other values in their place, can miss the bound.
Values may be sent and summed in bfloat16 or wider, within the bound.
A program may use at most 192 MiB of HBM per device.

```python
import jax
import jax.numpy as jnp
from jax import lax

D = 768
H = 12
HD = 64
FF = 3072
SEQ = 4096
PIECE = 256
KEYB = 512
NSEQ = 4
NPIECE = 4


def draw_starts(key, part):
    slot_len = SEQ // NPIECE
    offsets = jax.random.randint(key, (NSEQ, NPIECE), 0, slot_len - PIECE + 1, dtype=jnp.int32)
    offsets = offsets.at[0, 0].set(0)
    offsets = offsets.at[NSEQ - 1, NPIECE - 1].set(slot_len - PIECE)
    slot_begin = jnp.arange(NPIECE, dtype=jnp.int32) * slot_len
    return offsets + slot_begin[None, :]


def shard_levels(stream_key, shape, split, low, top_value):
    factor_of, own = 1.0, jax.random.fold_in(stream_key, 6)
    for position, blocks in split:
        steps = jnp.exp(jax.random.uniform(jax.random.fold_in(own, position), (blocks,), jnp.float32, low / len(split), top_value / len(split)))
        factor_of = factor_of * jnp.repeat(steps, shape[position] // blocks).reshape([-1 if axis == position else 1 for axis in range(len(shape))])
    return factor_of


def bell_draw(stream_key, shape, width, most, shards=(), kind=jnp.bfloat16):
    entries = jax.random.normal(stream_key, shape, jnp.float32) * width
    if len(shards) > 0:
        entries = shard_levels(stream_key, shape, shards, -0.22, 0.18) * entries
    return jnp.clip(entries, min=-most, max=most).astype(kind)


def setup_inputs(seed: int = 0) -> dict:
    streams_of = jax.random.split(jax.random.key(seed), 17)
    tokens = bell_draw(streams_of[0], (NSEQ, SEQ, D), 1.0, 6.0, ((0, 4), (1, 8)))
    cotangent = bell_draw(streams_of[1], (NSEQ, SEQ, D), 1.0, 6.0, ((0, 4), (1, 8)))
    starts = draw_starts(jax.random.fold_in(streams_of[16], 71), 0)
    w_qkv = bell_draw(streams_of[3], (D, 3 * D), D ** -0.5, 0.21875, ((0, 32),), jnp.float32)
    b_query = bell_draw(streams_of[4], (D,), 0.5, 3.0, ((0, 32),), jnp.float32)
    b_value = bell_draw(streams_of[5], (D,), 0.5, 3.0, ((0, 32),), jnp.float32)
    w_out = bell_draw(streams_of[6], (D, D), (max(1, 4 * D // SEQ)) ** -0.5, 6.0, ((0, 32),), jnp.float32)
    b_out = bell_draw(streams_of[7], (D,), 0.3, 2.0, ((0, 32),), jnp.float32)
    gain_one = jnp.clip(1.0 + 0.1 * jax.random.normal(streams_of[8], (D,), jnp.float32), 0.5, 1.5)
    shift_one = bell_draw(streams_of[9], (D,), 0.3, 2.0, ((0, 32),), jnp.float32)
    gain_two = jnp.clip(1.0 + 0.1 * jax.random.normal(streams_of[10], (D,), jnp.float32), 0.5, 1.5)
    shift_two = bell_draw(streams_of[11], (D,), 0.3, 2.0, ((0, 32),), jnp.float32)
    w_expand = bell_draw(streams_of[12], (D, FF), D ** -0.5, 0.21875, ((0, 32),), jnp.float32)
    b_expand = bell_draw(streams_of[13], (FF,), 0.5, 3.0, ((0, 32),), jnp.float32)
    w_shrink = bell_draw(streams_of[14], (FF, D), FF ** -0.5, 0.109375, ((0, 32),), jnp.float32)
    b_shrink = bell_draw(streams_of[15], (D,), 0.3, 2.0, ((0, 32),), jnp.float32)
    return dict(tokens=tokens, cotangent=cotangent, starts=starts, w_qkv=w_qkv, b_query=b_query, b_value=b_value, w_out=w_out, b_out=b_out, gain_one=gain_one, shift_one=shift_one, gain_two=gain_two, shift_two=shift_two, w_expand=w_expand, b_expand=b_expand, w_shrink=w_shrink, b_shrink=b_shrink)


epsilon = 1e-05
masked_score = -1e+30
gelu_coeff = 0.7978845608028654

@jax.custom_vjp
def low(v):
    return lax.optimization_barrier(v.astype(jnp.bfloat16)).astype(jnp.float32)

@jax.custom_vjp
def low_back(v):
    return v

def low_keep(v):
    return (low(v), None)

def low_pass(kept, grad):
    return (grad,)

def back_keep(v):
    return (v, None)

def back_low(kept, grad):
    return (low(grad),)
low.defvjp(low_keep, low_pass)
low_back.defvjp(back_keep, back_low)

def matmul_high(left, right):
    return jnp.dot(left, right, precision=lax.Precision.HIGHEST)

def layer_norm(values, gain_vec, shift_vec):
    center = values - lax.optimization_barrier(jnp.mean(values, axis=-1, keepdims=True))
    spread = lax.optimization_barrier(jnp.mean(center * center, axis=-1, keepdims=True))
    return center * lax.rsqrt(spread + epsilon) * gain_vec + shift_vec

def gelu_tanh(inputs):
    return 0.5 * inputs * (1.0 + jnp.tanh(gelu_coeff * (inputs + 0.044715 * inputs * inputs * inputs)))

def piece_ids(begins, positions):
    inside = (positions[:, None] >= begins[None, :]) & (positions[:, None] < begins[None, :] + PIECE)
    labels = jnp.arange(1, begins.shape[0] + 1, dtype=jnp.int32)
    return lax.optimization_barrier(jnp.sum(jnp.where(inside, labels[None, :], 0), axis=1)).astype(jnp.int32) - 1

def sequence_forward(inputs, begins, params):
    w_qkv, b_query, b_value, w_out, b_out, gain_one, shift_one, gain_two, shift_two, w_expand, b_expand, w_shrink, b_shrink = [low(master) for master in params]
    normed = low(layer_norm(inputs, gain_one, shift_one))
    joined = matmul_high(normed, w_qkv)
    queries = low(low_back(joined[:, :D] + b_query))
    keys_all = low(low_back(joined[:, D:2 * D]))
    values_all = low(low_back(joined[:, 2 * D:] + b_value))
    positions = jnp.arange(SEQ, dtype=jnp.int32)
    labels = piece_ids(begins, positions)
    key_heads = keys_all.reshape(SEQ, H, HD)
    value_heads = values_all.reshape(SEQ, H, HD)
    scaling = HD ** (-0.5)

    def attend(blockset):
        query_block, query_pos, query_lab = blockset
        scores = jnp.einsum('qhd,khd->hqk', query_block, key_heads, precision=lax.Precision.HIGHEST) * scaling
        scores = low_back(scores)
        allowed = (positions[None, :] <= query_pos[:, None]) | (labels[None, :] == query_lab[:, None]) & (query_lab[:, None] >= 0)
        masked = jnp.where(allowed[None, :, :], scores, masked_score)
        highest = lax.optimization_barrier(jnp.max(masked, axis=-1, keepdims=True))
        exponent = jnp.exp(masked - highest)
        probabilities = low(exponent / lax.optimization_barrier(jnp.sum(exponent, axis=-1, keepdims=True)))
        mixture = jnp.einsum('hqk,khd->qhd', probabilities, value_heads, precision=lax.Precision.HIGHEST)
        return mixture.reshape(query_block.shape[0], D)
    block_count = SEQ // KEYB
    attended = lax.map(jax.checkpoint(attend), (queries.reshape(block_count, KEYB, H, HD), positions.reshape(block_count, KEYB), labels.reshape(block_count, KEYB)))
    attention = low(low_back(attended.reshape(SEQ, D)))
    branch_one = low_back(matmul_high(attention, w_out) + b_out)
    hidden_one = inputs + branch_one
    normed_two = low(layer_norm(hidden_one, gain_two, shift_two))
    expanded = low_back(matmul_high(normed_two, w_expand) + b_expand)
    activated = low(gelu_tanh(expanded))
    branch_two = low_back(matmul_high(activated, w_shrink) + b_shrink)
    return hidden_one + branch_two

def reference(tokens, cotangent, starts, w_qkv, b_query, b_value, w_out, b_out, gain_one, shift_one, gain_two, shift_two, w_expand, b_expand, w_shrink, b_shrink):
    params = (w_qkv, b_query, b_value, w_out, b_out, gain_one, shift_one, gain_two, shift_two, w_expand, b_expand, w_shrink, b_shrink)
    inputs = tokens.astype(jnp.float32)
    upstream = cotangent.astype(jnp.float32)

    def one_sequence(running, element):
        seq_in, seq_up, begins = element

        def forward(values, masters):
            return sequence_forward(values, begins, masters)
        result, pullback = jax.vjp(forward, seq_in, params)
        grad_in, grad_params = pullback(seq_up)
        running = jax.tree.map(lambda summed_grad, addend: summed_grad + addend, running, grad_params)
        return (running, (result.astype(jnp.bfloat16), grad_in))
    initial = jax.tree.map(jnp.zeros_like, params)
    gradients, (outputs, input_grads) = lax.scan(one_sequence, initial, (inputs, upstream, starts))
    return (outputs, input_grads, gradients[0], gradients[1], gradients[2], gradients[3], gradients[4], gradients[5], gradients[6], gradients[7], gradients[8], gradients[9], gradients[10], gradients[11], gradients[12])
```

```python
import functools
import math

import jax
import jax.numpy as jnp
from jax import lax
from jax.experimental import pallas as pl
from jax.experimental.pallas import tpu as pltpu
from jax.sharding import PartitionSpec as P

HD = 64
PIECE = 256
KEYB = 512


epsilon = 1e-05
masked_score = -1e30
gelu_coeff = 0.7978845608028654


def layer_norm(values, gain_vec, shift_vec):
    center = values - jnp.mean(values, axis=-1, keepdims=True)
    spread = jnp.mean(center * center, axis=-1, keepdims=True)
    return center * lax.rsqrt(spread + epsilon) * gain_vec + shift_vec


def gelu_tanh(inputs):
    return (
        0.5 * inputs * (1.0 + jnp.tanh(gelu_coeff * (inputs + 0.044715 * inputs * inputs * inputs)))
    )


def piece_ids(begins, positions):
    inside = (positions[:, None] >= begins[None, :]) & (
        positions[:, None] < begins[None, :] + PIECE
    )
    labels = jnp.arange(1, begins.shape[0] + 1, dtype=jnp.int32)
    return jnp.sum(jnp.where(inside, labels[None, :], 0), axis=1) - 1


def block_scores(query_heads, key_heads, query_pos, query_lab, begins, block_index, scaling):
    key_block = lax.dynamic_slice_in_dim(key_heads, block_index * KEYB, KEYB, 0)
    key_pos = block_index * KEYB + jnp.arange(KEYB, dtype=jnp.int32)
    key_lab = piece_ids(begins, key_pos)
    scores = (
        jnp.einsum("qhd,khd->hqk", query_heads, key_block, preferred_element_type=jnp.float32)
        * scaling
    )
    allowed = (key_pos[None, :] <= query_pos[:, None]) | (
        key_lab[None, :] == query_lab[:, None]
    ) & (query_lab[:, None] >= 0)
    return jnp.where(allowed[None, :, :], scores, masked_score)


def attend_forward(
    query_heads, key_heads, value_heads, query_pos, query_lab, begins, needed, scaling
):
    local_rows = query_heads.shape[0]
    head_count = query_heads.shape[1]

    def stats_step(block_index, loop_state):
        highest, summed = loop_state
        masked = block_scores(
            query_heads, key_heads, query_pos, query_lab, begins, block_index, scaling
        )
        new_high = jnp.maximum(highest, jnp.max(masked, axis=-1))
        summed = summed * jnp.exp(highest - new_high) + jnp.sum(
            jnp.exp(masked - new_high[:, :, None]), axis=-1
        )
        return (new_high, summed)

    starting = (
        jnp.full((head_count, local_rows), masked_score, jnp.float32),
        jnp.zeros((head_count, local_rows), jnp.float32),
    )
    highest, summed = lax.fori_loop(0, needed, stats_step, starting)

    def mix_step(block_index, running):
        masked = block_scores(
            query_heads, key_heads, query_pos, query_lab, begins, block_index, scaling
        )
        prob_low = (jnp.exp(masked - highest[:, :, None]) / summed[:, :, None]).astype(jnp.bfloat16)
        value_block = lax.dynamic_slice_in_dim(value_heads, block_index * KEYB, KEYB, 0)
        return running + jnp.einsum(
            "hqk,khd->qhd", prob_low, value_block, preferred_element_type=jnp.float32
        )

    mixture = lax.fori_loop(0, needed, mix_step, jnp.zeros(query_heads.shape, jnp.float32))
    return (mixture, highest, summed)


def attend_backward(
    query_heads,
    key_heads,
    value_heads,
    grad_heads,
    mixture,
    query_pos,
    query_lab,
    begins,
    needed,
    highest,
    summed,
    scaling,
):
    row_delta = jnp.einsum("qhd,qhd->hq", grad_heads.astype(jnp.float32), mixture)

    def grad_step(block_index, loop_state):
        grad_query, grad_keys, grad_values = loop_state
        masked = block_scores(
            query_heads, key_heads, query_pos, query_lab, begins, block_index, scaling
        )
        prob_full = jnp.exp(masked - highest[:, :, None]) / summed[:, :, None]
        offset = block_index * KEYB
        value_block = lax.dynamic_slice_in_dim(value_heads, offset, KEYB, 0)
        grad_probs = jnp.einsum(
            "qhd,khd->hqk", grad_heads, value_block, preferred_element_type=jnp.float32
        )
        grad_scores = (prob_full * (grad_probs - row_delta[:, :, None])).astype(jnp.bfloat16)
        key_block = lax.dynamic_slice_in_dim(key_heads, offset, KEYB, 0)
        grad_query = (
            grad_query
            + jnp.einsum("hqk,khd->qhd", grad_scores, key_block, preferred_element_type=jnp.float32)
            * scaling
        )
        key_part = (
            jnp.einsum("hqk,qhd->khd", grad_scores, query_heads, preferred_element_type=jnp.float32)
            * scaling
        )
        value_part = jnp.einsum(
            "hqk,qhd->khd",
            prob_full.astype(jnp.bfloat16),
            grad_heads,
            preferred_element_type=jnp.float32,
        )
        grad_keys = lax.dynamic_update_slice_in_dim(
            grad_keys, lax.dynamic_slice_in_dim(grad_keys, offset, KEYB, 0) + key_part, offset, 0
        )
        grad_values = lax.dynamic_update_slice_in_dim(
            grad_values,
            lax.dynamic_slice_in_dim(grad_values, offset, KEYB, 0) + value_part,
            offset,
            0,
        )
        return (grad_query, grad_keys, grad_values)

    starting = (
        jnp.zeros(query_heads.shape, jnp.float32),
        jnp.zeros(key_heads.shape, jnp.float32),
        jnp.zeros(value_heads.shape, jnp.float32),
    )
    return lax.fori_loop(0, needed, grad_step, starting)


def general(
    tokens,
    cotangent,
    starts,
    w_qkv,
    b_query,
    b_value,
    w_out,
    b_out,
    gain_one,
    shift_one,
    gain_two,
    shift_two,
    w_expand,
    b_expand,
    w_shrink,
    b_shrink,
):
    (
        full_qkv,
        full_bq,
        full_bv,
        full_out,
        full_bo,
        full_gone,
        full_sone,
        full_gtwo,
        full_stwo,
        full_expand,
        full_bexp,
        full_shrink,
        full_bshr,
    ) = (
        lax.all_gather(w_qkv.astype(jnp.bfloat16), ("tok", "mdl"), axis=0, tiled=True),
        lax.all_gather(b_query.astype(jnp.bfloat16), ("tok", "mdl"), axis=0, tiled=True),
        lax.all_gather(b_value.astype(jnp.bfloat16), ("tok", "mdl"), axis=0, tiled=True),
        lax.all_gather(w_out.astype(jnp.bfloat16), ("tok", "mdl"), axis=0, tiled=True),
        lax.all_gather(b_out.astype(jnp.bfloat16), ("tok", "mdl"), axis=0, tiled=True),
        lax.all_gather(gain_one.astype(jnp.bfloat16), ("tok", "mdl"), axis=0, tiled=True),
        lax.all_gather(shift_one.astype(jnp.bfloat16), ("tok", "mdl"), axis=0, tiled=True),
        lax.all_gather(gain_two.astype(jnp.bfloat16), ("tok", "mdl"), axis=0, tiled=True),
        lax.all_gather(shift_two.astype(jnp.bfloat16), ("tok", "mdl"), axis=0, tiled=True),
        lax.all_gather(w_expand.astype(jnp.bfloat16), ("tok", "mdl"), axis=0, tiled=True),
        lax.all_gather(b_expand.astype(jnp.bfloat16), ("tok", "mdl"), axis=0, tiled=True),
        lax.all_gather(w_shrink.astype(jnp.bfloat16), ("tok", "mdl"), axis=0, tiled=True),
        lax.all_gather(b_shrink.astype(jnp.bfloat16), ("tok", "mdl"), axis=0, tiled=True),
    )
    query_bias = full_bq.astype(jnp.float32)
    value_bias = full_bv.astype(jnp.float32)
    out_bias = full_bo.astype(jnp.float32)
    gain_first = full_gone.astype(jnp.float32)
    shift_first = full_sone.astype(jnp.float32)
    gain_second = full_gtwo.astype(jnp.float32)
    shift_second = full_stwo.astype(jnp.float32)
    expand_bias = full_bexp.astype(jnp.float32)
    shrink_bias = full_bshr.astype(jnp.float32)
    local_rows = tokens.shape[1]
    model_width = tokens.shape[2]
    head_count = model_width // HD
    group_size = lax.axis_size("tok")
    member = lax.axis_index("tok")
    seq_len = local_rows * group_size
    scaling = HD ** (-0.5)
    needed = jnp.minimum(
        seq_len // KEYB, ((member + 1) * local_rows + PIECE - 1 + KEYB - 1) // KEYB
    )
    begins = starts[0]
    query_pos = member * local_rows + jnp.arange(local_rows, dtype=jnp.int32)
    query_lab = piece_ids(begins, query_pos)
    token_rows = tokens[0]
    cotangent_rows = cotangent[0]
    inputs = token_rows.astype(jnp.float32)
    normed = layer_norm(inputs, gain_first, shift_first).astype(jnp.bfloat16)
    joined = jnp.dot(normed, full_qkv, preferred_element_type=jnp.float32)
    queries = (joined[:, :model_width] + query_bias).astype(jnp.bfloat16)
    keys_own = joined[:, model_width : 2 * model_width].astype(jnp.bfloat16)
    values_own = (joined[:, 2 * model_width :] + value_bias).astype(jnp.bfloat16)
    key_full, value_full = (
        lax.all_gather(keys_own, "tok", axis=0, tiled=True),
        lax.all_gather(values_own, "tok", axis=0, tiled=True),
    )
    query_heads = queries.reshape(local_rows, head_count, HD)
    mixture, highest, summed = attend_forward(
        query_heads,
        key_full.reshape(seq_len, head_count, HD),
        value_full.reshape(seq_len, head_count, HD),
        query_pos,
        query_lab,
        begins,
        needed,
        scaling,
    )
    attention = mixture.reshape(local_rows, model_width).astype(jnp.bfloat16)
    hidden_one = inputs + (
        jnp.dot(attention, full_out, preferred_element_type=jnp.float32) + out_bias
    )
    normed_two = layer_norm(hidden_one, gain_second, shift_second).astype(jnp.bfloat16)
    expanded = jnp.dot(normed_two, full_expand, preferred_element_type=jnp.float32) + expand_bias
    activated = gelu_tanh(expanded).astype(jnp.bfloat16)
    layer_out = hidden_one + (
        jnp.dot(activated, full_shrink, preferred_element_type=jnp.float32) + shrink_bias
    )
    upstream = cotangent_rows.astype(jnp.float32)
    db_shrink = jnp.sum(upstream, axis=0)
    dw_shrink = jnp.einsum(
        "rf,rd->fd", activated, cotangent_rows, preferred_element_type=jnp.float32
    )
    grad_act = jnp.einsum(
        "rd,fd->rf", cotangent_rows, full_shrink, preferred_element_type=jnp.float32
    )
    gelu_pull = jax.vjp(gelu_tanh, expanded)[1]
    grad_expand = gelu_pull(grad_act)[0].astype(jnp.bfloat16)
    db_expand = jnp.sum(grad_expand.astype(jnp.float32), axis=0)
    dw_expand = jnp.einsum("rd,rf->df", normed_two, grad_expand, preferred_element_type=jnp.float32)
    grad_normed_two = jnp.einsum(
        "rf,df->rd", grad_expand, full_expand, preferred_element_type=jnp.float32
    )
    norm_pull = jax.vjp(layer_norm, hidden_one, gain_second, shift_second)[1]
    grad_hidden_part, dgain_two, dshift_two = norm_pull(grad_normed_two)
    grad_hidden = upstream + grad_hidden_part
    grad_attn = grad_hidden.astype(jnp.bfloat16)
    db_out = jnp.sum(grad_attn.astype(jnp.float32), axis=0)
    dw_out = jnp.einsum("rd,re->de", attention, grad_attn, preferred_element_type=jnp.float32)
    grad_mix = jnp.einsum(
        "re,de->rd", grad_attn, full_out, preferred_element_type=jnp.float32
    ).astype(jnp.bfloat16)
    key_back, value_back = (key_full, value_full)
    grad_query, grad_keys, grad_values = attend_backward(
        query_heads,
        key_back.reshape(seq_len, head_count, HD),
        value_back.reshape(seq_len, head_count, HD),
        grad_mix.reshape(local_rows, head_count, HD),
        mixture,
        query_pos,
        query_lab,
        begins,
        needed,
        highest,
        summed,
        scaling,
    )
    key_share, value_share = (
        lax.psum_scatter(
            grad_keys.reshape(seq_len, model_width).astype(jnp.bfloat16),
            "tok",
            scatter_dimension=0,
            tiled=True,
        ).astype(jnp.float32),
        lax.psum_scatter(
            grad_values.reshape(seq_len, model_width).astype(jnp.bfloat16),
            "tok",
            scatter_dimension=0,
            tiled=True,
        ).astype(jnp.float32),
    )
    grad_joined = jnp.concatenate(
        [
            grad_query.reshape(local_rows, model_width).astype(jnp.bfloat16),
            key_share.astype(jnp.bfloat16),
            value_share.astype(jnp.bfloat16),
        ],
        axis=1,
    )
    db_query = jnp.sum(grad_joined[:, :model_width].astype(jnp.float32), axis=0)
    db_value = jnp.sum(grad_joined[:, 2 * model_width :].astype(jnp.float32), axis=0)
    dw_qkv = jnp.einsum("rd,re->de", normed, grad_joined, preferred_element_type=jnp.float32)
    grad_normed = jnp.einsum("re,de->rd", grad_joined, full_qkv, preferred_element_type=jnp.float32)
    norm_pull_first = jax.vjp(layer_norm, inputs, gain_first, shift_first)[1]
    grad_input_part, dgain_one, dshift_one = norm_pull_first(grad_normed)
    dtokens = grad_hidden + grad_input_part
    (
        dw_qkv,
        db_query,
        db_value,
        dw_out,
        db_out,
        dgain_one,
        dshift_one,
        dgain_two,
        dshift_two,
        dw_expand,
        db_expand,
        dw_shrink,
        db_shrink,
    ) = (
        lax.psum_scatter(dw_qkv, ("tok", "mdl"), scatter_dimension=0, tiled=True),
        lax.psum_scatter(db_query, ("tok", "mdl"), scatter_dimension=0, tiled=True),
        lax.psum_scatter(db_value, ("tok", "mdl"), scatter_dimension=0, tiled=True),
        lax.psum_scatter(dw_out, ("tok", "mdl"), scatter_dimension=0, tiled=True),
        lax.psum_scatter(db_out, ("tok", "mdl"), scatter_dimension=0, tiled=True),
        lax.psum_scatter(dgain_one, ("tok", "mdl"), scatter_dimension=0, tiled=True),
        lax.psum_scatter(dshift_one, ("tok", "mdl"), scatter_dimension=0, tiled=True),
        lax.psum_scatter(dgain_two, ("tok", "mdl"), scatter_dimension=0, tiled=True),
        lax.psum_scatter(dshift_two, ("tok", "mdl"), scatter_dimension=0, tiled=True),
        lax.psum_scatter(dw_expand, ("tok", "mdl"), scatter_dimension=0, tiled=True),
        lax.psum_scatter(db_expand, ("tok", "mdl"), scatter_dimension=0, tiled=True),
        lax.psum_scatter(dw_shrink, ("tok", "mdl"), scatter_dimension=0, tiled=True),
        lax.psum_scatter(db_shrink, ("tok", "mdl"), scatter_dimension=0, tiled=True),
    )
    return (
        layer_out.astype(jnp.bfloat16).reshape(1, local_rows, model_width),
        dtokens.reshape(1, local_rows, model_width),
        dw_qkv,
        db_query,
        db_value,
        dw_out,
        db_out,
        dgain_one,
        dshift_one,
        dgain_two,
        dshift_two,
        dw_expand,
        db_expand,
        dw_shrink,
        db_shrink,
    )


BLK = 512

C2 = math.log2(math.e) * HD ** -0.5
NEG=-1e30
F32=jnp.float32; BF=jnp.bfloat16

def task_index(u, role):
    slot = (u >= 8).astype(jnp.int32)
    n = u - 8
    i_sh = 2 * n + ((n % 2) + role) % 2
    return slot, jnp.where(u >= 8, i_sh, u)

def nn(a,b): return lax.dot_general(a,b,(((1,),(0,)),((),())),preferred_element_type=F32)
def nt(a,b): return lax.dot_general(a,b,(((1,),(1,)),((),())),preferred_element_type=F32)

def piece_mask(k0, q0, nk, nq, s):
    kp = k0 + lax.broadcasted_iota(jnp.int32, (nk, nq), 0)
    qp = q0 + lax.broadcasted_iota(jnp.int32, (nk, nq), 1)
    kc = k0 + lax.broadcasted_iota(jnp.int32, (nk, 1), 0)
    qr = q0 + lax.broadcasted_iota(jnp.int32, (1, nq), 1)
    kin = ((kc >= s) & (kc < s + PIECE)).astype(F32)
    qin = ((qr >= s) & (qr < s + PIECE)).astype(F32)
    return kp, qp, (kin * qin) > 0.5

def fwd_kernel(nb, role_fn, starts_ref, x_ref, o_ref, of_ref, l_ref, kn, acc, ms, ls):
    role = role_fn()
    for s in range(2):
        for j in range(nb):
            kn[s, j] = x_ref[s, j, 1].T
    def tile(slot, j, i, k0, nk, q0, nq, mask):
        q = x_ref[slot, i, 0, :, q0:q0+nq]
        k = kn[slot, j, k0:k0+nk, :]
        s2 = nn(k, q) * C2
        if mask is not None:
            st = starts_ref[slot, i // 2]
            kp, qp, pin = piece_mask(j * BLK + k0, i * BLK + q0, nk, nq, st)
            ok = pin if mask == "piece" else (kp <= qp) | pin
            s2 = jnp.where(ok, s2, NEG)
        m_old = ms[:, q0:q0+nq]
        m_new = jnp.maximum(m_old, jnp.max(s2, axis=0, keepdims=True))
        a = jnp.exp2(m_old - m_new)
        p = jnp.exp2(s2 - m_new)
        ls[:, q0:q0+nq] = ls[:, q0:q0+nq] * a + jnp.sum(p, axis=0, keepdims=True)
        v = x_ref[slot, j, 2, :, k0:k0+nk]
        acc[:, q0:q0+nq] = acc[:, q0:q0+nq] * a + nn(v, p.astype(BF))
        ms[:, q0:q0+nq] = m_new
    def task(u, _):
        slot, i = task_index(u, role)
        ms[...] = jnp.full_like(ms, NEG); ls[...] = jnp.zeros_like(ls); acc[...] = jnp.zeros_like(acc)
        def inner(j, _):
            tile(slot, j, i, 0, BLK, 0, BLK, None); return 0
        lax.fori_loop(0, i, inner, 0)
        tile(slot, i, i, 0, BLK, 0, BLK, "diag")
        @pl.when(i % 2 == 0)
        def _():
            tile(slot, i + 1, i, 0, PIECE, BLK - PIECE, PIECE, "piece")
        out = acc[...] / ls[...]
        of_ref[u] = out
        o_ref[u] = out.astype(BF)
        l_ref[u] = ms[...] + jnp.log2(ls[...])
        return 0
    lax.fori_loop(0, 12, task, 0)

def attn_fwd(starts2, x, role_fn, nb=8):
    V=pl.BlockSpec(memory_space=pltpu.VMEM)
    return pl.pallas_call(functools.partial(fwd_kernel, nb, role_fn),
        out_shape=(jax.ShapeDtypeStruct((12,HD,BLK),BF),jax.ShapeDtypeStruct((12,HD,BLK),F32),jax.ShapeDtypeStruct((12,1,BLK),F32)),
        in_specs=[pl.BlockSpec(memory_space=pltpu.SMEM),V],out_specs=(V,V,V),
        scratch_shapes=[pltpu.VMEM((2,nb,BLK,HD),BF),pltpu.VMEM((HD,BLK),F32),pltpu.VMEM((1,BLK),F32),pltpu.VMEM((1,BLK),F32)],
        name="attn_fwd",compiler_params=pltpu.CompilerParams(vmem_limit_bytes=48<<20))(starts2,x)

def bwd_kernel(nb, role_fn, starts_ref, x_ref, do_ref, of_ref, l_ref, dq_ref, f_ref, p_ref, kn, vn, dkv, dq):
    role = role_fn()
    for s in range(2):
        for j in range(nb):
            kn[s, j] = x_ref[s, j, 1].T
            vn[s, j] = x_ref[s, j, 2].T
    dkv[...] = jnp.zeros_like(dkv)
    def tile(slot, j, i, u, k0, nk, q0, nq, mask, delta):
        q = x_ref[slot, i, 0, :, q0:q0+nq]
        g = do_ref[slot, i, :, q0:q0+nq]
        k = kn[slot, j, k0:k0+nk, :]
        v = vn[slot, j, k0:k0+nk, :]
        p = jnp.exp2(nn(k, q) * C2 - l_ref[u, :, q0:q0+nq])
        if mask is not None:
            st = starts_ref[slot, i // 2]
            kp, qp, pin = piece_mask(j * BLK + k0, i * BLK + q0, nk, nq, st)
            ok = pin if mask == "piece" else (kp <= qp) | pin
            p = jnp.where(ok, p, 0.0)
        dp = nn(v, g)
        ds = (p * (dp - delta[:, q0:q0+nq])).astype(BF)
        dkv[slot, j, 1, :, k0:k0+nk] += nt(g, p.astype(BF))
        dkv[slot, j, 0, :, k0:k0+nk] += nt(q, ds)
        kt = x_ref[slot, j, 1, :, k0:k0+nk]
        dq[:, q0:q0+nq] += nn(kt, ds)
    def task(u, _):
        slot, i = task_index(u, role)
        dq[...] = jnp.zeros_like(dq)
        delta = jnp.sum(do_ref[slot, i].astype(F32) * of_ref[u], axis=0, keepdims=True)
        def inner(j, _):
            tile(slot, j, i, u, 0, BLK, 0, BLK, None, delta); return 0
        lax.fori_loop(0, i, inner, 0)
        tile(slot, i, i, u, 0, BLK, 0, BLK, "diag", delta)
        @pl.when(i % 2 == 0)
        def _():
            tile(slot, i + 1, i, u, 0, PIECE, BLK - PIECE, PIECE, "piece", delta)
        dq_ref[u] = (dq[...] * HD ** -0.5).astype(BF)
        return 0
    lax.fori_loop(0, 12, task, 0)
    for j in range(nb):
        f_ref[j, 0] = (dkv[0, j, 0] * HD ** -0.5).astype(BF)
        f_ref[j, 1] = dkv[0, j, 1].astype(BF)
        p_ref[j, 0] = dkv[1, j, 0] * HD ** -0.5
        p_ref[j, 1] = dkv[1, j, 1]

def attn_bwd(starts2, x, do, of, l, role_fn, nb=8):
    V=pl.BlockSpec(memory_space=pltpu.VMEM)
    return pl.pallas_call(functools.partial(bwd_kernel, nb, role_fn),
        out_shape=(jax.ShapeDtypeStruct((12,HD,BLK),BF),jax.ShapeDtypeStruct((nb,2,HD,BLK),BF),jax.ShapeDtypeStruct((nb,2,HD,BLK),F32)),
        in_specs=[pl.BlockSpec(memory_space=pltpu.SMEM),V,V,V,V],out_specs=(V,V,V),
        scratch_shapes=[pltpu.VMEM((2,nb,BLK,HD),BF),pltpu.VMEM((2,nb,BLK,HD),BF),pltpu.VMEM((2,nb,2,HD,BLK),F32),pltpu.VMEM((HD,BLK),F32)],
        name="attn_bwd",compiler_params=pltpu.CompilerParams(vmem_limit_bytes=48<<20))(starts2,x,do,of,l)


MESH_ID = pl.DeviceIdType.MESH
ANYS = pl.BlockSpec(memory_space=pl.ANY)
VMEMS = pl.BlockSpec(memory_space=pltpu.VMEM)


def place():
    t = lax.axis_index("tok")
    m = lax.axis_index("mdl")
    return t, m, t // 2, t % 2, m // 2, m % 2


def meet(peers):
    barrier = pltpu.get_barrier_semaphore()
    for peer in peers:
        pl.semaphore_signal(barrier, inc=1, device_id=peer, device_id_type=MESH_ID)
    pl.semaphore_wait(barrier, len(peers))


def chip_group(t, m):
    return [(t ^ k, m ^ b) for k in range(8) for b in range(2) if (k, b) != (0, 0)]


def remote(src, dst, ssem, rsem, dev):
    return pltpu.make_async_remote_copy(
        src_ref=src, dst_ref=dst, send_sem=ssem, recv_sem=rsem, device_id=dev, device_id_type=MESH_ID
    )


def spread_kernel(head_of, x_ref, o_ref, s_full, r_full, s_sh, r_sh, s_fw, r_fw):
    t, m, z, x, y, c = place()
    meet([(t ^ k, m) for k in range(1, 8)] + [(t, m ^ 1)])
    own = x == c

    def full(k):
        d = t ^ k
        return head_of(x_ref, 3 * (d // 2) + 2 * (d % 2)), o_ref.at[0, t], s_full.at[k], r_full.at[t], (d, m)

    def shared(k):
        zd = z ^ k
        return head_of(x_ref, 3 * zd + 1), o_ref.at[1, t], s_sh.at[k], r_sh.at[t], (2 * zd + c, m)

    order = [2, 4, 6, 3, 5, 7, 1]
    for k in (1, 2, 3):
        remote(*shared(k)).start()
    here = shared(0)

    @pl.when(own)
    def _():
        pltpu.make_async_copy(here[0], here[1], here[3]).start()

    @pl.when(jnp.logical_not(own))
    def _():
        remote(*here).start()

    for k in order:
        remote(*full(k)).start()
    loc = full(0)
    pltpu.make_async_copy(loc[0], loc[1], loc[3]).start()

    def forward(k):
        b = t ^ k
        return remote(o_ref.at[1, b], o_ref.at[1, b], s_fw.at[k], r_fw.at[b], (t, m ^ 1))

    @pl.when(own)
    def _():
        for k in (0, 1, 2, 3, 6, 7, 4, 5):
            b = t ^ k
            pltpu.make_async_copy(o_ref.at[1, b], o_ref.at[1, b], r_sh.at[b]).wait()
            forward(k).start()

    for k in range(8):
        b = t ^ k
        pltpu.make_async_copy(o_ref.at[0, b], o_ref.at[0, b], r_full.at[b]).wait()

    @pl.when(own)
    def _():
        for k in range(8):
            forward(k).wait_send()

    @pl.when(jnp.logical_not(own))
    def _():
        for k in range(8):
            forward(k).wait_recv()
        remote(*here).wait_send()

    for k in (1, 2, 3):
        remote(*shared(k)).wait_send()
    for k in range(1, 8):
        remote(*full(k)).wait_send()


def spread(x, parts, cid):
    lead = (2, 8) + ((3,) if parts == 3 else ())
    head_of = (lambda r, h: r.at[:, h]) if parts == 3 else (lambda r, h: r.at[h])
    D = pltpu.SemaphoreType.DMA
    return pl.pallas_call(
        functools.partial(spread_kernel, head_of),
        out_shape=jax.ShapeDtypeStruct(lead + x.shape[-2:], x.dtype),
        in_specs=[ANYS],
        out_specs=ANYS,
        scratch_shapes=[D((8,)), D((8,)), D((4,)), D((8,)), D((8,)), D((8,))],
        name="spread%d" % parts,
        compiler_params=pltpu.CompilerParams(collective_id=cid, has_side_effects=True),
    )(x)


def role_blocks(role):
    return [2 * n + (n % 2 + role) % 2 for n in range(4)]


def collect_kernel(x_ref, o_ref, s_full, s_sh, recv):
    t, m, z, x, y, c = place()
    meet(chip_group(t, m))
    role = (x + c) % 2
    hf = 3 * z + 2 * x
    hs = 3 * z + 1
    ms = 2 * y + x

    def full(k):
        u = t ^ k
        return x_ref.at[u], o_ref.at[hf], s_full.at[k], recv.at[hf], (u, m)

    blocks = role_blocks(role)

    def shared(n):
        return x_ref.at[8 + n], o_ref.at[hs], s_sh.at[n], recv.at[hs], (blocks[n], ms)

    for k in (4, 5, 6, 7, 2, 3, 1):
        remote(*full(k)).start()
    loc = full(0)
    pltpu.make_async_copy(loc[0], loc[1], loc[3]).start()
    for n in range(4):
        mine = (blocks[n] == t) & (role == 0)
        sh = shared(n)

        @pl.when(mine)
        def _():
            pltpu.make_async_copy(sh[0], sh[1], sh[3]).start()

        @pl.when(jnp.logical_not(mine))
        def _():
            remote(*sh).start()

    for h in range(12):
        pltpu.make_async_copy(o_ref.at[h], o_ref.at[h], recv.at[h]).wait()
    for k in range(1, 8):
        remote(*full(k)).wait_send()
    for n in range(4):
        mine = (blocks[n] == t) & (role == 0)
        sh = shared(n)

        @pl.when(jnp.logical_not(mine))
        def _():
            remote(*sh).wait_send()


def collect(x, cid):
    D = pltpu.SemaphoreType.DMA
    return pl.pallas_call(
        collect_kernel,
        out_shape=jax.ShapeDtypeStruct(x.shape, x.dtype),
        in_specs=[ANYS],
        out_specs=ANYS,
        scratch_shapes=[D((8,)), D((4,)), D((12,))],
        name="collect",
        compiler_params=pltpu.CompilerParams(collective_id=cid, has_side_effects=True),
    )(x)


def collect_grads_kernel(q_ref, f_ref, p_ref, o_ref, got, stage, sq, sqs, skv, skvs, sp, rp, rq, rkv):
    t, m, z, x, y, c = place()
    meet(chip_group(t, m))
    role = (x + c) % 2
    own = role == 0
    hf = 3 * z + 2 * x
    hs = 3 * z + 1
    ms = 2 * y + x
    blocks = role_blocks(role)

    def part(k):
        b = t ^ k
        return remote(p_ref.at[b], got.at[b], sp.at[k], rp.at[b], (t, m ^ 1))

    def fullq(k):
        u = t ^ k
        return q_ref.at[u], o_ref.at[0, hf], sq.at[k], rq.at[hf], (u, m)

    def fullkv(k):
        u = t ^ k
        return f_ref.at[u], o_ref.at[pl.ds(1, 2), hf], skv.at[k], rkv.at[hf], (u, m)

    def sharedq(n):
        return q_ref.at[8 + n], o_ref.at[0, hs], sqs.at[n], rq.at[hs], (blocks[n], ms)

    def sharedkv(k):
        u = t ^ k
        return stage.at[u], o_ref.at[pl.ds(1, 2), hs], skvs.at[k], rkv.at[hs], (u, m)

    order = (4, 5, 6, 7, 2, 3, 1, 0)

    @pl.when(jnp.logical_not(own))
    def _():
        for k in order:
            part(k).start()

    for k in order[:-1]:
        remote(*fullkv(k)).start()
        remote(*fullq(k)).start()
    a = fullq(0)
    pltpu.make_async_copy(a[0], a[1], a[3]).start()
    a = fullkv(0)
    pltpu.make_async_copy(a[0], a[1], a[3]).start()
    for n in range(4):
        mine = (blocks[n] == t) & own
        sh = sharedq(n)

        @pl.when(mine)
        def _():
            pltpu.make_async_copy(sh[0], sh[1], sh[3]).start()

        @pl.when(jnp.logical_not(mine))
        def _():
            remote(*sh).start()

    @pl.when(own)
    def _():
        for k in order:
            b = t ^ k
            part(k).wait_recv()
            stage[b] = (p_ref[b] + got[b]).astype(BF)
            a = sharedkv(k)
            if k:
                remote(*a).start()
            else:
                pltpu.make_async_copy(a[0], a[1], a[3]).start()

    for h in range(12):
        pltpu.make_async_copy(o_ref.at[0, h], o_ref.at[0, h], rq.at[h]).wait()
        pltpu.make_async_copy(o_ref.at[pl.ds(1, 2), h], o_ref.at[pl.ds(1, 2), h], rkv.at[h]).wait()
    for k in range(1, 8):
        remote(*fullq(k)).wait_send()
        remote(*fullkv(k)).wait_send()
    for n in range(4):
        mine = (blocks[n] == t) & own
        sh = sharedq(n)

        @pl.when(jnp.logical_not(mine))
        def _():
            remote(*sh).wait_send()

    @pl.when(own)
    def _():
        for k in range(1, 8):
            remote(*sharedkv(k)).wait_send()

    @pl.when(jnp.logical_not(own))
    def _():
        for k in range(8):
            part(k).wait_send()


def collect_grads(q, f, p, cid):
    D = pltpu.SemaphoreType.DMA
    return pl.pallas_call(
        collect_grads_kernel,
        out_shape=jax.ShapeDtypeStruct((3,) + q.shape, q.dtype),
        in_specs=[ANYS, ANYS, VMEMS],
        out_specs=ANYS,
        scratch_shapes=[
            pltpu.VMEM(p.shape, F32),
            pltpu.VMEM(p.shape, BF),
            D((8,)), D((4,)), D((8,)), D((8,)), D((8,)), D((8,)), D((12,)), D((12,)),
        ],
        name="collect_grads",
        compiler_params=pltpu.CompilerParams(collective_id=cid, has_side_effects=True, vmem_limit_bytes=32 << 20),
    )(q, f, p)


def gather_kernel(count, *refs):
    ins, outs = refs[:count], refs[count : 2 * count]
    send, recv, local = refs[2 * count :]
    t, m, z, x, y, c = place()
    xn, yn, sib = (t ^ 1, m), (t, m ^ 2), (t, m ^ 1)
    meet([(t ^ 2, m), (t ^ 4, m), (t ^ 6, m), xn, yn, sib])
    started = []

    def push(idx, dev, src=None):
        e = len(started)
        todo = []
        for a in range(count):
            cp = remote(outs[a].at[idx] if src is None else src[a], outs[a].at[idx], send.at[e, a], recv.at[a, idx], dev)
            cp.start()
            todo.append(cp)
        started.append(todo)

    def arrived(idx):
        for a in range(count):
            pltpu.make_async_copy(outs[a].at[idx], outs[a].at[idx], recv.at[a, idx]).wait()

    me = 4 * t + m
    for dev in [(t ^ 2, m), (t ^ 4, m), (t ^ 6, m), xn, yn, sib]:
        push(me, dev, ins)
    keep = [pltpu.make_async_copy(ins[a], outs[a].at[me], local.at[a]) for a in range(count)]
    for cp in keep:
        cp.start()
    for k in range(4):
        col = t ^ (2 * k)
        if k:
            arrived(4 * col + m)
            for dev in (xn, yn, sib):
                push(4 * col + m, dev)
        xi, yi = 4 * (col ^ 1) + m, 4 * col + (m ^ 2)
        arrived(xi)
        if k < 2:
            push(xi, yn)
        push(xi, sib)
        arrived(yi)
        if k >= 2:
            push(yi, xn)
        push(yi, sib)
    for k in range(4):
        di = 4 * (t ^ (2 * k) ^ 1) + (m ^ 2)
        arrived(di)
        push(di, sib)
    for k in range(4):
        for a in (0, 1):
            for b in (0, 2):
                arrived(4 * (t ^ (2 * k) ^ a) + (m ^ b ^ 1))
    for todo in started:
        for cp in todo:
            cp.wait_send()
    for cp in keep:
        cp.wait()


def gather(arrays, cid, name):
    D = pltpu.SemaphoreType.DMA
    n = len(arrays)
    return pl.pallas_call(
        functools.partial(gather_kernel, n),
        out_shape=tuple(jax.ShapeDtypeStruct((32,) + a.shape, a.dtype) for a in arrays),
        in_specs=[ANYS] * n,
        out_specs=tuple([ANYS] * n),
        scratch_shapes=[D((31, n)), D((n, 32)), D((n,))],
        name=name,
        compiler_params=pltpu.CompilerParams(collective_id=cid, has_side_effects=True),
    )(*arrays)


def scatter_kernel(count, *refs):
    ins, outs = refs[:count], refs[count : 2 * count]
    acc, r1, rx, ry, rd, rz = (refs[2 * count + i * count : 2 * count + (i + 1) * count] for i in range(6))
    s1, v1, ss, vx, vy, vd, vz = refs[8 * count :]
    t, m, z, x, y, c = place()
    xn, yn, sib = (t ^ 1, m), (t, m ^ 2), (t, m ^ 1)
    meet([(t ^ 2, m), (t ^ 4, m), (t ^ 6, m), xn, yn, sib])

    def owner(n):
        k, a, b = n // 4, (n // 2) % 2, n % 2
        return t ^ (2 * k + a), m ^ (2 * b)

    def first(n, a):
        tt, mm = owner(n)
        return remote(ins[a].at[4 * tt + (mm ^ 1)], r1[a].at[n], s1.at[n, a], v1.at[n, a], sib)

    order = [15, 11, 14, 13, 10, 9, 7, 3, 6, 5, 2, 1, 12, 8, 4, 0]
    for n in order:
        for a in range(count):
            first(n, a).start()
    started = []

    def push(n, dst, slot, vsem, dev):
        e = len(started)
        todo = []
        for a in range(count):
            cp = remote(acc[a].at[n], dst[a].at[slot], ss.at[e, a], vsem.at[slot, a], dev)
            cp.start()
            todo.append(cp)
        started.append(todo)

    def add(n, more=()):
        tt, mm = owner(n)
        for a in range(count):
            first(n, a).wait_recv()
            total = ins[a][4 * tt + mm].astype(F32) + r1[a][n].astype(F32)
            for buf, slot, vsem in more:
                pltpu.make_async_copy(buf[a].at[slot], buf[a].at[slot], vsem.at[slot, a]).wait()
                total = total + buf[a][slot].astype(F32)
            if n == 0:
                outs[a][...] = total
            else:
                acc[a][n] = total.astype(acc[a].dtype)

    for k in (3, 2, 1, 0):
        add(4 * k + 3)
        push(4 * k + 3, rd, k, vd, yn if k < 2 else xn)
        if k >= 2:
            add(4 * k + 2)
            push(4 * k + 2, rx, k, vx, xn)
        else:
            add(4 * k + 1)
            push(4 * k + 1, ry, k, vy, yn)
    for k in (3, 2, 1, 0):
        if k < 2:
            add(4 * k + 2, [(rd, k, vd)])
            push(4 * k + 2, rx, k, vx, xn)
        else:
            add(4 * k + 1, [(rd, k, vd)])
            push(4 * k + 1, ry, k, vy, yn)
    for k in (3, 2, 1):
        add(4 * k, [(rx, k, vx), (ry, k, vy)])
        push(4 * k, rz, k, vz, (t ^ (2 * k), m))
    add(0, [(rx, 0, vx), (ry, 0, vy), (rz, 1, vz), (rz, 2, vz), (rz, 3, vz)])
    for n in range(16):
        for a in range(count):
            first(n, a).wait_send()
    for todo in started:
        for cp in todo:
            cp.wait_send()


def scatter(arrays, cid, name):
    D = pltpu.SemaphoreType.DMA
    n = len(arrays)
    shard = [(a.shape[1:], a.dtype) for a in arrays]
    bufs = [pltpu.VMEM((k,) + s, d) for k in (16, 16, 4, 4, 4, 4) for s, d in shard]
    return pl.pallas_call(
        functools.partial(scatter_kernel, n),
        out_shape=tuple(jax.ShapeDtypeStruct(s, F32) for s, d in shard),
        in_specs=[VMEMS] * n,
        out_specs=tuple([VMEMS] * n),
        scratch_shapes=bufs + [D((16, n)), D((16, n)), D((15, n)), D((4, n)), D((4, n)), D((4, n)), D((4, n))],
        name=name,
        compiler_params=pltpu.CompilerParams(collective_id=cid, has_side_effects=True, vmem_limit_bytes=56 << 20),
    )(*arrays)


def packed(pieces):
    flat = jnp.concatenate(pieces, axis=-1)
    fill = 1024 - flat.shape[-1]
    flat = jnp.pad(flat, [(0, 0)] * (flat.ndim - 1) + [(0, fill)])
    return flat.reshape(flat.shape[:-1] + (8, 128))


def by_heads(
    tokens,
    cotangent,
    starts,
    w_qkv,
    b_query,
    b_value,
    w_out,
    b_out,
    gain_one,
    shift_one,
    gain_two,
    shift_two,
    w_expand,
    b_expand,
    w_shrink,
    b_shrink,
):
    rows, width = tokens.shape[1:]
    hidden = b_expand.shape[0] * 32
    small = [b_query, b_value, b_out, gain_one, shift_one, gain_two, shift_two, b_shrink, b_expand]
    small = [v.astype(BF).astype(F32) for v in small] + [starts[0].astype(F32)]
    full_qkv, full_out, full_expand, full_shrink, smalls = gather(
        [w_qkv.astype(BF), w_out.astype(BF), w_expand.astype(BF), w_shrink.astype(BF), packed(small)],
        0,
        "gather",
    )
    full_qkv = full_qkv.reshape(width, -1)
    full_out = full_out.reshape(width, -1)
    full_expand = full_expand.reshape(width, -1)
    full_shrink = full_shrink.reshape(hidden, -1)
    smalls = smalls.reshape(32, 1024)
    step = width // 32
    vecs = [smalls[:, i * step : (i + 1) * step].reshape(width) for i in range(8)]
    query_bias, value_bias, out_bias, gain_first, shift_first, gain_second, shift_second, shrink_bias = vecs
    expand_bias = smalls[:, 8 * step : 8 * step + hidden // 32].reshape(hidden)
    at = 8 * step + hidden // 32
    all_starts = smalls[:4, at : at + 4].astype(jnp.int32)
    t, m, z, x, y, c = place()
    starts2 = jnp.stack([starts[0], lax.dynamic_index_in_dim(all_starts, 2 * y + x, 0, keepdims=False)])

    def role_fn():
        t, m, z, x, y, c = place()
        return (x + c) % 2

    inputs = tokens[0].astype(F32)
    upstream_low = cotangent[0]
    normed = layer_norm(inputs, gain_first, shift_first).astype(BF)
    joined = jnp.einsum("de,rd->er", full_qkv, normed, preferred_element_type=F32)
    bias = jnp.concatenate([query_bias, jnp.zeros_like(query_bias), value_bias])
    joined = (joined + bias[:, None]).astype(BF).reshape(3, 12, HD, rows)
    heads = spread(joined, 3, 1)
    out_low, out_full, log_sum = attn_fwd(starts2, heads, role_fn)
    attention = collect(out_low, 2).reshape(width, rows)
    hidden_one = inputs + (
        jnp.einsum("dr,de->re", attention, full_out, preferred_element_type=F32) + out_bias
    )
    normed_two = layer_norm(hidden_one, gain_second, shift_second).astype(BF)
    expanded = jnp.dot(normed_two, full_expand, preferred_element_type=F32) + expand_bias
    activated = gelu_tanh(expanded).astype(BF)
    layer_out = hidden_one + (jnp.dot(activated, full_shrink, preferred_element_type=F32) + shrink_bias)
    upstream = upstream_low.astype(F32)
    db_shrink = jnp.sum(upstream, axis=0)
    dw_shrink = jnp.einsum("rf,rd->fd", activated, upstream_low, preferred_element_type=F32)
    grad_act = jnp.einsum("rd,fd->rf", upstream_low, full_shrink, preferred_element_type=F32)
    grad_expand = jax.vjp(gelu_tanh, expanded)[1](grad_act)[0].astype(BF)
    db_expand = jnp.sum(grad_expand.astype(F32), axis=0)
    dw_expand = jnp.einsum("rd,rf->df", normed_two, grad_expand, preferred_element_type=F32)
    grad_normed_two = jnp.einsum("rf,df->rd", grad_expand, full_expand, preferred_element_type=F32)
    pull = jax.vjp(layer_norm, hidden_one, gain_second, shift_second)[1]
    grad_hidden_part, dgain_two, dshift_two = pull(grad_normed_two)
    grad_hidden = upstream + grad_hidden_part
    grad_attn = grad_hidden.astype(BF)
    db_out = jnp.sum(grad_attn.astype(F32), axis=0)
    dw_out = jnp.einsum("dr,re->de", attention, grad_attn, preferred_element_type=F32)
    grad_mix = jnp.einsum("de,re->dr", full_out, grad_attn, preferred_element_type=F32)
    grad_heads = spread(grad_mix.astype(BF).reshape(12, HD, rows), 1, 3)
    dq, dkv, shared_dkv = attn_bwd(starts2, heads, grad_heads, out_full, log_sum, role_fn)
    grad_joined = collect_grads(dq, dkv, shared_dkv, 4).reshape(3 * width, rows)
    db_query = jnp.sum(grad_joined[:width].astype(F32), axis=1)
    db_value = jnp.sum(grad_joined[2 * width :].astype(F32), axis=1)
    dw_qkv = jnp.einsum("rd,er->de", normed, grad_joined, preferred_element_type=F32)
    grad_normed = jnp.einsum("er,de->rd", grad_joined, full_qkv, preferred_element_type=F32)
    pull = jax.vjp(layer_norm, inputs, gain_first, shift_first)[1]
    grad_input_part, dgain_one, dshift_one = pull(grad_normed)
    dtokens = grad_hidden + grad_input_part
    parts = [db_query, db_value, db_out, dgain_one, dshift_one, dgain_two, dshift_two, db_shrink, db_expand]
    dw_qkv, dw_out, dw_expand, dw_shrink, smalls = scatter(
        [w.astype(BF).reshape((32, -1) + w.shape[1:]) for w in (dw_qkv, dw_out, dw_expand, dw_shrink)]
        + [packed([v.reshape(32, -1) for v in parts])],
        5,
        "scatter",
    )
    flat = smalls.reshape(1024)
    vecs = [flat[i * step : (i + 1) * step] for i in range(8)]
    db_query, db_value, db_out, dgain_one, dshift_one, dgain_two, dshift_two, db_shrink = vecs
    db_expand = flat[8 * step : at]
    return (
        layer_out.astype(BF).reshape(1, rows, width),
        dtokens.reshape(1, rows, width),
        dw_qkv,
        db_query,
        db_value,
        dw_out,
        db_out,
        dgain_one,
        dshift_one,
        dgain_two,
        dshift_two,
        dw_expand,
        db_expand,
        dw_shrink,
        db_shrink,
    )


def solution(mesh):
    rows, vector, seq = P(("tok", "mdl"), None), P(("tok", "mdl")), P("mdl", "tok", None)
    by_name = dict(m=rows, v=vector, s=seq)
    fits = mesh.shape["tok"] == 8 and mesh.shape["mdl"] == 4
    return jax.shard_map(
        by_heads if fits else general,
        mesh=mesh,
        in_specs=(seq, seq, P("mdl", None)) + tuple(by_name[k] for k in "mvvmvvvvvmvmv"),
        out_specs=tuple(by_name[k] for k in "ssmvvmvvvvvmvmv"),
        check_vma=False,
    )
```

```python
import functools
import math

import jax
import jax.numpy as jnp
from jax import lax
from jax.experimental import pallas as pl
from jax.experimental.pallas import tpu as pltpu
from jax.sharding import PartitionSpec as P

HD = 64
PIECE = 256
KEYB = 512


epsilon = 1e-05
masked_score = -1e30
gelu_coeff = 0.7978845608028654


def layer_norm(values, gain_vec, shift_vec):
    center = values - jnp.mean(values, axis=-1, keepdims=True)
    spread = jnp.mean(center * center, axis=-1, keepdims=True)
    return center * lax.rsqrt(spread + epsilon) * gain_vec + shift_vec


def gelu_tanh(inputs):
    return (
        0.5 * inputs * (1.0 + jnp.tanh(gelu_coeff * (inputs + 0.044715 * inputs * inputs * inputs)))
    )


def piece_ids(begins, positions):
    inside = (positions[:, None] >= begins[None, :]) & (
        positions[:, None] < begins[None, :] + PIECE
    )
    labels = jnp.arange(1, begins.shape[0] + 1, dtype=jnp.int32)
    return jnp.sum(jnp.where(inside, labels[None, :], 0), axis=1) - 1


def block_scores(query_heads, key_heads, query_pos, query_lab, begins, block_index, scaling):
    key_block = lax.dynamic_slice_in_dim(key_heads, block_index * KEYB, KEYB, 0)
    key_pos = block_index * KEYB + jnp.arange(KEYB, dtype=jnp.int32)
    key_lab = piece_ids(begins, key_pos)
    scores = (
        jnp.einsum("qhd,khd->hqk", query_heads, key_block, preferred_element_type=jnp.float32)
        * scaling
    )
    allowed = (key_pos[None, :] <= query_pos[:, None]) | (
        key_lab[None, :] == query_lab[:, None]
    ) & (query_lab[:, None] >= 0)
    return jnp.where(allowed[None, :, :], scores, masked_score)


def attend_forward(
    query_heads, key_heads, value_heads, query_pos, query_lab, begins, needed, scaling
):
    local_rows = query_heads.shape[0]
    head_count = query_heads.shape[1]

    def stats_step(block_index, loop_state):
        highest, summed = loop_state
        masked = block_scores(
            query_heads, key_heads, query_pos, query_lab, begins, block_index, scaling
        )
        new_high = jnp.maximum(highest, jnp.max(masked, axis=-1))
        summed = summed * jnp.exp(highest - new_high) + jnp.sum(
            jnp.exp(masked - new_high[:, :, None]), axis=-1
        )
        return (new_high, summed)

    starting = (
        jnp.full((head_count, local_rows), masked_score, jnp.float32),
        jnp.zeros((head_count, local_rows), jnp.float32),
    )
    highest, summed = lax.fori_loop(0, needed, stats_step, starting)

    def mix_step(block_index, running):
        masked = block_scores(
            query_heads, key_heads, query_pos, query_lab, begins, block_index, scaling
        )
        prob_low = (jnp.exp(masked - highest[:, :, None]) / summed[:, :, None]).astype(jnp.bfloat16)
        value_block = lax.dynamic_slice_in_dim(value_heads, block_index * KEYB, KEYB, 0)
        return running + jnp.einsum(
            "hqk,khd->qhd", prob_low, value_block, preferred_element_type=jnp.float32
        )

    mixture = lax.fori_loop(0, needed, mix_step, jnp.zeros(query_heads.shape, jnp.float32))
    return (mixture, highest, summed)


def attend_backward(
    query_heads,
    key_heads,
    value_heads,
    grad_heads,
    mixture,
    query_pos,
    query_lab,
    begins,
    needed,
    highest,
    summed,
    scaling,
):
    row_delta = jnp.einsum("qhd,qhd->hq", grad_heads.astype(jnp.float32), mixture)

    def grad_step(block_index, loop_state):
        grad_query, grad_keys, grad_values = loop_state
        masked = block_scores(
            query_heads, key_heads, query_pos, query_lab, begins, block_index, scaling
        )
        prob_full = jnp.exp(masked - highest[:, :, None]) / summed[:, :, None]
        offset = block_index * KEYB
        value_block = lax.dynamic_slice_in_dim(value_heads, offset, KEYB, 0)
        grad_probs = jnp.einsum(
            "qhd,khd->hqk", grad_heads, value_block, preferred_element_type=jnp.float32
        )
        grad_scores = (prob_full * (grad_probs - row_delta[:, :, None])).astype(jnp.bfloat16)
        key_block = lax.dynamic_slice_in_dim(key_heads, offset, KEYB, 0)
        grad_query = (
            grad_query
            + jnp.einsum("hqk,khd->qhd", grad_scores, key_block, preferred_element_type=jnp.float32)
            * scaling
        )
        key_part = (
            jnp.einsum("hqk,qhd->khd", grad_scores, query_heads, preferred_element_type=jnp.float32)
            * scaling
        )
        value_part = jnp.einsum(
            "hqk,qhd->khd",
            prob_full.astype(jnp.bfloat16),
            grad_heads,
            preferred_element_type=jnp.float32,
        )
        grad_keys = lax.dynamic_update_slice_in_dim(
            grad_keys, lax.dynamic_slice_in_dim(grad_keys, offset, KEYB, 0) + key_part, offset, 0
        )
        grad_values = lax.dynamic_update_slice_in_dim(
            grad_values,
            lax.dynamic_slice_in_dim(grad_values, offset, KEYB, 0) + value_part,
            offset,
            0,
        )
        return (grad_query, grad_keys, grad_values)

    starting = (
        jnp.zeros(query_heads.shape, jnp.float32),
        jnp.zeros(key_heads.shape, jnp.float32),
        jnp.zeros(value_heads.shape, jnp.float32),
    )
    return lax.fori_loop(0, needed, grad_step, starting)


def general(
    tokens,
    cotangent,
    starts,
    w_qkv,
    b_query,
    b_value,
    w_out,
    b_out,
    gain_one,
    shift_one,
    gain_two,
    shift_two,
    w_expand,
    b_expand,
    w_shrink,
    b_shrink,
):
    (
        full_qkv,
        full_bq,
        full_bv,
        full_out,
        full_bo,
        full_gone,
        full_sone,
        full_gtwo,
        full_stwo,
        full_expand,
        full_bexp,
        full_shrink,
        full_bshr,
    ) = (
        lax.all_gather(w_qkv.astype(jnp.bfloat16), ("tok", "mdl"), axis=0, tiled=True),
        lax.all_gather(b_query.astype(jnp.bfloat16), ("tok", "mdl"), axis=0, tiled=True),
        lax.all_gather(b_value.astype(jnp.bfloat16), ("tok", "mdl"), axis=0, tiled=True),
        lax.all_gather(w_out.astype(jnp.bfloat16), ("tok", "mdl"), axis=0, tiled=True),
        lax.all_gather(b_out.astype(jnp.bfloat16), ("tok", "mdl"), axis=0, tiled=True),
        lax.all_gather(gain_one.astype(jnp.bfloat16), ("tok", "mdl"), axis=0, tiled=True),
        lax.all_gather(shift_one.astype(jnp.bfloat16), ("tok", "mdl"), axis=0, tiled=True),
        lax.all_gather(gain_two.astype(jnp.bfloat16), ("tok", "mdl"), axis=0, tiled=True),
        lax.all_gather(shift_two.astype(jnp.bfloat16), ("tok", "mdl"), axis=0, tiled=True),
        lax.all_gather(w_expand.astype(jnp.bfloat16), ("tok", "mdl"), axis=0, tiled=True),
        lax.all_gather(b_expand.astype(jnp.bfloat16), ("tok", "mdl"), axis=0, tiled=True),
        lax.all_gather(w_shrink.astype(jnp.bfloat16), ("tok", "mdl"), axis=0, tiled=True),
        lax.all_gather(b_shrink.astype(jnp.bfloat16), ("tok", "mdl"), axis=0, tiled=True),
    )
    query_bias = full_bq.astype(jnp.float32)
    value_bias = full_bv.astype(jnp.float32)
    out_bias = full_bo.astype(jnp.float32)
    gain_first = full_gone.astype(jnp.float32)
    shift_first = full_sone.astype(jnp.float32)
    gain_second = full_gtwo.astype(jnp.float32)
    shift_second = full_stwo.astype(jnp.float32)
    expand_bias = full_bexp.astype(jnp.float32)
    shrink_bias = full_bshr.astype(jnp.float32)
    local_rows = tokens.shape[1]
    model_width = tokens.shape[2]
    head_count = model_width // HD
    group_size = lax.axis_size("tok")
    member = lax.axis_index("tok")
    seq_len = local_rows * group_size
    scaling = HD ** (-0.5)
    needed = jnp.minimum(
        seq_len // KEYB, ((member + 1) * local_rows + PIECE - 1 + KEYB - 1) // KEYB
    )
    begins = starts[0]
    query_pos = member * local_rows + jnp.arange(local_rows, dtype=jnp.int32)
    query_lab = piece_ids(begins, query_pos)
    token_rows = tokens[0]
    cotangent_rows = cotangent[0]
    inputs = token_rows.astype(jnp.float32)
    normed = layer_norm(inputs, gain_first, shift_first).astype(jnp.bfloat16)
    joined = jnp.dot(normed, full_qkv, preferred_element_type=jnp.float32)
    queries = (joined[:, :model_width] + query_bias).astype(jnp.bfloat16)
    keys_own = joined[:, model_width : 2 * model_width].astype(jnp.bfloat16)
    values_own = (joined[:, 2 * model_width :] + value_bias).astype(jnp.bfloat16)
    key_full, value_full = (
        lax.all_gather(keys_own, "tok", axis=0, tiled=True),
        lax.all_gather(values_own, "tok", axis=0, tiled=True),
    )
    query_heads = queries.reshape(local_rows, head_count, HD)
    mixture, highest, summed = attend_forward(
        query_heads,
        key_full.reshape(seq_len, head_count, HD),
        value_full.reshape(seq_len, head_count, HD),
        query_pos,
        query_lab,
        begins,
        needed,
        scaling,
    )
    attention = mixture.reshape(local_rows, model_width).astype(jnp.bfloat16)
    hidden_one = inputs + (
        jnp.dot(attention, full_out, preferred_element_type=jnp.float32) + out_bias
    )
    normed_two = layer_norm(hidden_one, gain_second, shift_second).astype(jnp.bfloat16)
    expanded = jnp.dot(normed_two, full_expand, preferred_element_type=jnp.float32) + expand_bias
    activated = gelu_tanh(expanded).astype(jnp.bfloat16)
    layer_out = hidden_one + (
        jnp.dot(activated, full_shrink, preferred_element_type=jnp.float32) + shrink_bias
    )
    upstream = cotangent_rows.astype(jnp.float32)
    db_shrink = jnp.sum(upstream, axis=0)
    dw_shrink = jnp.einsum(
        "rf,rd->fd", activated, cotangent_rows, preferred_element_type=jnp.float32
    )
    grad_act = jnp.einsum(
        "rd,fd->rf", cotangent_rows, full_shrink, preferred_element_type=jnp.float32
    )
    gelu_pull = jax.vjp(gelu_tanh, expanded)[1]
    grad_expand = gelu_pull(grad_act)[0].astype(jnp.bfloat16)
    db_expand = jnp.sum(grad_expand.astype(jnp.float32), axis=0)
    dw_expand = jnp.einsum("rd,rf->df", normed_two, grad_expand, preferred_element_type=jnp.float32)
    grad_normed_two = jnp.einsum(
        "rf,df->rd", grad_expand, full_expand, preferred_element_type=jnp.float32
    )
    norm_pull = jax.vjp(layer_norm, hidden_one, gain_second, shift_second)[1]
    grad_hidden_part, dgain_two, dshift_two = norm_pull(grad_normed_two)
    grad_hidden = upstream + grad_hidden_part
    grad_attn = grad_hidden.astype(jnp.bfloat16)
    db_out = jnp.sum(grad_attn.astype(jnp.float32), axis=0)
    dw_out = jnp.einsum("rd,re->de", attention, grad_attn, preferred_element_type=jnp.float32)
    grad_mix = jnp.einsum(
        "re,de->rd", grad_attn, full_out, preferred_element_type=jnp.float32
    ).astype(jnp.bfloat16)
    key_back, value_back = (key_full, value_full)
    grad_query, grad_keys, grad_values = attend_backward(
        query_heads,
        key_back.reshape(seq_len, head_count, HD),
        value_back.reshape(seq_len, head_count, HD),
        grad_mix.reshape(local_rows, head_count, HD),
        mixture,
        query_pos,
        query_lab,
        begins,
        needed,
        highest,
        summed,
        scaling,
    )
    key_share, value_share = (
        lax.psum_scatter(
            grad_keys.reshape(seq_len, model_width).astype(jnp.bfloat16),
            "tok",
            scatter_dimension=0,
            tiled=True,
        ).astype(jnp.float32),
        lax.psum_scatter(
            grad_values.reshape(seq_len, model_width).astype(jnp.bfloat16),
            "tok",
            scatter_dimension=0,
            tiled=True,
        ).astype(jnp.float32),
    )
    grad_joined = jnp.concatenate(
        [
            grad_query.reshape(local_rows, model_width).astype(jnp.bfloat16),
            key_share.astype(jnp.bfloat16),
            value_share.astype(jnp.bfloat16),
        ],
        axis=1,
    )
    db_query = jnp.sum(grad_joined[:, :model_width].astype(jnp.float32), axis=0)
    db_value = jnp.sum(grad_joined[:, 2 * model_width :].astype(jnp.float32), axis=0)
    dw_qkv = jnp.einsum("rd,re->de", normed, grad_joined, preferred_element_type=jnp.float32)
    grad_normed = jnp.einsum("re,de->rd", grad_joined, full_qkv, preferred_element_type=jnp.float32)
    norm_pull_first = jax.vjp(layer_norm, inputs, gain_first, shift_first)[1]
    grad_input_part, dgain_one, dshift_one = norm_pull_first(grad_normed)
    dtokens = grad_hidden + grad_input_part
    (
        dw_qkv,
        db_query,
        db_value,
        dw_out,
        db_out,
        dgain_one,
        dshift_one,
        dgain_two,
        dshift_two,
        dw_expand,
        db_expand,
        dw_shrink,
        db_shrink,
    ) = (
        lax.psum_scatter(dw_qkv, ("tok", "mdl"), scatter_dimension=0, tiled=True),
        lax.psum_scatter(db_query, ("tok", "mdl"), scatter_dimension=0, tiled=True),
        lax.psum_scatter(db_value, ("tok", "mdl"), scatter_dimension=0, tiled=True),
        lax.psum_scatter(dw_out, ("tok", "mdl"), scatter_dimension=0, tiled=True),
        lax.psum_scatter(db_out, ("tok", "mdl"), scatter_dimension=0, tiled=True),
        lax.psum_scatter(dgain_one, ("tok", "mdl"), scatter_dimension=0, tiled=True),
        lax.psum_scatter(dshift_one, ("tok", "mdl"), scatter_dimension=0, tiled=True),
        lax.psum_scatter(dgain_two, ("tok", "mdl"), scatter_dimension=0, tiled=True),
        lax.psum_scatter(dshift_two, ("tok", "mdl"), scatter_dimension=0, tiled=True),
        lax.psum_scatter(dw_expand, ("tok", "mdl"), scatter_dimension=0, tiled=True),
        lax.psum_scatter(db_expand, ("tok", "mdl"), scatter_dimension=0, tiled=True),
        lax.psum_scatter(dw_shrink, ("tok", "mdl"), scatter_dimension=0, tiled=True),
        lax.psum_scatter(db_shrink, ("tok", "mdl"), scatter_dimension=0, tiled=True),
    )
    return (
        layer_out.astype(jnp.bfloat16).reshape(1, local_rows, model_width),
        dtokens.reshape(1, local_rows, model_width),
        dw_qkv,
        db_query,
        db_value,
        dw_out,
        db_out,
        dgain_one,
        dshift_one,
        dgain_two,
        dshift_two,
        dw_expand,
        db_expand,
        dw_shrink,
        db_shrink,
    )


BLK = 512
LOG_SCALE = math.log2(math.e) * HD ** (-0.5)
F32 = jnp.float32
BF = jnp.bfloat16


def nn(a, b):
    return lax.dot_general(a, b, (((1,), (0,)), ((), ())), preferred_element_type=F32)


def nt(a, b):
    return lax.dot_general(a, b, (((1,), (1,)), ((), ())), preferred_element_type=F32)


def diag_units(task):
    return [
        (2 * task, 0, "diag", 0, BLK, 0, BLK),
        (2 * task, 1, None, 0, BLK, 0, BLK),
        (2 * task + 1, 1, "diag", 0, BLK, 0, BLK),
        (2 * task + 1, 0, "piece", 0, PIECE, BLK - PIECE, PIECE),
    ]


def unit_mask(unit, task, begin):
    j, h, kind, k0, nk, q0, nq = unit
    keys = j * BLK + k0
    queries = (2 * task + h) * BLK + q0
    kc = keys + lax.broadcasted_iota(jnp.int32, (nk, 1), 0)
    qr = queries + lax.broadcasted_iota(jnp.int32, (1, nq), 1)
    kin = ((kc >= begin) & (kc < begin + PIECE)).astype(F32)
    qin = ((qr >= begin) & (qr < begin + PIECE)).astype(F32)
    both = (kin * qin) > 0.5
    if kind == "piece":
        return both
    kp = keys + lax.broadcasted_iota(jnp.int32, (nk, nq), 0)
    qp = queries + lax.broadcasted_iota(jnp.int32, (nk, nq), 1)
    return (kp <= qp) | both


def forward_units(slot, task, units, begin, xv, kn, acc, ms, ls):
    def score(unit):
        j, h, kind, k0, nk, q0, nq = unit
        s = nn(kn[slot, j, k0 : k0 + nk, :], xv[slot, 2 * task + h, 0, :, q0 : q0 + nq]) * LOG_SCALE
        if kind:
            s = jnp.where(unit_mask(unit, task, begin), s, masked_score)
        return s

    ahead = score(units[0])
    for n, unit in enumerate(units):
        j, h, kind, k0, nk, q0, nq = unit
        now = ahead
        if n + 1 < len(units):
            ahead = score(units[n + 1])
        qs = slice(q0, q0 + nq)
        high = jnp.maximum(ms[h, :, qs], jnp.max(now, axis=0, keepdims=True))
        fade = jnp.exp2(ms[h, :, qs] - high)
        p = jnp.exp2(now - high)
        ls[h, :, qs] = ls[h, :, qs] * fade + jnp.sum(p, axis=0, keepdims=True)
        ms[h, :, qs] = high
        acc[h, :, qs] = acc[h, :, qs] * fade + nn(xv[slot, j, 2, :, k0 : k0 + nk], p.astype(BF))


def forward_task(slot, task, begin, xv, kn, acc, ms, ls):
    ms[...] = jnp.full_like(ms, masked_score)
    ls[...] = jnp.zeros_like(ls)
    acc[...] = jnp.zeros_like(acc)

    def step(j, carry):
        forward_units(
            slot, task, [(j, h, None, 0, BLK, 0, BLK) for h in range(2)], begin, xv, kn, acc, ms, ls
        )
        return carry

    lax.fori_loop(0, 2 * task, step, 0)
    forward_units(slot, task, diag_units(task), begin, xv, kn, acc, ms, ls)


def backward_units(slot, task, units, begin, xv, gv, kn, vn, lsum, delta, dkv, dq):
    def score(unit):
        j, h, kind, k0, nk, q0, nq = unit
        b = 2 * task + h
        s = nn(kn[slot, j, k0 : k0 + nk, :], xv[slot, b, 0, :, q0 : q0 + nq]) * LOG_SCALE
        return s, nn(vn[slot, j, k0 : k0 + nk, :], gv[slot, b, :, q0 : q0 + nq])

    ahead = score(units[0])
    for n, unit in enumerate(units):
        j, h, kind, k0, nk, q0, nq = unit
        b = 2 * task + h
        s, dp = ahead
        if n + 1 < len(units):
            ahead = score(units[n + 1])
        p = jnp.exp2(s - lsum[slot, b, :, q0 : q0 + nq])
        if kind:
            p = jnp.where(unit_mask(unit, task, begin), p, 0.0)
        ds = (p * (dp - delta[slot, b, :, q0 : q0 + nq])).astype(BF)
        dkv[slot, j, 1, :, k0 : k0 + nk] += nt(gv[slot, b, :, q0 : q0 + nq], p.astype(BF))
        dkv[slot, j, 0, :, k0 : k0 + nk] += nt(xv[slot, b, 0, :, q0 : q0 + nq], ds)
        dq[slot, b, :, q0 : q0 + nq] += nn(xv[slot, j, 1, :, k0 : k0 + nk], ds)


MESH_ID = pl.DeviceIdType.MESH
ANYS = pl.BlockSpec(memory_space=pl.ANY)
VMEMS = pl.BlockSpec(memory_space=pltpu.VMEM)
SMEMS = pl.BlockSpec(memory_space=pltpu.SMEM)
DMA = pltpu.SemaphoreType.DMA


def place():
    t = lax.axis_index("tok")
    m = lax.axis_index("mdl")
    return t, m, t // 2, t % 2, m // 2, m % 2


def meet(peers):
    barrier = pltpu.get_barrier_semaphore()
    for peer in peers:
        pl.semaphore_signal(barrier, inc=1, device_id=peer, device_id_type=MESH_ID)
    pl.semaphore_wait(barrier, len(peers))


def chip_group(t, m):
    return [(t ^ k, m ^ b) for k in range(8) for b in range(2) if (k, b) != (0, 0)]


def column_group(t, m):
    return [(t ^ 2, m), (t ^ 4, m), (t ^ 6, m), (t ^ 1, m), (t, m ^ 2), (t, m ^ 1)]


def remote(src, dst, ssem, rsem, dev):
    return pltpu.make_async_remote_copy(
        src_ref=src, dst_ref=dst, send_sem=ssem, recv_sem=rsem, device_id=dev, device_id_type=MESH_ID
    )


def landed(ref, sem):
    pltpu.make_async_copy(ref, ref, sem).wait()


def send_unless(here, src, dst, ssem, rsem, dev):
    @pl.when(here)
    def _():
        pltpu.make_async_copy(src, dst, rsem).start()

    @pl.when(jnp.logical_not(here))
    def _():
        remote(src, dst, ssem, rsem, dev).start()


def sent_unless(here, src, dst, ssem, rsem, dev):
    @pl.when(jnp.logical_not(here))
    def _():
        remote(src, dst, ssem, rsem, dev).wait_send()


class Pushes:
    def __init__(self, outs, send, recv):
        self.outs, self.send, self.recv, self.started = outs, send, recv, []

    def push(self, shard, dev, src=None):
        e = len(self.started)
        todo = []
        for a, out in enumerate(self.outs):
            cp = remote(
                out.at[shard] if src is None else src[a],
                out.at[shard],
                self.send.at[e, a],
                self.recv.at[a, shard],
                dev,
            )
            cp.start()
            todo.append(cp)
        self.started.append(todo)

    def arrived(self, shard):
        for a, out in enumerate(self.outs):
            landed(out.at[shard], self.recv.at[a, shard])

    def finish(self):
        for todo in self.started:
            for cp in todo:
                cp.wait_send()


def first_gather_kernel(now, later, *refs):
    n = now + later
    ins, outs = refs[:n], refs[n : 2 * n]
    send, recv, local, send_z, recv_z = refs[2 * n :]
    t, m, z, x, y, c = place()
    xn, yn, sib = (t ^ 1, m), (t, m ^ 2), (t, m ^ 1)
    meet(column_group(t, m))
    work = Pushes(outs[:now], send, recv)
    column = Pushes(outs[now:], send_z, recv_z)
    me = 4 * t + m
    for dev in [(t ^ 2, m), (t ^ 4, m), (t ^ 6, m), xn, yn, sib]:
        work.push(me, dev, ins[:now])
    for dev in [(t ^ 2, m), (t ^ 4, m), (t ^ 6, m)]:
        column.push(me, dev, ins[now:])
    keep = [pltpu.make_async_copy(ins[a], outs[a].at[me], local.at[a]) for a in range(n)]
    for cp in keep:
        cp.start()
    for k in range(4):
        col = t ^ (2 * k)
        if k:
            work.arrived(4 * col + m)
            for dev in (xn, yn, sib):
                work.push(4 * col + m, dev)
        xi, yi = 4 * (col ^ 1) + m, 4 * col + (m ^ 2)
        work.arrived(xi)
        if k < 2:
            work.push(xi, yn)
        work.push(xi, sib)
        work.arrived(yi)
        if k >= 2:
            work.push(yi, xn)
        work.push(yi, sib)
    for k in range(4):
        di = 4 * (t ^ (2 * k) ^ 1) + (m ^ 2)
        work.arrived(di)
        work.push(di, sib)
    for k in range(4):
        for a in (0, 1):
            for b in (0, 2):
                work.arrived(4 * (t ^ (2 * k) ^ a) + (m ^ b ^ 1))
    for k in (1, 2, 3):
        column.arrived(4 * (t ^ (2 * k)) + m)
    work.finish()
    column.finish()
    for cp in keep:
        cp.wait()


def first_gather(now, later, cid):
    arrays = now + later
    a, b = len(now), len(later)
    return pl.pallas_call(
        functools.partial(first_gather_kernel, a, b),
        out_shape=tuple(jax.ShapeDtypeStruct((32,) + w.shape, w.dtype) for w in arrays),
        in_specs=[ANYS] * (a + b),
        out_specs=tuple([ANYS] * (a + b)),
        scratch_shapes=[DMA((31, a)), DMA((a, 32)), DMA((a + b,)), DMA((3, b)), DMA((b, 32))],
        name="first_gather",
        compiler_params=pltpu.CompilerParams(collective_id=cid, has_side_effects=True),
    )(*arrays)


def attend_kernel(count, starts_ref, j_ref, *refs):
    outs = refs[count : count + 4]
    heads, of_ref, l_ref, att = outs
    weights = refs[count + 4 : 2 * count + 4]
    (xv, kn, acc, ms, ls, stage, s_full, r_full, s_sh, r_sh, s_fw, r_fw, s_out, r_out, keep, send, recv) = refs[
        2 * count + 4 :
    ]
    t, m, z, x, y, c = place()
    xn, yn, sib = (t ^ 1, m), (t, m ^ 2), (t, m ^ 1)
    meet(chip_group(t, m) + [yn])
    own = x == c
    role = (x + c) % 2
    hf, hs, owner_m = 3 * z + 2 * x, 3 * z + 1, 2 * y + x

    def full(k):
        d = t ^ k
        return j_ref.at[:, 3 * (d // 2) + 2 * (d % 2)], xv.at[0, t], s_full.at[k], r_full.at[t], (d, m)

    def shared(k):
        zd = z ^ k
        return j_ref.at[:, 3 * zd + 1], xv.at[1, t], s_sh.at[k], r_sh.at[t], (2 * zd + c, m)

    for k in (4, 5, 6, 7, 2, 3, 1):
        remote(*full(k)).start()
    loc = full(0)
    pltpu.make_async_copy(loc[0], loc[1], loc[3]).start()
    for k in (2, 3, 1):
        remote(*shared(k)).start()
    send_unless(own, *shared(0))

    work = Pushes(weights, send, recv)
    for k in range(4):
        for dev in (xn, yn, sib):
            work.push(4 * (t ^ (2 * k)) + m, dev)

    def keep_head(slot):
        cp = pltpu.make_async_copy(xv.at[slot], heads.at[slot], keep.at[slot])
        cp.start()
        return cp

    for b in range(8):
        landed(xv.at[0, b], r_full.at[b])
    kept = [keep_head(0)]
    for b in range(8):
        kn[0, b] = xv[0, b, 1].T

    def finish_task(slot, task, row, head, mdl, alone):
        for h in range(2):
            b, u = 2 * task + h, 2 * row + h
            out = acc[h] / ls[h]
            of_ref[u] = out
            stage[u] = out.astype(BF)
            l_ref[u] = ms[h] + jnp.log2(ls[h])
            send_unless((b == t) & alone, stage.at[u], att.at[head], s_out.at[u], r_out.at[head], (b, mdl))

    def full_task(w, carry):
        forward_task(0, w, starts_ref[0, w], xv, kn, acc, ms, ls)
        finish_task(0, w, w, hf, m, t >= 0)
        return carry

    lax.fori_loop(0, 3, full_task, 0)

    for k in range(4):
        col = t ^ (2 * k)
        xi, yi = 4 * (col ^ 1) + m, 4 * col + (m ^ 2)
        work.arrived(xi)
        if k < 2:
            work.push(xi, yn)
        work.push(xi, sib)
        work.arrived(yi)
        if k >= 2:
            work.push(yi, xn)
        work.push(yi, sib)

    def forward(k):
        b = t ^ k
        return remote(xv.at[1, b], xv.at[1, b], s_fw.at[k], r_fw.at[b], sib)

    @pl.when(own)
    def _():
        for k in (0, 1, 2, 3, 6, 7, 4, 5):
            landed(xv.at[1, t ^ k], r_sh.at[t ^ k])
            forward(k).start()

    lax.fori_loop(3, 4, full_task, 0)

    @pl.when(jnp.logical_not(own))
    def _():
        for k in range(8):
            forward(k).wait_recv()

    kept.append(keep_head(1))
    for b in range(8):
        kn[1, b] = xv[1, b, 1].T

    def shared_task(n, carry):
        task = jnp.where(n == 0, role, 3 - role)
        forward_task(1, task, starts_ref[1, task], xv, kn, acc, ms, ls)
        finish_task(1, task, 4 + n, hs, owner_m, own)
        return carry

    lax.fori_loop(0, 2, shared_task, 0)

    for k in range(4):
        di = 4 * (t ^ (2 * k) ^ 1) + (m ^ 2)
        work.arrived(di)
        work.push(di, sib)
    for h in range(12):
        landed(att.at[h], r_out.at[h])
    for k in range(4):
        for a in (0, 1):
            for b in (0, 2):
                work.arrived(4 * (t ^ (2 * k) ^ a) + (m ^ b ^ 1))
    work.finish()
    for k in range(1, 8):
        remote(*full(k)).wait_send()
    for k in (1, 2, 3):
        remote(*shared(k)).wait_send()
    sent_unless(own, *shared(0))

    @pl.when(own)
    def _():
        for k in range(8):
            forward(k).wait_send()

    for w in range(4):
        for h in range(2):
            b, u = 2 * w + h, 2 * w + h
            sent_unless(b == t, stage.at[u], att.at[hf], s_out.at[u], r_out.at[hf], (b, m))
    for n in range(2):
        task = role if n == 0 else 3 - role
        for h in range(2):
            b, u = 2 * task + h, 8 + 2 * n + h
            sent_unless((b == t) & own, stage.at[u], att.at[hs], s_out.at[u], r_out.at[hs], (b, owner_m))
    for cp in kept:
        cp.wait()


def attend(starts2, joined, weights, cid):
    n = len(weights)
    head = (HD, BLK)
    S = jax.ShapeDtypeStruct
    outs = pl.pallas_call(
        functools.partial(attend_kernel, n),
        out_shape=(S((2, 8, 3) + head, BF), S((12,) + head, F32), S((12, 1, BLK), F32), S((12,) + head, BF))
        + tuple(S(w.shape, w.dtype) for w in weights),
        in_specs=[SMEMS, ANYS] + [ANYS] * n,
        out_specs=(ANYS, VMEMS, VMEMS, ANYS) + (ANYS,) * n,
        scratch_shapes=[
            pltpu.VMEM((2, 8, 3) + head, BF),
            pltpu.VMEM((2, 8, BLK, HD), BF),
            pltpu.VMEM((2,) + head, F32),
            pltpu.VMEM((2, 1, BLK), F32),
            pltpu.VMEM((2, 1, BLK), F32),
            pltpu.VMEM((12,) + head, BF),
        ]
        + [DMA((8,)), DMA((8,)), DMA((4,)), DMA((8,)), DMA((8,)), DMA((8,)), DMA((12,)), DMA((12,)), DMA((2,))]
        + [DMA((28, n)), DMA((n, 32))],
        input_output_aliases={2 + a: 4 + a for a in range(n)},
        name="attend",
        compiler_params=pltpu.CompilerParams(collective_id=cid, has_side_effects=True, vmem_limit_bytes=40 << 20),
    )(starts2, joined, *weights)
    return outs[:4], outs[4:]


class Sums:
    def __init__(self, ins, acc, r1, rx, ry, rd, s1, v1, ss, vx, vy, vd):
        self.t, self.m = lax.axis_index("tok"), lax.axis_index("mdl")
        self.ins, self.acc, self.r1, self.rx, self.ry, self.rd = ins, acc, r1, rx, ry, rd
        self.s1, self.v1, self.ss, self.vx, self.vy, self.vd = s1, v1, ss, vx, vy, vd
        self.count = len(ins)
        self.started = []

    def owner(self, n):
        return self.t ^ (2 * (n // 4) + (n // 2) % 2), self.m ^ (2 * (n % 2))

    def first(self, n, a):
        tt, mm = self.owner(n)
        return remote(
            self.ins[a].at[4 * tt + (mm ^ 1)], self.r1[a].at[n], self.s1.at[n, a], self.v1.at[n, a], (self.t, self.m ^ 1)
        )

    def begin(self):
        for n in (15, 11, 14, 10, 7, 3, 5, 1, 6, 2, 13, 9, 12, 8, 4, 0):
            for a in range(self.count):
                self.first(n, a).start()

    def push(self, n, dst, slot, vsem, dev):
        e = len(self.started)
        todo = []
        for a in range(self.count):
            cp = remote(self.acc[a].at[n], dst[a].at[slot], self.ss.at[e, a], vsem.at[slot, a], dev)
            cp.start()
            todo.append(cp)
        self.started.append(todo)

    def total(self, n, a, more=()):
        tt, mm = self.owner(n)
        self.first(n, a).wait_recv()
        out = self.ins[a][4 * tt + mm].astype(F32) + self.r1[a][n].astype(F32)
        for buf, slot, vsem in more:
            landed(buf[a].at[slot], vsem.at[slot, a])
            out = out + buf[a][slot].astype(F32)
        return out

    def add(self, n, more=()):
        for a in range(self.count):
            self.acc[a][n] = self.total(n, a, more).astype(self.acc[a].dtype)

    def early(self):
        xn, yn = (self.t ^ 1, self.m), (self.t, self.m ^ 2)
        for k in (3, 2, 1, 0):
            self.add(4 * k + 3)
            self.push(4 * k + 3, self.rd, k, self.vd, yn if k < 2 else xn)
        for k in (3, 2, 1, 0):
            if k >= 2:
                self.add(4 * k + 2)
                self.push(4 * k + 2, self.rx, k, self.vx, xn)
            else:
                self.add(4 * k + 1)
                self.push(4 * k + 1, self.ry, k, self.vy, yn)

    def late(self):
        xn, yn = (self.t ^ 1, self.m), (self.t, self.m ^ 2)
        for k in (3, 2, 1, 0):
            via = [(self.rd, k, self.vd)]
            if k < 2:
                self.add(4 * k + 2, via)
                self.push(4 * k + 2, self.rx, k, self.vx, xn)
            else:
                self.add(4 * k + 1, via)
                self.push(4 * k + 1, self.ry, k, self.vy, yn)

    def column(self, k, a):
        return self.total(4 * k, a, [(self.rx, k, self.vx), (self.ry, k, self.vy)])

    def finish(self):
        for n in range(16):
            for a in range(self.count):
                self.first(n, a).wait_send()
        for todo in self.started:
            for cp in todo:
                cp.wait_send()


def sums_scratch(arrays):
    n = len(arrays)
    bufs = [pltpu.VMEM((k,) + a.shape[1:], a.dtype) for k in (16, 16, 4, 4, 4) for a in arrays]
    return bufs + [DMA((16, n)), DMA((16, n)), DMA((12, n)), DMA((4, n)), DMA((4, n)), DMA((4, n))]


def take_sums(ins, refs):
    n = len(ins)
    bufs = [refs[i * n : (i + 1) * n] for i in range(5)]
    return Sums(ins, *bufs, *refs[5 * n : 5 * n + 6]), refs[5 * n + 6 :]


def attend_back_kernel(count, starts_ref, g_ref, xv, of_ref, l_ref, *refs):
    ins, gj, sums = refs[:count], refs[count], refs[count + 1 : 2 * count + 1]
    work, rest = take_sums(ins, refs[2 * count + 1 :])
    (gv, kn, vn, dkv, dq, lsum, delta, stage, stage_kv, got, stage_sh) = rest[:11]
    (s_full, r_full, s_sh, r_sh, s_fw, r_fw, s_q, r_q, s_kv, r_kv, s_shkv, s_part, r_part) = rest[11:]
    t, m, z, x, y, c = place()
    sib = (t, m ^ 1)
    meet(chip_group(t, m) + [(t, m ^ 2)])
    own = x == c
    role = (x + c) % 2
    hf, hs, owner_m = 3 * z + 2 * x, 3 * z + 1, 2 * y + x
    order = (4, 5, 6, 7, 2, 3, 1)

    def full(k):
        d = t ^ k
        return g_ref.at[3 * (d // 2) + 2 * (d % 2)], gv.at[0, t], s_full.at[k], r_full.at[t], (d, m)

    def shared(k):
        zd = z ^ k
        return g_ref.at[3 * zd + 1], gv.at[1, t], s_sh.at[k], r_sh.at[t], (2 * zd + c, m)

    for k in (2, 3, 1):
        remote(*shared(k)).start()
    send_unless(own, *shared(0))
    for k in order:
        remote(*full(k)).start()
    loc = full(0)
    pltpu.make_async_copy(loc[0], loc[1], loc[3]).start()
    work.begin()

    for s in range(2):
        for b in range(8):
            kn[s, b] = xv[s, b, 1].T
            vn[s, b] = xv[s, b, 2].T
    dkv[...] = jnp.zeros_like(dkv)
    dq[...] = jnp.zeros_like(dq)

    def forward(k):
        b = t ^ k
        return remote(gv.at[1, b], gv.at[1, b], s_fw.at[k], r_fw.at[b], sib)

    @pl.when(own)
    def _():
        for k in (0, 1, 2, 3, 6, 7, 4, 5):
            landed(gv.at[1, t ^ k], r_sh.at[t ^ k])
            forward(k).start()

    work.early()

    @pl.when(jnp.logical_not(own))
    def _():
        for k in range(8):
            forward(k).wait_recv()

    def ready(slot, b, u):
        lsum[slot, b] = l_ref[u]
        delta[slot, b] = jnp.sum(gv[slot, b].astype(F32) * of_ref[u], axis=0, keepdims=True)

    def out_q(slot, b, u):
        stage[u] = (dq[slot, b] * HD ** (-0.5)).astype(BF)
        if slot:
            send_unless((b == t) & own, stage.at[u], gj.at[0, hs], s_q.at[u], r_q.at[hs], (b, owner_m))
        else:
            send_unless(b == t, stage.at[u], gj.at[0, hf], s_q.at[u], r_q.at[hf], (b, m))

    args = (xv, gv, kn, vn, lsum, delta, dkv, dq)

    def shared_task(n, carry):
        task = jnp.where(n == 0, role, 3 - role)
        begin = starts_ref[1, task]
        for h in range(2):
            ready(1, 2 * task + h, 8 + 2 * n + h)

        def step(j, carry):
            backward_units(1, task, [(j, h, None, 0, BLK, 0, BLK) for h in range(2)], begin, *args)
            return carry

        lax.fori_loop(0, 2 * task, step, 0)
        backward_units(1, task, diag_units(task), begin, *args)
        for h in range(2):
            out_q(1, 2 * task + h, 8 + 2 * n + h)
        return carry

    lax.fori_loop(0, 2, shared_task, 0)

    def part(k):
        b = t ^ k
        return remote(dkv.at[1, b], got.at[b], s_part.at[k], r_part.at[b], sib)

    def shared_kv(k):
        b = t ^ k
        return stage_sh.at[b], gj.at[pl.ds(1, 2), hs], s_shkv.at[k], r_kv.at[hs], (b, m)

    @pl.when(jnp.logical_not(own))
    def _():
        for k in order + (0,):
            part(k).start()

    work.late()
    for b in range(8):
        landed(gv.at[0, b], r_full.at[b])
        ready(0, b, b)

    def full_keys(s, carry):
        keys = z ^ (3 - s)
        backward_units(0, keys, diag_units(keys), starts_ref[0, keys], *args)

        def step(task, carry):
            units = [(2 * keys + b, h, None, 0, BLK, 0, BLK) for b in range(2) for h in range(2)]
            backward_units(0, task, units, 0, *args)
            return carry

        lax.fori_loop(keys + 1, 4, step, 0)
        for i in range(2):
            b = 2 * keys + i
            stage_kv[b, 0] = (dkv[0, b, 0] * HD ** (-0.5)).astype(BF)
            stage_kv[b, 1] = dkv[0, b, 1].astype(BF)
            send_unless(b == t, stage_kv.at[b], gj.at[pl.ds(1, 2), hf], s_kv.at[b], r_kv.at[hf], (b, m))

        @pl.when(own & (s == 0))
        def _():
            for k in order + (0,):
                b = t ^ k
                part(k).wait_recv()
                stage_sh[b, 0] = ((dkv[1, b, 0] + got[b, 0]) * HD ** (-0.5)).astype(BF)
                stage_sh[b, 1] = (dkv[1, b, 1] + got[b, 1]).astype(BF)
                a = shared_kv(k)
                if k:
                    remote(*a).start()
                else:
                    pltpu.make_async_copy(a[0], a[1], a[3]).start()

        return carry

    lax.fori_loop(0, 4, full_keys, 0)
    for b in range(8):
        out_q(0, b, b)
    for k in range(4):
        for a in range(count):
            sums[a][k] = work.column(k, a).astype(BF)

    for h in range(12):
        landed(gj.at[0, h], r_q.at[h])
        landed(gj.at[pl.ds(1, 2), h], r_kv.at[h])
    work.finish()
    for k in range(1, 8):
        remote(*full(k)).wait_send()
    for k in (1, 2, 3):
        remote(*shared(k)).wait_send()
    sent_unless(own, *shared(0))
    for b in range(8):
        sent_unless(b == t, stage.at[b], gj.at[0, hf], s_q.at[b], r_q.at[hf], (b, m))
        sent_unless(b == t, stage_kv.at[b], gj.at[pl.ds(1, 2), hf], s_kv.at[b], r_kv.at[hf], (b, m))
    for n in range(2):
        task = role if n == 0 else 3 - role
        for h in range(2):
            b, u = 2 * task + h, 8 + 2 * n + h
            sent_unless((b == t) & own, stage.at[u], gj.at[0, hs], s_q.at[u], r_q.at[hs], (b, owner_m))

    @pl.when(own)
    def _():
        for k in range(8):
            forward(k).wait_send()
        for k in range(1, 8):
            remote(*shared_kv(k)).wait_send()

    @pl.when(jnp.logical_not(own))
    def _():
        for k in range(8):
            part(k).wait_send()


def attend_back(starts2, grad_mix, heads, out_full, log_sum, grads, cid):
    n = len(grads)
    head = (HD, BLK)
    S = jax.ShapeDtypeStruct
    V = pltpu.VMEM
    outs = pl.pallas_call(
        functools.partial(attend_back_kernel, n),
        out_shape=(S((3, 12) + head, BF),) + tuple(S((4,) + g.shape[1:], BF) for g in grads),
        in_specs=[SMEMS, ANYS, VMEMS, VMEMS, VMEMS] + [VMEMS] * n,
        out_specs=(ANYS,) + (VMEMS,) * n,
        scratch_shapes=sums_scratch(grads)
        + [
            V((2, 8) + head, BF),
            V((2, 8, BLK, HD), BF),
            V((2, 8, BLK, HD), BF),
            V((2, 8, 2) + head, F32),
            V((2, 8) + head, F32),
            V((2, 8, 1, BLK), F32),
            V((2, 8, 1, BLK), F32),
            V((12,) + head, BF),
            V((8, 2) + head, BF),
            V((8, 2) + head, F32),
            V((8, 2) + head, BF),
        ]
        + [DMA((8,)), DMA((8,)), DMA((4,)), DMA((8,)), DMA((8,)), DMA((8,)), DMA((12,)), DMA((12,))]
        + [DMA((8,)), DMA((12,)), DMA((8,)), DMA((8,)), DMA((8,))],
        name="attend_back",
        compiler_params=pltpu.CompilerParams(collective_id=cid, has_side_effects=True, vmem_limit_bytes=58 << 20),
    )(starts2, grad_mix, heads, out_full, log_sum, *grads)
    return outs[0], outs[1:]


def last_sums_kernel(now, later, *refs):
    n = now + later
    ins, part, outs = refs[:now], refs[now:n], refs[n : 2 * n]
    work, rest = take_sums(ins, refs[2 * n :])
    rz, rzp = rest[:now], rest[now:n]
    sz, vz, szp, vzp = rest[n:]
    t, m, z, x, y, c = place()
    meet(column_group(t, m))
    work.begin()
    along = []
    for k in (3, 2, 1):
        for a in range(later):
            cp = remote(part[a].at[k], rzp[a].at[k], szp.at[k, a], vzp.at[k, a], (t ^ (2 * k), m))
            cp.start()
            along.append(cp)
    work.early()
    work.late()
    for k in (3, 2, 1):
        for a in range(now):
            work.acc[a][4 * k] = work.column(k, a).astype(work.acc[a].dtype)
            cp = remote(work.acc[a].at[4 * k], rz[a].at[k], sz.at[k, a], vz.at[k, a], (t ^ (2 * k), m))
            cp.start()
            along.append(cp)
    for a in range(later):
        total = part[a][0].astype(F32)
        for k in (1, 2, 3):
            landed(rzp[a].at[k], vzp.at[k, a])
            total = total + rzp[a][k].astype(F32)
        outs[now + a][...] = total
    for a in range(now):
        total = work.column(0, a)
        for k in (1, 2, 3):
            landed(rz[a].at[k], vz.at[k, a])
            total = total + rz[a][k].astype(F32)
        outs[a][...] = total
    work.finish()
    for cp in along:
        cp.wait_send()


def last_sums(now, later, cid):
    a, b = len(now), len(later)
    arrays = list(now) + list(later)
    return pl.pallas_call(
        functools.partial(last_sums_kernel, a, b),
        out_shape=tuple(jax.ShapeDtypeStruct(w.shape[1:], F32) for w in arrays),
        in_specs=[VMEMS] * (a + b),
        out_specs=(VMEMS,) * (a + b),
        scratch_shapes=sums_scratch(now)
        + [pltpu.VMEM((4,) + w.shape[1:], w.dtype) for w in arrays]
        + [DMA((4, a)), DMA((4, a)), DMA((4, b)), DMA((4, b))],
        name="last_sums",
        compiler_params=pltpu.CompilerParams(collective_id=cid, has_side_effects=True, vmem_limit_bytes=40 << 20),
    )(*arrays)


def packed(pieces):
    flat = jnp.concatenate(pieces, axis=-1)
    fill = 1024 - flat.shape[-1]
    flat = jnp.pad(flat, [(0, 0)] * (flat.ndim - 1) + [(0, fill)])
    return flat.reshape(flat.shape[:-1] + (8, 128))


def by_heads(
    tokens,
    cotangent,
    starts,
    w_qkv,
    b_query,
    b_value,
    w_out,
    b_out,
    gain_one,
    shift_one,
    gain_two,
    shift_two,
    w_expand,
    b_expand,
    w_shrink,
    b_shrink,
):
    rows, width = tokens.shape[1:]
    hidden = b_expand.shape[0] * 32
    small = [b_query, b_value, b_out, gain_one, shift_one, gain_two, shift_two, b_shrink, b_expand]
    small = [v.astype(BF).astype(F32) for v in small] + [starts[0].astype(F32)]
    full_qkv, smalls, *rest = first_gather(
        [w_qkv.astype(BF), packed(small)], [w_out.astype(BF), w_expand.astype(BF), w_shrink.astype(BF)], 0
    )
    full_qkv = full_qkv.reshape(width, -1)
    smalls = smalls.reshape(32, 1024)
    step = width // 32
    vecs = [smalls[:, i * step : (i + 1) * step].reshape(width) for i in range(8)]
    query_bias, value_bias, out_bias, gain_first, shift_first, gain_second, shift_second, shrink_bias = vecs
    expand_bias = smalls[:, 8 * step : 8 * step + hidden // 32].reshape(hidden)
    at = 8 * step + hidden // 32
    all_starts = smalls[:4, at : at + 4].astype(jnp.int32)
    t, m, z, x, y, c = place()
    starts2 = jnp.stack([starts[0], lax.dynamic_index_in_dim(all_starts, 2 * y + x, 0, keepdims=False)])

    inputs = tokens[0].astype(F32)
    upstream_low = cotangent[0]
    normed = layer_norm(inputs, gain_first, shift_first).astype(BF)
    joined = jnp.einsum("de,rd->er", full_qkv, normed, preferred_element_type=F32)
    bias = jnp.concatenate([query_bias, jnp.zeros_like(query_bias), value_bias])
    joined = (joined + bias[:, None]).astype(BF).reshape(3, 12, HD, rows)
    (heads, out_full, log_sum, attention), rest = attend(starts2, joined, rest, 1)
    full_out, full_expand, full_shrink = (w.reshape(-1, w.shape[-1]) for w in rest)
    attention = attention.reshape(width, rows)
    hidden_one = inputs + (
        jnp.einsum("dr,de->re", attention, full_out, preferred_element_type=F32) + out_bias
    )
    normed_two = layer_norm(hidden_one, gain_second, shift_second).astype(BF)
    expanded = jnp.dot(normed_two, full_expand, preferred_element_type=F32) + expand_bias
    activated = gelu_tanh(expanded).astype(BF)
    layer_out = hidden_one + (jnp.dot(activated, full_shrink, preferred_element_type=F32) + shrink_bias)
    upstream = upstream_low.astype(F32)
    db_shrink = jnp.sum(upstream, axis=0)
    dw_shrink = jnp.einsum("rf,rd->fd", activated, upstream_low, preferred_element_type=F32)
    grad_act = jnp.einsum("rd,fd->rf", upstream_low, full_shrink, preferred_element_type=F32)
    grad_expand = jax.vjp(gelu_tanh, expanded)[1](grad_act)[0].astype(BF)
    db_expand = jnp.sum(grad_expand.astype(F32), axis=0)
    dw_expand = jnp.einsum("rd,rf->df", normed_two, grad_expand, preferred_element_type=F32)
    grad_normed_two = jnp.einsum("rf,df->rd", grad_expand, full_expand, preferred_element_type=F32)
    pull = jax.vjp(layer_norm, hidden_one, gain_second, shift_second)[1]
    grad_hidden_part, dgain_two, dshift_two = pull(grad_normed_two)
    grad_hidden = upstream + grad_hidden_part
    grad_attn = grad_hidden.astype(BF)
    db_out = jnp.sum(grad_attn.astype(F32), axis=0)
    dw_out = jnp.einsum("dr,re->de", attention, grad_attn, preferred_element_type=F32)
    grad_mix = jnp.einsum("de,re->dr", full_out, grad_attn, preferred_element_type=F32)
    shards = lambda w: w.astype(BF).reshape((32, -1) + w.shape[1:])
    grad_joined, rest = attend_back(
        starts2,
        grad_mix.astype(BF).reshape(12, HD, rows),
        heads,
        out_full,
        log_sum,
        [shards(dw_out), shards(dw_expand), shards(dw_shrink)],
        2,
    )
    grad_joined = grad_joined.reshape(3 * width, rows)
    db_query = jnp.sum(grad_joined[:width].astype(F32), axis=1)
    db_value = jnp.sum(grad_joined[2 * width :].astype(F32), axis=1)
    dw_qkv = jnp.einsum("rd,er->de", normed, grad_joined, preferred_element_type=F32)
    grad_normed = jnp.einsum("er,de->rd", grad_joined, full_qkv, preferred_element_type=F32)
    pull = jax.vjp(layer_norm, inputs, gain_first, shift_first)[1]
    grad_input_part, dgain_one, dshift_one = pull(grad_normed)
    dtokens = grad_hidden + grad_input_part
    parts = [db_query, db_value, db_out, dgain_one, dshift_one, dgain_two, dshift_two, db_shrink, db_expand]
    dw_qkv, smalls, dw_out, dw_expand, dw_shrink = last_sums(
        [shards(dw_qkv), packed([v.reshape(32, -1) for v in parts])], rest, 3
    )
    flat = smalls.reshape(1024)
    vecs = [flat[i * step : (i + 1) * step] for i in range(8)]
    db_query, db_value, db_out, dgain_one, dshift_one, dgain_two, dshift_two, db_shrink = vecs
    db_expand = flat[8 * step : at]
    return (
        layer_out.astype(BF).reshape(1, rows, width),
        dtokens.reshape(1, rows, width),
        dw_qkv,
        db_query,
        db_value,
        dw_out,
        db_out,
        dgain_one,
        dshift_one,
        dgain_two,
        dshift_two,
        dw_expand,
        db_expand,
        dw_shrink,
        db_shrink,
    )


def solution(mesh):
    rows, vector, seq = P(("tok", "mdl"), None), P(("tok", "mdl")), P("mdl", "tok", None)
    by_name = dict(m=rows, v=vector, s=seq)
    fits = mesh.shape["tok"] == 8 and mesh.shape["mdl"] == 4
    return jax.shard_map(
        by_heads if fits else general,
        mesh=mesh,
        in_specs=(seq, seq, P("mdl", None)) + tuple(by_name[k] for k in "mvvmvvvvvmvmv"),
        out_specs=tuple(by_name[k] for k in "ssmvvmvvvvvmvmv"),
        check_vma=False,
    )
```

```python
import functools
import math

import jax
import jax.numpy as jnp
from jax import lax
from jax.experimental import pallas as pl
from jax.experimental.pallas import tpu as pltpu
from jax.sharding import PartitionSpec as P

HD = 64
PIECE = 256
KEYB = 512


epsilon = 1e-05
masked_score = -1e30
gelu_coeff = 0.7978845608028654


def layer_norm(values, gain_vec, shift_vec):
    center = values - jnp.mean(values, axis=-1, keepdims=True)
    spread = jnp.mean(center * center, axis=-1, keepdims=True)
    return center * lax.rsqrt(spread + epsilon) * gain_vec + shift_vec


def gelu_tanh(inputs):
    return (
        0.5 * inputs * (1.0 + jnp.tanh(gelu_coeff * (inputs + 0.044715 * inputs * inputs * inputs)))
    )


def piece_ids(begins, positions):
    inside = (positions[:, None] >= begins[None, :]) & (
        positions[:, None] < begins[None, :] + PIECE
    )
    labels = jnp.arange(1, begins.shape[0] + 1, dtype=jnp.int32)
    return jnp.sum(jnp.where(inside, labels[None, :], 0), axis=1) - 1


def block_scores(query_heads, key_heads, query_pos, query_lab, begins, block_index, scaling):
    key_block = lax.dynamic_slice_in_dim(key_heads, block_index * KEYB, KEYB, 0)
    key_pos = block_index * KEYB + jnp.arange(KEYB, dtype=jnp.int32)
    key_lab = piece_ids(begins, key_pos)
    scores = (
        jnp.einsum("qhd,khd->hqk", query_heads, key_block, preferred_element_type=jnp.float32)
        * scaling
    )
    allowed = (key_pos[None, :] <= query_pos[:, None]) | (
        key_lab[None, :] == query_lab[:, None]
    ) & (query_lab[:, None] >= 0)
    return jnp.where(allowed[None, :, :], scores, masked_score)


def attend_forward(
    query_heads, key_heads, value_heads, query_pos, query_lab, begins, needed, scaling
):
    local_rows = query_heads.shape[0]
    head_count = query_heads.shape[1]

    def stats_step(block_index, loop_state):
        highest, summed = loop_state
        masked = block_scores(
            query_heads, key_heads, query_pos, query_lab, begins, block_index, scaling
        )
        new_high = jnp.maximum(highest, jnp.max(masked, axis=-1))
        summed = summed * jnp.exp(highest - new_high) + jnp.sum(
            jnp.exp(masked - new_high[:, :, None]), axis=-1
        )
        return (new_high, summed)

    starting = (
        jnp.full((head_count, local_rows), masked_score, jnp.float32),
        jnp.zeros((head_count, local_rows), jnp.float32),
    )
    highest, summed = lax.fori_loop(0, needed, stats_step, starting)

    def mix_step(block_index, running):
        masked = block_scores(
            query_heads, key_heads, query_pos, query_lab, begins, block_index, scaling
        )
        prob_low = (jnp.exp(masked - highest[:, :, None]) / summed[:, :, None]).astype(jnp.bfloat16)
        value_block = lax.dynamic_slice_in_dim(value_heads, block_index * KEYB, KEYB, 0)
        return running + jnp.einsum(
            "hqk,khd->qhd", prob_low, value_block, preferred_element_type=jnp.float32
        )

    mixture = lax.fori_loop(0, needed, mix_step, jnp.zeros(query_heads.shape, jnp.float32))
    return (mixture, highest, summed)


def attend_backward(
    query_heads,
    key_heads,
    value_heads,
    grad_heads,
    mixture,
    query_pos,
    query_lab,
    begins,
    needed,
    highest,
    summed,
    scaling,
):
    row_delta = jnp.einsum("qhd,qhd->hq", grad_heads.astype(jnp.float32), mixture)

    def grad_step(block_index, loop_state):
        grad_query, grad_keys, grad_values = loop_state
        masked = block_scores(
            query_heads, key_heads, query_pos, query_lab, begins, block_index, scaling
        )
        prob_full = jnp.exp(masked - highest[:, :, None]) / summed[:, :, None]
        offset = block_index * KEYB
        value_block = lax.dynamic_slice_in_dim(value_heads, offset, KEYB, 0)
        grad_probs = jnp.einsum(
            "qhd,khd->hqk", grad_heads, value_block, preferred_element_type=jnp.float32
        )
        grad_scores = (prob_full * (grad_probs - row_delta[:, :, None])).astype(jnp.bfloat16)
        key_block = lax.dynamic_slice_in_dim(key_heads, offset, KEYB, 0)
        grad_query = (
            grad_query
            + jnp.einsum("hqk,khd->qhd", grad_scores, key_block, preferred_element_type=jnp.float32)
            * scaling
        )
        key_part = (
            jnp.einsum("hqk,qhd->khd", grad_scores, query_heads, preferred_element_type=jnp.float32)
            * scaling
        )
        value_part = jnp.einsum(
            "hqk,qhd->khd",
            prob_full.astype(jnp.bfloat16),
            grad_heads,
            preferred_element_type=jnp.float32,
        )
        grad_keys = lax.dynamic_update_slice_in_dim(
            grad_keys, lax.dynamic_slice_in_dim(grad_keys, offset, KEYB, 0) + key_part, offset, 0
        )
        grad_values = lax.dynamic_update_slice_in_dim(
            grad_values,
            lax.dynamic_slice_in_dim(grad_values, offset, KEYB, 0) + value_part,
            offset,
            0,
        )
        return (grad_query, grad_keys, grad_values)

    starting = (
        jnp.zeros(query_heads.shape, jnp.float32),
        jnp.zeros(key_heads.shape, jnp.float32),
        jnp.zeros(value_heads.shape, jnp.float32),
    )
    return lax.fori_loop(0, needed, grad_step, starting)


def general(
    tokens,
    cotangent,
    starts,
    w_qkv,
    b_query,
    b_value,
    w_out,
    b_out,
    gain_one,
    shift_one,
    gain_two,
    shift_two,
    w_expand,
    b_expand,
    w_shrink,
    b_shrink,
):
    (
        full_qkv,
        full_bq,
        full_bv,
        full_out,
        full_bo,
        full_gone,
        full_sone,
        full_gtwo,
        full_stwo,
        full_expand,
        full_bexp,
        full_shrink,
        full_bshr,
    ) = (
        lax.all_gather(w_qkv.astype(jnp.bfloat16), ("tok", "mdl"), axis=0, tiled=True),
        lax.all_gather(b_query.astype(jnp.bfloat16), ("tok", "mdl"), axis=0, tiled=True),
        lax.all_gather(b_value.astype(jnp.bfloat16), ("tok", "mdl"), axis=0, tiled=True),
        lax.all_gather(w_out.astype(jnp.bfloat16), ("tok", "mdl"), axis=0, tiled=True),
        lax.all_gather(b_out.astype(jnp.bfloat16), ("tok", "mdl"), axis=0, tiled=True),
        lax.all_gather(gain_one.astype(jnp.bfloat16), ("tok", "mdl"), axis=0, tiled=True),
        lax.all_gather(shift_one.astype(jnp.bfloat16), ("tok", "mdl"), axis=0, tiled=True),
        lax.all_gather(gain_two.astype(jnp.bfloat16), ("tok", "mdl"), axis=0, tiled=True),
        lax.all_gather(shift_two.astype(jnp.bfloat16), ("tok", "mdl"), axis=0, tiled=True),
        lax.all_gather(w_expand.astype(jnp.bfloat16), ("tok", "mdl"), axis=0, tiled=True),
        lax.all_gather(b_expand.astype(jnp.bfloat16), ("tok", "mdl"), axis=0, tiled=True),
        lax.all_gather(w_shrink.astype(jnp.bfloat16), ("tok", "mdl"), axis=0, tiled=True),
        lax.all_gather(b_shrink.astype(jnp.bfloat16), ("tok", "mdl"), axis=0, tiled=True),
    )
    query_bias = full_bq.astype(jnp.float32)
    value_bias = full_bv.astype(jnp.float32)
    out_bias = full_bo.astype(jnp.float32)
    gain_first = full_gone.astype(jnp.float32)
    shift_first = full_sone.astype(jnp.float32)
    gain_second = full_gtwo.astype(jnp.float32)
    shift_second = full_stwo.astype(jnp.float32)
    expand_bias = full_bexp.astype(jnp.float32)
    shrink_bias = full_bshr.astype(jnp.float32)
    local_rows = tokens.shape[1]
    model_width = tokens.shape[2]
    head_count = model_width // HD
    group_size = lax.axis_size("tok")
    member = lax.axis_index("tok")
    seq_len = local_rows * group_size
    scaling = HD ** (-0.5)
    needed = jnp.minimum(
        seq_len // KEYB, ((member + 1) * local_rows + PIECE - 1 + KEYB - 1) // KEYB
    )
    begins = starts[0]
    query_pos = member * local_rows + jnp.arange(local_rows, dtype=jnp.int32)
    query_lab = piece_ids(begins, query_pos)
    token_rows = tokens[0]
    cotangent_rows = cotangent[0]
    inputs = token_rows.astype(jnp.float32)
    normed = layer_norm(inputs, gain_first, shift_first).astype(jnp.bfloat16)
    joined = jnp.dot(normed, full_qkv, preferred_element_type=jnp.float32)
    queries = (joined[:, :model_width] + query_bias).astype(jnp.bfloat16)
    keys_own = joined[:, model_width : 2 * model_width].astype(jnp.bfloat16)
    values_own = (joined[:, 2 * model_width :] + value_bias).astype(jnp.bfloat16)
    key_full, value_full = (
        lax.all_gather(keys_own, "tok", axis=0, tiled=True),
        lax.all_gather(values_own, "tok", axis=0, tiled=True),
    )
    query_heads = queries.reshape(local_rows, head_count, HD)
    mixture, highest, summed = attend_forward(
        query_heads,
        key_full.reshape(seq_len, head_count, HD),
        value_full.reshape(seq_len, head_count, HD),
        query_pos,
        query_lab,
        begins,
        needed,
        scaling,
    )
    attention = mixture.reshape(local_rows, model_width).astype(jnp.bfloat16)
    hidden_one = inputs + (
        jnp.dot(attention, full_out, preferred_element_type=jnp.float32) + out_bias
    )
    normed_two = layer_norm(hidden_one, gain_second, shift_second).astype(jnp.bfloat16)
    expanded = jnp.dot(normed_two, full_expand, preferred_element_type=jnp.float32) + expand_bias
    activated = gelu_tanh(expanded).astype(jnp.bfloat16)
    layer_out = hidden_one + (
        jnp.dot(activated, full_shrink, preferred_element_type=jnp.float32) + shrink_bias
    )
    upstream = cotangent_rows.astype(jnp.float32)
    db_shrink = jnp.sum(upstream, axis=0)
    dw_shrink = jnp.einsum(
        "rf,rd->fd", activated, cotangent_rows, preferred_element_type=jnp.float32
    )
    grad_act = jnp.einsum(
        "rd,fd->rf", cotangent_rows, full_shrink, preferred_element_type=jnp.float32
    )
    gelu_pull = jax.vjp(gelu_tanh, expanded)[1]
    grad_expand = gelu_pull(grad_act)[0].astype(jnp.bfloat16)
    db_expand = jnp.sum(grad_expand.astype(jnp.float32), axis=0)
    dw_expand = jnp.einsum("rd,rf->df", normed_two, grad_expand, preferred_element_type=jnp.float32)
    grad_normed_two = jnp.einsum(
        "rf,df->rd", grad_expand, full_expand, preferred_element_type=jnp.float32
    )
    norm_pull = jax.vjp(layer_norm, hidden_one, gain_second, shift_second)[1]
    grad_hidden_part, dgain_two, dshift_two = norm_pull(grad_normed_two)
    grad_hidden = upstream + grad_hidden_part
    grad_attn = grad_hidden.astype(jnp.bfloat16)
    db_out = jnp.sum(grad_attn.astype(jnp.float32), axis=0)
    dw_out = jnp.einsum("rd,re->de", attention, grad_attn, preferred_element_type=jnp.float32)
    grad_mix = jnp.einsum(
        "re,de->rd", grad_attn, full_out, preferred_element_type=jnp.float32
    ).astype(jnp.bfloat16)
    key_back, value_back = (key_full, value_full)
    grad_query, grad_keys, grad_values = attend_backward(
        query_heads,
        key_back.reshape(seq_len, head_count, HD),
        value_back.reshape(seq_len, head_count, HD),
        grad_mix.reshape(local_rows, head_count, HD),
        mixture,
        query_pos,
        query_lab,
        begins,
        needed,
        highest,
        summed,
        scaling,
    )
    key_share, value_share = (
        lax.psum_scatter(
            grad_keys.reshape(seq_len, model_width).astype(jnp.bfloat16),
            "tok",
            scatter_dimension=0,
            tiled=True,
        ).astype(jnp.float32),
        lax.psum_scatter(
            grad_values.reshape(seq_len, model_width).astype(jnp.bfloat16),
            "tok",
            scatter_dimension=0,
            tiled=True,
        ).astype(jnp.float32),
    )
    grad_joined = jnp.concatenate(
        [
            grad_query.reshape(local_rows, model_width).astype(jnp.bfloat16),
            key_share.astype(jnp.bfloat16),
            value_share.astype(jnp.bfloat16),
        ],
        axis=1,
    )
    db_query = jnp.sum(grad_joined[:, :model_width].astype(jnp.float32), axis=0)
    db_value = jnp.sum(grad_joined[:, 2 * model_width :].astype(jnp.float32), axis=0)
    dw_qkv = jnp.einsum("rd,re->de", normed, grad_joined, preferred_element_type=jnp.float32)
    grad_normed = jnp.einsum("re,de->rd", grad_joined, full_qkv, preferred_element_type=jnp.float32)
    norm_pull_first = jax.vjp(layer_norm, inputs, gain_first, shift_first)[1]
    grad_input_part, dgain_one, dshift_one = norm_pull_first(grad_normed)
    dtokens = grad_hidden + grad_input_part
    (
        dw_qkv,
        db_query,
        db_value,
        dw_out,
        db_out,
        dgain_one,
        dshift_one,
        dgain_two,
        dshift_two,
        dw_expand,
        db_expand,
        dw_shrink,
        db_shrink,
    ) = (
        lax.psum_scatter(dw_qkv, ("tok", "mdl"), scatter_dimension=0, tiled=True),
        lax.psum_scatter(db_query, ("tok", "mdl"), scatter_dimension=0, tiled=True),
        lax.psum_scatter(db_value, ("tok", "mdl"), scatter_dimension=0, tiled=True),
        lax.psum_scatter(dw_out, ("tok", "mdl"), scatter_dimension=0, tiled=True),
        lax.psum_scatter(db_out, ("tok", "mdl"), scatter_dimension=0, tiled=True),
        lax.psum_scatter(dgain_one, ("tok", "mdl"), scatter_dimension=0, tiled=True),
        lax.psum_scatter(dshift_one, ("tok", "mdl"), scatter_dimension=0, tiled=True),
        lax.psum_scatter(dgain_two, ("tok", "mdl"), scatter_dimension=0, tiled=True),
        lax.psum_scatter(dshift_two, ("tok", "mdl"), scatter_dimension=0, tiled=True),
        lax.psum_scatter(dw_expand, ("tok", "mdl"), scatter_dimension=0, tiled=True),
        lax.psum_scatter(db_expand, ("tok", "mdl"), scatter_dimension=0, tiled=True),
        lax.psum_scatter(dw_shrink, ("tok", "mdl"), scatter_dimension=0, tiled=True),
        lax.psum_scatter(db_shrink, ("tok", "mdl"), scatter_dimension=0, tiled=True),
    )
    return (
        layer_out.astype(jnp.bfloat16).reshape(1, local_rows, model_width),
        dtokens.reshape(1, local_rows, model_width),
        dw_qkv,
        db_query,
        db_value,
        dw_out,
        db_out,
        dgain_one,
        dshift_one,
        dgain_two,
        dshift_two,
        dw_expand,
        db_expand,
        dw_shrink,
        db_shrink,
    )


BLK = 512
LOG_SCALE = math.log2(math.e) * HD ** (-0.5)
F32 = jnp.float32
BF = jnp.bfloat16


def nn(a, b):
    return lax.dot_general(a, b, (((1,), (0,)), ((), ())), preferred_element_type=F32)


def nt(a, b):
    return lax.dot_general(a, b, (((1,), (1,)), ((), ())), preferred_element_type=F32)


def diag_units(task):
    return [
        (2 * task, 0, "diag", 0, BLK, 0, BLK),
        (2 * task, 1, None, 0, BLK, 0, BLK),
        (2 * task + 1, 1, "diag", 0, BLK, 0, BLK),
        (2 * task + 1, 0, "piece", 0, PIECE, BLK - PIECE, PIECE),
    ]


def unit_mask(unit, task, begin):
    j, h, kind, k0, nk, q0, nq = unit
    keys = j * BLK + k0
    queries = (2 * task + h) * BLK + q0
    kc = keys + lax.broadcasted_iota(jnp.int32, (nk, 1), 0)
    qr = queries + lax.broadcasted_iota(jnp.int32, (1, nq), 1)
    kin = ((kc >= begin) & (kc < begin + PIECE)).astype(F32)
    qin = ((qr >= begin) & (qr < begin + PIECE)).astype(F32)
    both = (kin * qin) > 0.5
    if kind == "piece":
        return both
    return (kc <= qr) | both


def forward_units(slot, task, units, begin, xv, kn, acc, ms, ls):
    def score(unit):
        j, h, kind, k0, nk, q0, nq = unit
        s = nn(kn[slot, j, k0 : k0 + nk, :], xv[slot, 2 * task + h, 0, :, q0 : q0 + nq]) * LOG_SCALE
        if kind:
            s = jnp.where(unit_mask(unit, task, begin), s, masked_score)
        return s

    ahead = score(units[0])
    for n, unit in enumerate(units):
        j, h, kind, k0, nk, q0, nq = unit
        now = ahead
        if n + 1 < len(units):
            ahead = score(units[n + 1])
        qs = slice(q0, q0 + nq)
        high = jnp.maximum(ms[h, :, qs], jnp.max(now, axis=0, keepdims=True))
        fade = jnp.exp2(ms[h, :, qs] - high)
        p = jnp.exp2(now - high)
        ls[h, :, qs] = ls[h, :, qs] * fade + jnp.sum(p, axis=0, keepdims=True)
        ms[h, :, qs] = high
        acc[h, :, qs] = acc[h, :, qs] * fade + nn(xv[slot, j, 2, :, k0 : k0 + nk], p.astype(BF))


def forward_task(slot, task, begin, xv, kn, acc, ms, ls):
    ms[...] = jnp.full_like(ms, masked_score)
    ls[...] = jnp.zeros_like(ls)
    acc[...] = jnp.zeros_like(acc)

    def step(j, carry):
        forward_units(
            slot, task, [(j, h, None, 0, BLK, 0, BLK) for h in range(2)], begin, xv, kn, acc, ms, ls
        )
        return carry

    lax.fori_loop(0, 2 * task, step, 0)
    forward_units(slot, task, diag_units(task), begin, xv, kn, acc, ms, ls)


def backward_units(slot, task, row, key, units, begin, xv, gv, kn, vn, lsum, delta, dkv, dq):
    def score(unit):
        j, h, kind, k0, nk, q0, nq = unit
        b = 2 * task + h
        s = nn(kn[slot, j, k0 : k0 + nk, :], xv[slot, b, 0, :, q0 : q0 + nq]) * LOG_SCALE
        return s, nn(vn[slot, j, k0 : k0 + nk, :], gv[slot, b, :, q0 : q0 + nq])

    ahead = score(units[0])
    for n, unit in enumerate(units):
        j, h, kind, k0, nk, q0, nq = unit
        b = 2 * task + h
        s, dp = ahead
        if n + 1 < len(units):
            ahead = score(units[n + 1])
        p = jnp.exp2(s - lsum[slot, b, :, q0 : q0 + nq])
        if kind:
            p = jnp.where(unit_mask(unit, task, begin), p, 0.0)
        ds = (p * (dp - delta[slot, b, :, q0 : q0 + nq])).astype(BF)
        dkv[key + j, 1, :, k0 : k0 + nk] += nt(gv[slot, b, :, q0 : q0 + nq], p.astype(BF))
        dkv[key + j, 0, :, k0 : k0 + nk] += nt(xv[slot, b, 0, :, q0 : q0 + nq], ds)
        dq[row + h, :, q0 : q0 + nq] += nn(xv[slot, j, 1, :, k0 : k0 + nk], ds)


MESH_ID = pl.DeviceIdType.MESH
ANYS = pl.BlockSpec(memory_space=pl.ANY)
VMEMS = pl.BlockSpec(memory_space=pltpu.VMEM)
SMEMS = pl.BlockSpec(memory_space=pltpu.SMEM)
DMA = pltpu.SemaphoreType.DMA


def place():
    t = lax.axis_index("tok")
    m = lax.axis_index("mdl")
    return t, m, t // 2, t % 2, m // 2, m % 2


def greet(peers):
    barrier = pltpu.get_barrier_semaphore()
    for peer in peers:
        pl.semaphore_signal(barrier, inc=1, device_id=peer, device_id_type=MESH_ID)
    return lambda: pl.semaphore_wait(barrier, len(peers))


def meet(peers):
    greet(peers)()


def chip_group(t, m):
    return [(t ^ k, m ^ b) for k in range(8) for b in range(2) if (k, b) != (0, 0)]


def column_group(t, m):
    return [(t ^ 2, m), (t ^ 4, m), (t ^ 6, m), (t ^ 1, m), (t, m ^ 2), (t, m ^ 1)]


def remote(src, dst, ssem, rsem, dev):
    return pltpu.make_async_remote_copy(
        src_ref=src, dst_ref=dst, send_sem=ssem, recv_sem=rsem, device_id=dev, device_id_type=MESH_ID
    )


def landed(ref, sem):
    pltpu.make_async_copy(ref, ref, sem).wait()


def send_unless(here, src, dst, ssem, rsem, dev):
    @pl.when(here)
    def _():
        pltpu.make_async_copy(src, dst, rsem).start()

    @pl.when(jnp.logical_not(here))
    def _():
        remote(src, dst, ssem, rsem, dev).start()


def sent_unless(here, src, dst, ssem, rsem, dev):
    @pl.when(jnp.logical_not(here))
    def _():
        remote(src, dst, ssem, rsem, dev).wait_send()


class Pushes:
    def __init__(self, outs, send, recv):
        self.outs, self.send, self.recv, self.started = outs, send, recv, []

    def push(self, shard, dev, src=None):
        e = len(self.started)
        todo = []
        for a, out in enumerate(self.outs):
            cp = remote(
                out.at[shard] if src is None else src[a],
                out.at[shard],
                self.send.at[e, a],
                self.recv.at[a, shard],
                dev,
            )
            cp.start()
            todo.append(cp)
        self.started.append(todo)

    def arrived(self, shard):
        for a, out in enumerate(self.outs):
            landed(out.at[shard], self.recv.at[a, shard])

    def finish(self):
        for todo in self.started:
            for cp in todo:
                cp.wait_send()


class Line:
    def __init__(self, outs, send, recv):
        self.outs, self.send, self.recv = outs, send, recv
        self.t, self.m = lax.axis_index("tok"), lax.axis_index("mdl")
        self.z = self.t // 2
        self.chips = lax.axis_size("tok") // 2

    def ways(self, hop):
        up = (0, (self.z >= hop) & (self.z < self.chips - 1), self.t - 2 * hop, self.t + 2)
        down = (1, (self.z + hop < self.chips) & (self.z > 0), self.t + 2 * hop, self.t - 2)
        return up, down

    def copies(self, hop, way, shard, to, src=None):
        at = 4 * shard + self.m
        return [
            remote(
                out.at[at] if src is None else src[a],
                out.at[at],
                self.send.at[2 * hop + way, a],
                self.recv.at[a, at],
                (to, self.m),
            )
            for a, out in enumerate(self.outs)
        ]

    def own(self, src):
        for way, there, shard, to in self.ways(0):

            @pl.when(there)
            def _():
                for cp in self.copies(0, way, shard, to, src):
                    cp.start()

    def hop(self, hop):
        for way, there, shard, to in self.ways(hop):
            comes = (self.z >= hop) if way == 0 else (self.z + hop < self.chips)

            @pl.when(comes)
            def _():
                at = 4 * shard + self.m
                for a, out in enumerate(self.outs):
                    landed(out.at[at], self.recv.at[a, at])

            if hop < self.chips - 1:

                @pl.when(there)
                def _():
                    for cp in self.copies(hop, way, shard, to):
                        cp.start()

    def finish(self, src):
        for hop in range(self.chips - 1):
            for way, there, shard, to in self.ways(hop):

                @pl.when(there)
                def _():
                    for cp in self.copies(hop, way, shard, to, src if hop == 0 else None):
                        cp.wait_send()


def in_parts(shape, body):
    rows, width = shape
    if rows % 24 or width % 768:
        body((slice(None), slice(None)))
        return
    across = width // 768

    def step(i, carry):
        r = pl.multiple_of(i // across * 24, 8)
        c = pl.multiple_of(i % across * 768, 128)
        body((pl.ds(r, 24), pl.ds(c, 768)))
        return carry

    lax.fori_loop(0, rows // 24 * across, step, 0)


class Sums:
    def __init__(self, ins, acc, r1, rx, ry, rd, s1, v1, ss, vx, vy, vd, own=None):
        self.own = own
        self.t, self.m = lax.axis_index("tok"), lax.axis_index("mdl")
        self.ins, self.acc, self.r1, self.rx, self.ry, self.rd = ins, acc, r1, rx, ry, rd
        self.s1, self.v1, self.ss, self.vx, self.vy, self.vd = s1, v1, ss, vx, vy, vd
        self.count = len(ins)
        self.started = []

    def owner(self, n):
        return self.t ^ (2 * (n // 4) + (n // 2) % 2), self.m ^ (2 * (n % 2))

    def first(self, n, a):
        tt, mm = self.owner(n)
        return remote(
            self.ins[a].at[4 * tt + (mm ^ 1)], self.r1[a].at[n], self.s1.at[n, a], self.v1.at[n, a], (self.t, self.m ^ 1)
        )

    def begin(self, which=None):
        for n in (15, 11, 14, 10, 7, 3, 5, 1, 6, 2, 13, 9, 12, 8, 4, 0):
            for a in range(self.count) if which is None else which:
                self.first(n, a).start()
                if self.own is not None:
                    tt, mm = self.owner(n)
                    pltpu.make_async_copy(self.ins[a].at[4 * tt + mm], self.acc[a].at[n], self.own.at[n, a]).start()

    def hop(self, e, n, dst, slot, vsem, by_x):
        dev = (self.t ^ 1, self.m) if by_x else (self.t, self.m ^ 2)
        return [
            remote(self.acc[a].at[n], dst[a].at[slot], self.ss.at[e, a], vsem.at[slot, a], dev)
            for a in range(self.count)
        ]

    def push(self, *what):
        e = len(self.started)
        self.started.append(what)
        for cp in self.hop(e, *what):
            cp.start()

    def total(self, n, a, more, store):
        tt, mm = self.owner(n)
        self.first(n, a).wait_recv()
        if self.own is not None:
            landed(self.acc[a].at[n], self.own.at[n, a])
        for buf, slot, vsem in more:
            landed(buf[a].at[slot], vsem.at[slot, a])

        def add_part(part):
            out = self.acc[a][(n,) + part] if self.own is not None else self.ins[a][(4 * tt + mm,) + part]
            out = out.astype(F32) + self.r1[a][(n,) + part].astype(F32)
            for buf, slot, vsem in more:
                out = out + buf[a][(slot,) + part].astype(F32)
            store(part, out)

        in_parts(self.acc[a].shape[1:], add_part)

    def add(self, n, more=()):
        for a in range(self.count):
            self.add_one(n, a, more)

    def add_one(self, n, a, more):
        def store(part, out):
            self.acc[a][(n,) + part] = out.astype(self.acc[a].dtype)

        self.total(n, a, more, store)

    def early(self, by_y):
        for k in (3, 2, 1, 0):
            self.add(4 * k + 3)
            self.push(4 * k + 3, self.rd, k, self.vd, k >= by_y)
        for k in (3, 2, 1, 0):
            if k >= by_y:
                self.add(4 * k + 2)
                self.push(4 * k + 2, self.rx, k, self.vx, True)
            else:
                self.add(4 * k + 1)
                self.push(4 * k + 1, self.ry, k, self.vy, False)

    def late(self, by_y):
        for k in (3, 2, 1, 0):
            via = [(self.rd, k, self.vd)]
            if k < by_y:
                self.add(4 * k + 2, via)
                self.push(4 * k + 2, self.rx, k, self.vx, True)
            else:
                self.add(4 * k + 1, via)
                self.push(4 * k + 1, self.ry, k, self.vy, False)

    def column(self, k, a):
        self.add_one(4 * k, a, [(self.rx, k, self.vx), (self.ry, k, self.vy)])

    def column_out(self, a, out):
        def store(part, total):
            out[part] = total

        self.total(0, a, [(self.rx, 0, self.vx), (self.ry, 0, self.vy)], store)

    def finish(self):
        for n in range(16):
            for a in range(self.count):
                self.first(n, a).wait_send()
        for e, what in enumerate(self.started):
            for cp in self.hop(e, *what):
                cp.wait_send()


def sums_scratch(shards, outside):
    n = len(shards)
    bufs = [pltpu.VMEM((k,) + s, d) for k in (16, 16, 4, 4, 4) for s, d in shards]
    sems = [DMA((16, n)), DMA((16, n)), DMA((12, n)), DMA((4, n)), DMA((4, n)), DMA((4, n))]
    return bufs + sems + ([DMA((16, n))] if outside else [])


def take_sums(ins, refs, outside):
    n = len(ins)
    bufs = [refs[i * n : (i + 1) * n] for i in range(5)]
    end = 5 * n + 6 + outside
    return Sums(ins, *bufs, *refs[5 * n : end]), refs[end:]


SMALL_ROWS = 16


def side_by_side(smalls, width):
    step = width // 32
    lane = lax.broadcasted_iota(jnp.int32, (128, width), 0)
    col = lax.broadcasted_iota(jnp.int32, (128, width), 1)
    pick = (lax.rem(col, step) == lane).astype(BF)
    every = lax.dot_general(
        smalls.reshape(32 * SMALL_ROWS, 128).astype(BF), pick, (((1,), (0,)), ((), ())), preferred_element_type=F32
    )
    shard = lax.broadcasted_iota(jnp.int32, (32, SMALL_ROWS, width), 0)
    at = lax.broadcasted_iota(jnp.int32, (32, SMALL_ROWS, width), 2) // step
    return jnp.sum(jnp.where(shard == at, every.reshape(32, SMALL_ROWS, width), 0.0), axis=0)


def attend_kernel(*refs):
    (tokens_ref, starts_ref), masters, vectors = refs[:2], refs[2:6], refs[6:15]
    full_qkv, smalls_out, weights, (heads, of_ref, l_ref, att, begins) = refs[15], refs[16], refs[17:20], refs[20:25]
    (low_qkv, low0, low1, low2, small, smalls, wq, normed, jv, xv, kn, acc, ms, ls, stage) = refs[25:40]
    (s1, v1, local, s_full, r_full, s_sh, r_sh, s_fw, r_fw, s_out, r_out, keep, send, recv, send_z) = refs[40:]
    t, m, z, x, y, c = place()
    xn, yn, sib = (t ^ 1, m), (t, m ^ 2), (t, m ^ 1)
    own = x == c
    role = (x + c) % 2
    hf, hs, owner_m = 3 * z + 2 * x, 3 * z + 1, 2 * y + x
    lows = (low0, low1, low2)
    me = 4 * t + m
    step = low_qkv.shape[0]
    width = 32 * step

    met = greet(chip_group(t, m) + [yn])
    low_qkv[...] = masters[0][...].astype(BF)
    small[...] = jnp.zeros_like(small)
    for v in range(8):
        small[v : v + 1, 0:step] = vectors[v][...].astype(BF).astype(F32)
    for q in range(4):
        small[8 + q : 9 + q, 0:step] = vectors[8][:, q * step : (q + 1) * step].astype(BF).astype(F32)
    small[12:13, 0 : starts_ref.shape[1]] = starts_ref[...].astype(F32)
    smalls[me] = small[...]
    met()

    class Shards:
        def __init__(self, ref):
            self.at = self
            self.ref = ref

        def __getitem__(self, shard):
            return self.ref.at[pl.ds(pl.multiple_of(step * shard, 8), step)]

    first = Pushes((Shards(full_qkv), smalls), s1, v1)
    for dev in [(t ^ 2, m), (t ^ 4, m), (t ^ 6, m), xn, yn, sib]:
        first.push(me, dev, (low_qkv, small))
    work = Pushes(weights, send, recv)
    for low, master in zip(lows, masters[1:]):
        low[...] = master[...].astype(BF)
    column = Line(weights, send_z, recv)
    own_rows = [pltpu.make_async_copy(low_qkv, Shards(full_qkv)[me], local.at[0])]
    own_rows += [pltpu.make_async_copy(lows[a], weights[a].at[me], local.at[1 + a]) for a in range(3)]
    for cp in own_rows:
        cp.start()

    values = tokens_ref[...].astype(F32)
    center = values - jnp.mean(values, axis=-1, keepdims=True)
    spread = jnp.mean(center * center, axis=-1, keepdims=True)
    xhat = center * lax.rsqrt(spread + epsilon)

    for k in range(1, 4):
        shard = 4 * (t ^ (2 * k)) + m
        first.arrived(shard)
        for dev in (xn, yn, sib):
            first.push(shard, dev)
    column.own(lows)
    for k in range(4):
        col = t ^ (2 * k)
        xi, yi = 4 * (col ^ 1) + m, 4 * col + (m ^ 2)
        first.arrived(xi)
        if k < 2:
            first.push(xi, yn)
        first.push(xi, sib)
        first.arrived(yi)
        if k >= 2:
            first.push(yi, xn)
        first.push(yi, sib)
    column.hop(1)
    for k in range(4):
        di = 4 * (t ^ (2 * k) ^ 1) + (m ^ 2)
        first.arrived(di)
        first.push(di, sib)
    for k in range(4):
        for a in (0, 1):
            for b in (0, 2):
                first.arrived(4 * (t ^ (2 * k) ^ a) + (m ^ b ^ 1))
    column.hop(2)
    for cp in own_rows:
        cp.wait()
    load = pltpu.make_async_copy(full_qkv, wq, local.at[4])
    load.start()
    share = pltpu.make_async_copy(smalls, smalls_out, local.at[5])
    share.start()
    flat = side_by_side(smalls[...], width)
    normed[...] = (xhat * flat[3:4] + flat[4:5]).astype(BF)
    bias = jnp.concatenate([flat[0:1], jnp.zeros_like(flat[0:1]), flat[1:2]], axis=1)
    begins[0] = smalls[m, 12:13, :].astype(jnp.int32)
    begins[1] = smalls[owner_m, 12:13, :].astype(jnp.int32)
    load.wait()
    for n in range(9):
        part = slice(n * 256, (n + 1) * 256)
        block = lax.dot_general(
            normed[...], wq[:, part], (((1,), (0,)), ((), ())), preferred_element_type=F32
        )
        block = (block + bias[:, part]).T.astype(BF)
        for h in range(4):
            g = 4 * n + h
            jv[g // 12, g % 12] = block[h * HD : (h + 1) * HD]

    def full(k):
        d = t ^ k
        return jv.at[:, 3 * (d // 2) + 2 * (d % 2)], xv.at[0, t], s_full.at[k], r_full.at[t], (d, m)

    def shared(k):
        zd = z ^ k
        return jv.at[:, 3 * zd + 1], xv.at[1, t], s_sh.at[k], r_sh.at[t], (2 * zd + c, m)

    for k in (4, 5, 6, 7, 2, 3, 1):
        remote(*full(k)).start()
    loc = full(0)
    pltpu.make_async_copy(loc[0], loc[1], loc[3]).start()
    for dev in (xn, yn, sib):
        work.push(me, dev, lows)
    column.hop(3)
    for k in range(1, 4):
        for dev in (xn, yn, sib):
            work.push(4 * (t ^ (2 * k)) + m, dev)
    for k in range(1, 8):
        remote(*full(k)).wait_send()
    for k in (2, 3, 1):
        remote(*shared(k)).start()
    send_unless(own, *shared(0))

    def keep_head(slot):
        cp = pltpu.make_async_copy(xv.at[slot], heads.at[slot], keep.at[slot])
        cp.start()
        return cp

    for b in range(8):
        landed(xv.at[0, b], r_full.at[b])
    kept = [keep_head(0)]
    for b in range(8):
        kn[0, b] = xv[0, b, 1].T

    def begin_of(slot, task):
        lane = lax.broadcasted_iota(jnp.int32, (1, 128), 1)
        return jnp.sum(jnp.where(lane == task, begins[slot], 0), axis=1, keepdims=True)

    def finish_task(slot, task, row, head, mdl, alone):
        for h in range(2):
            b, u = 2 * task + h, 2 * row + h
            out = acc[h] / ls[h]
            of_ref[u] = out
            stage[u] = out.astype(BF)
            l_ref[u] = ms[h] + jnp.log2(ls[h])
            send_unless((b == t) & alone, stage.at[u], att.at[head], s_out.at[u], r_out.at[head], (b, mdl))

    def full_task(w, carry):
        forward_task(0, w, begin_of(0, w), xv, kn, acc, ms, ls)
        finish_task(0, w, w, hf, m, t >= 0)
        return carry

    lax.fori_loop(0, 3, full_task, 0)

    for k in range(4):
        col = t ^ (2 * k)
        xi, yi = 4 * (col ^ 1) + m, 4 * col + (m ^ 2)
        work.arrived(xi)
        if k < 3:
            work.push(xi, yn)
        work.push(xi, sib)
        work.arrived(yi)
        if k == 3:
            work.push(yi, xn)
        work.push(yi, sib)

    def forward(k):
        b = t ^ k
        return remote(xv.at[1, b], xv.at[1, b], s_fw.at[k], r_fw.at[b], sib)

    @pl.when(own)
    def _():
        for k in (0, 1, 2, 3, 6, 7, 4, 5):
            landed(xv.at[1, t ^ k], r_sh.at[t ^ k])
            forward(k).start()

    lax.fori_loop(3, 4, full_task, 0)

    @pl.when(jnp.logical_not(own))
    def _():
        for k in range(8):
            forward(k).wait_recv()

    kept.append(keep_head(1))
    for b in range(8):
        kn[1, b] = xv[1, b, 1].T

    def shared_task(n, carry):
        task = jnp.where(n == 0, role, 3 - role)
        forward_task(1, task, begin_of(1, task), xv, kn, acc, ms, ls)
        finish_task(1, task, 4 + n, hs, owner_m, own)
        return carry

    lax.fori_loop(0, 2, shared_task, 0)

    for k in range(4):
        di = 4 * (t ^ (2 * k) ^ 1) + (m ^ 2)
        work.arrived(di)
        work.push(di, sib)
    for h in range(12):
        landed(att.at[h], r_out.at[h])
    for k in range(4):
        for a in (0, 1):
            for b in (0, 2):
                work.arrived(4 * (t ^ (2 * k) ^ a) + (m ^ b ^ 1))
    first.finish()
    work.finish()
    column.finish(lows)
    for k in (1, 2, 3):
        remote(*shared(k)).wait_send()
    sent_unless(own, *shared(0))

    @pl.when(own)
    def _():
        for k in range(8):
            forward(k).wait_send()

    for w in range(4):
        for h in range(2):
            b, u = 2 * w + h, 2 * w + h
            sent_unless(b == t, stage.at[u], att.at[hf], s_out.at[u], r_out.at[hf], (b, m))
    for n in range(2):
        task = role if n == 0 else 3 - role
        for h in range(2):
            b, u = 2 * task + h, 8 + 2 * n + h
            sent_unless((b == t) & own, stage.at[u], att.at[hs], s_out.at[u], r_out.at[hs], (b, owner_m))
    for cp in kept:
        cp.wait()
    share.wait()


def attend(tokens, starts, masters, vectors, cid):
    rows, width = tokens.shape
    step = width // 32
    head = (HD, BLK)
    S, V = jax.ShapeDtypeStruct, pltpu.VMEM
    outs = pl.pallas_call(
        attend_kernel,
        out_shape=(S((width, 3 * width), BF), S((32, SMALL_ROWS, 128), F32))
        + tuple(S((32,) + w.shape, BF) for w in masters[1:])
        + (S((2, 8, 3) + head, BF), S((12,) + head, F32), S((12, 1, BLK), F32), S((12,) + head, BF), S((2, 1, 128), jnp.int32)),
        in_specs=[VMEMS] * 15,
        out_specs=(ANYS,) * 6 + (VMEMS, VMEMS, ANYS, VMEMS),
        scratch_shapes=[V(w.shape, BF) for w in masters]
        + [
            V((SMALL_ROWS, 128), F32),
            V((32, SMALL_ROWS, 128), F32),
            V((width, 3 * width), BF),
            V((rows, width), BF),
            V((3, 12) + head, BF),
            V((2, 8, 3) + head, BF),
            V((2, 8, BLK, HD), BF),
            V((2,) + head, F32),
            V((2, 1, BLK), F32),
            V((2, 1, BLK), F32),
            V((12,) + head, BF),
        ]
        + [DMA((31, 2)), DMA((2, 32)), DMA((6,))]
        + [DMA((8,)), DMA((8,)), DMA((4,)), DMA((8,)), DMA((8,)), DMA((8,)), DMA((12,)), DMA((12,)), DMA((2,))]
        + [DMA((28, 3)), DMA((3, 32)), DMA((6, 3))],
        name="attend",
        compiler_params=pltpu.CompilerParams(collective_id=cid, has_side_effects=True, vmem_limit_bytes=62 << 20),
    )(tokens, starts, *masters, *vectors)
    return outs[0], outs[1], outs[2:5], outs[5:]


FF_BLOCK = 512
HBMS = pl.BlockSpec(memory_space=pltpu.HBM)


def shard_rows(rows, step):
    r, n = rows.shape
    count = n // step
    shard = lax.broadcasted_iota(jnp.int32, (count, r, n), 0)
    at = lax.broadcasted_iota(jnp.int32, (count, r, n), 2) // step
    spread = jnp.where(shard == at, rows[None], 0.0).reshape(count * r, n)
    col = lax.broadcasted_iota(jnp.int32, (n, 128), 0)
    lane = lax.broadcasted_iota(jnp.int32, (n, 128), 1)
    pick = (lax.rem(col, step) == lane).astype(F32)
    out = lax.dot_general(
        spread, pick, (((1,), (0,)), ((), ())), precision=lax.Precision.HIGHEST, preferred_element_type=F32
    )
    return out.reshape(count, r, 128)


def expand_row(smalls, hidden):
    step = hidden // 128
    lane = lax.broadcasted_iota(jnp.int32, (128, hidden), 0)
    col = lax.broadcasted_iota(jnp.int32, (128, hidden), 1)
    pick = (lax.rem(col, step) == lane).astype(BF)
    every = nn(smalls[:, 8:12, :].reshape(128, 128).astype(BF), pick)
    return jnp.sum(jnp.where(lane == col // step, every, 0.0), axis=0, keepdims=True)


def middle_kernel(
    x_ref, c_ref, att_any, smalls_any, wo_any, we_ref, ws_ref,
    out_ref, gh_ref, gm_any, dwo_any, dwe_ref, dws_ref, flat, vec_ref, dbe_ref,
    be, hidden, xhat, inv, n2, n2t, out_acc, dn2, att_ref, smalls_ref, wo_ref, gm_ref, dwo_ref, sems,
):
    i = pl.program_id(0)
    last = pl.num_programs(0) - 1
    width = x_ref.shape[1]

    @pl.when(i == 0)
    def _():
        pairs = ((smalls_any, smalls_ref), (att_any, att_ref), (wo_any, wo_ref))
        loads = [pltpu.make_async_copy(a, b, sems.at[n]) for n, (a, b) in enumerate(pairs)]
        for cp in loads:
            cp.start()
        loads[0].wait()
        flat[...] = side_by_side(smalls_ref[...], width)
        row = expand_row(smalls_ref[...], be.shape[0] * FF_BLOCK)
        for n in range(be.shape[0]):
            be[n] = row[:, n * FF_BLOCK : (n + 1) * FF_BLOCK]
        loads[1].wait()
        loads[2].wait()
        branch = nn(att_ref[...].T, wo_ref[...]) + flat[2:3]
        h = x_ref[...].astype(F32) + branch
        hidden[...] = h
        center = h - jnp.mean(h, axis=-1, keepdims=True)
        scale = lax.rsqrt(jnp.mean(center * center, axis=-1, keepdims=True) + epsilon)
        inv[...] = scale
        xhat[...] = center * scale
        low = (xhat[...] * flat[5:6] + flat[6:7]).astype(BF)
        n2[...] = low
        n2t[...] = low.T
        out_acc[...] = jnp.zeros_like(out_acc)
        dn2[...] = jnp.zeros_like(dn2)

    u = nn(n2[...], we_ref[...]) + be[i]
    square = u * u
    th = jnp.tanh(gelu_coeff * (u + 0.044715 * square * u))
    half = 0.5 * (1.0 + th)
    act = (u * half).astype(BF)
    slope = half + 0.5 * u * (1.0 - th * th) * (gelu_coeff * (1.0 + 3.0 * 0.044715 * square))
    out_acc[...] += nn(act, ws_ref[...])
    ge = nt(c_ref[...], ws_ref[...]) * slope
    ge = ge.astype(BF)
    dbe_ref[...] = jnp.sum(ge.astype(F32), axis=0, keepdims=True)
    dws_ref[...] = nn(act.T, c_ref[...]).astype(BF)
    dwe_ref[...] = nn(n2t[...], ge).astype(BF)
    dn2[...] += nt(ge, we_ref[...])

    @pl.when(i == last)
    def _():
        out_ref[...] = (hidden[...] + (out_acc[...] + flat[7:8])).astype(BF)
        up = c_ref[...].astype(F32)
        e = dn2[...]
        f = e * flat[5:6]
        xh = xhat[...]
        dv = f - jnp.mean(f, axis=-1, keepdims=True) - xh * jnp.mean(f * xh, axis=-1, keepdims=True)
        gh = up + dv * inv[...]
        gh_ref[...] = gh
        ga = gh.astype(BF)
        gm_ref[...] = nt(wo_ref[...], ga).astype(BF)
        saves = [pltpu.make_async_copy(gm_ref, gm_any, sems.at[3])]
        saves[0].start()
        dwo_ref[...] = nn(att_ref[...], ga).astype(BF)
        saves.append(pltpu.make_async_copy(dwo_ref, dwo_any, sems.at[4]))
        saves[1].start()
        vec_ref[0:1] = jnp.sum(ga.astype(F32), axis=0, keepdims=True)
        vec_ref[1:2] = jnp.sum(e * xh, axis=0, keepdims=True)
        vec_ref[2:3] = jnp.sum(e, axis=0, keepdims=True)
        vec_ref[3:4] = jnp.sum(up, axis=0, keepdims=True)
        vec_ref[4:8] = jnp.zeros((4, width), F32)
        for cp in saves:
            cp.wait()


def middle(x, c, att, smalls, wo, we, ws):
    rows, width = x.shape
    hidden = we.shape[1]
    S, V = jax.ShapeDtypeStruct, pltpu.VMEM
    n = hidden // FF_BLOCK
    across = pl.BlockSpec((width, FF_BLOCK), lambda i: (0, i))
    down = pl.BlockSpec((FF_BLOCK, width), lambda i: (i, 0))
    whole = lambda a: pl.BlockSpec(a.shape, lambda i: (0,) * len(a.shape), pipeline_mode=pl.Buffered(1))
    outs = (
        S((rows, width), BF),
        S((rows, width), F32),
        S((width, rows), BF),
        S((width, width), BF),
        S((width, hidden), BF),
        S((hidden, width), BF),
        S((SMALL_ROWS, width), F32),
        S((8, width), F32),
        S((1, hidden), F32),
    )
    return pl.pallas_call(
        middle_kernel,
        grid=(n,),
        out_shape=outs,
        in_specs=[whole(x), whole(c), HBMS, HBMS, HBMS, across, down],
        out_specs=(whole(outs[0]), whole(outs[1]), HBMS, HBMS)
        + (across, down, whole(outs[6]), whole(outs[7]), pl.BlockSpec((1, FF_BLOCK), lambda i: (0, i))),
        scratch_shapes=[
            V((n, 1, FF_BLOCK), F32),
            V((rows, width), F32),
            V((rows, width), F32),
            V((rows, 1), F32),
            V((rows, width), BF),
            V((width, rows), BF),
            V((rows, width), F32),
            V((rows, width), F32),
            V(att.shape, BF),
            V(smalls.shape, F32),
            V(wo.shape, BF),
            V((width, rows), BF),
            V((width, width), BF),
            DMA((5,)),
        ],
        name="middle",
        compiler_params=pltpu.CompilerParams(vmem_limit_bytes=62 << 20),
    )(x, c, att, smalls, wo, we, ws)


def attend_back_kernel(*refs):
    g_ref, heads_ref, of_ref, l_ref, tokens_ref, begins, flat_ref, packed_ref, wq_ref = refs[:9]
    ins, dx_ref, last_outs, outs = refs[9:12], refs[12], refs[13:15], refs[15:18]
    work, rest = take_sums(ins, refs[18:], True)
    dwq, small, gj, wq, normed_t, rzp = rest[0], rest[1], rest[2], rest[3], rest[4], rest[5:8]
    tail, rest = take_sums((dwq, small), rest[8:], False)
    rz, rest = rest[:2], rest[2:]
    (xv, gv, kn, vn, dkv, dq, lsum, delta, stage, stage_kv, got, stage_sh, ofv, dxv) = rest[:14]
    (s_full, r_full, s_sh, r_sh, s_fw, r_fw, s_q, r_q, s_kv, r_kv, s_shkv, s_part, r_part) = rest[14:27]
    szp, vzp, sz, vz, local = rest[27:]
    count = len(ins)
    t, m, z, x, y, c = place()
    sib = (t, m ^ 1)
    met = greet(chip_group(t, m) + [(t, m ^ 2)])
    def load_of(first):
        return pltpu.make_async_copy(of_ref.at[pl.ds(first, 4)], ofv, local.at[5])

    loads = [pltpu.make_async_copy(heads_ref.at[s, :, 2], stage_kv.at[:, s], local.at[s]) for s in range(2)]
    loads += [pltpu.make_async_copy(heads_ref.at[s, :, pl.ds(0, 2)], xv.at[s], local.at[2 + s]) for s in range(2)]
    load_of(8).start()
    for cp in loads:
        cp.start()
    met()
    own = x == c
    role = (x + c) % 2
    hf, hs, owner_m = 3 * z + 2 * x, 3 * z + 1, 2 * y + x
    order = (4, 5, 6, 7, 2, 3, 1)

    def full(k):
        d = t ^ k
        return g_ref.at[3 * (d // 2) + 2 * (d % 2)], gv.at[0, t], s_full.at[k], r_full.at[t], (d, m)

    def shared(k):
        zd = z ^ k
        return g_ref.at[3 * zd + 1], gv.at[1, t], s_sh.at[k], r_sh.at[t], (2 * zd + c, m)

    for k in (2, 3, 1):
        remote(*shared(k)).start()
    send_unless(own, *shared(0))
    loc = full(0)
    pltpu.make_async_copy(loc[0], loc[1], loc[3]).start()
    work.begin()
    for cp in loads:
        cp.wait()
    for s in range(2):
        for b in range(8):
            kn[s, b] = xv[s, b, 1].T
            vn[s, b] = stage_kv[b, s].T
    dkv[...] = jnp.zeros_like(dkv)
    dq[...] = jnp.zeros_like(dq)
    for k in (1, 2, 3):
        remote(*shared(k)).wait_send()
    sent_unless(own, *shared(0))
    for k in order:
        remote(*full(k)).start()

    def forward(k):
        b = t ^ k
        return remote(gv.at[1, b], gv.at[1, b], s_fw.at[k], r_fw.at[b], sib)

    @pl.when(own)
    def _():
        for k in (0, 1, 2, 3, 6, 7, 4, 5):
            landed(gv.at[1, t ^ k], r_sh.at[t ^ k])
            forward(k).start()

    work.early(4)

    @pl.when(jnp.logical_not(own))
    def _():
        for k in range(8):
            forward(k).wait_recv()

    def begin_of(slot, task):
        lane = lax.broadcasted_iota(jnp.int32, (1, 128), 1)
        return jnp.sum(jnp.where(lane == task, begins[slot], 0), axis=1, keepdims=True)

    def ready(slot, b, u):
        lsum[slot, b] = l_ref[u]
        delta[slot, b] = jnp.sum(gv[slot, b].astype(F32) * ofv[u % 4], axis=0, keepdims=True)

    def out_q(slot, b, u):
        stage[u] = (dq[u] * HD ** (-0.5)).astype(BF)
        if slot:
            send_unless((b == t) & own, stage.at[u], gj.at[0, hs], s_q.at[u], r_q.at[hs], (b, owner_m))
        else:
            send_unless(b == t, stage.at[u], gj.at[0, hf], s_q.at[u], r_q.at[hf], (b, m))

    args = (xv, gv, kn, vn, lsum, delta, dkv, dq)

    def shared_task(n, carry):
        task = jnp.where(n == 0, role, 3 - role)
        begin = begin_of(1, task)

        def step(j, carry):
            backward_units(1, task, 8 + 2 * n, 0, [(j, h, None, 0, BLK, 0, BLK) for h in range(2)], begin, *args)
            return carry

        lax.fori_loop(0, 2 * task, step, 0)
        backward_units(1, task, 8 + 2 * n, 0, diag_units(task), begin, *args)
        for h in range(2):
            out_q(1, 2 * task + h, 8 + 2 * n + h)
        return carry

    load_of(8).wait()
    for n in range(2):
        task = role if n == 0 else 3 - role
        for h in range(2):
            ready(1, 2 * task + h, 8 + 2 * n + h)
    load_of(0).start()
    lax.fori_loop(0, 2, shared_task, 0)

    def part(k):
        b = t ^ k
        return remote(dkv.at[b], got.at[b], s_part.at[k], r_part.at[b], sib)

    def shared_kv(k):
        b = t ^ k
        return stage_sh.at[b], gj.at[pl.ds(1, 2), hs], s_shkv.at[k], r_kv.at[hs], (b, m)

    @pl.when(jnp.logical_not(own))
    def _():
        for k in order + (0,):
            part(k).start()

    for b in range(8):
        landed(gv.at[0, b], r_full.at[b])
    load_of(0).wait()
    for b in range(4):
        ready(0, b, b)
    load_of(4).start()
    load_of(4).wait()
    for b in range(4, 8):
        ready(0, b, b)

    @pl.when(own)
    def _():
        for k in order + (0,):
            b = t ^ k
            part(k).wait_recv()
            stage_sh[b, 0] = ((dkv[b, 0] + got[b, 0]) * HD ** (-0.5)).astype(BF)
            stage_sh[b, 1] = (dkv[b, 1] + got[b, 1]).astype(BF)
            a = shared_kv(k)
            if k:
                remote(*a).start()
            else:
                pltpu.make_async_copy(a[0], a[1], a[3]).start()

    def full_keys(s, carry):
        keys = z ^ (3 - s)
        dkv[8:10] = jnp.zeros((2,) + dkv.shape[1:], F32)
        backward_units(0, keys, 2 * keys, 8 - 2 * keys, diag_units(keys), begin_of(0, keys), *args)

        def step(n, carry):
            task, j = n // 2, 2 * keys + n % 2
            units = [(j, h, None, 0, BLK, 0, BLK) for h in range(2)]
            backward_units(0, task, 2 * task, 8 - 2 * keys, units, 0, *args)
            return carry

        lax.fori_loop(2 * keys + 2, 8, step, 0)
        for i in range(2):
            b = 2 * keys + i
            stage_kv[b, 0] = (dkv[8 + i, 0] * HD ** (-0.5)).astype(BF)
            stage_kv[b, 1] = dkv[8 + i, 1].astype(BF)
            send_unless(b == t, stage_kv.at[b], gj.at[pl.ds(1, 2), hf], s_kv.at[b], r_kv.at[hf], (b, m))

        @pl.when(s == 1)
        def _():
            work.late(4)

        return carry

    lax.fori_loop(0, 4, full_keys, 0)
    for b in range(8):
        out_q(0, b, b)
    along = []

    def z_push(sums, k, a, buf, ssem, vsem):
        sums.column(k, a)
        cp = remote(sums.acc[a].at[4 * k], buf[a].at[k - 1], ssem.at[k, a], vsem.at[k, a], (t ^ (2 * k), m))
        cp.start()
        along.append(cp)


    width = tokens_ref.shape[1]
    step = width // 32
    gain, shift = flat_ref[3:4], flat_ref[4:5]

    def norm(half):
        values = tokens_ref[half].astype(F32)
        center = values - jnp.mean(values, axis=-1, keepdims=True)
        inv = lax.rsqrt(jnp.mean(center * center, axis=-1, keepdims=True) + epsilon)
        return center * inv, inv

    load = pltpu.make_async_copy(wq_ref, wq, local.at[4])
    load.start()
    halves = [slice(n * 256, (n + 1) * 256) for n in range(tokens_ref.shape[0] // 256)]
    for half in halves:
        normed_t[:, half] = (norm(half)[0] * gain + shift).astype(BF).T

    for h in range(12):
        landed(gj.at[0, h], r_q.at[h])
        landed(gj.at[pl.ds(1, 2), h], r_kv.at[h])
    load.wait()
    for k in (3, 2, 1):
        for a in range(count):
            z_push(work, k, a, rzp, szp, vzp)
    for n in range(9):
        grads = gj[n // 3, 4 * (n % 3) : 4 * (n % 3) + 4].reshape(256, BLK)
        block = nt(normed_t[...], grads)
        dwq[:, :, n * 256 : (n + 1) * 256] = block.reshape(32, step, 256).astype(BF)
    tail.begin([0])
    dgain, dshift = jnp.zeros((1, width), F32), jnp.zeros((1, width), F32)
    for half in halves:
        e = jnp.zeros((width, 256), F32)
        for n in range(9):
            grads = gj[n // 3, 4 * (n % 3) : 4 * (n % 3) + 4, :, half].reshape(256, 256)
            e = e + nn(wq[:, n * 256 : (n + 1) * 256], grads)
        e = e.T
        xhat, inv = norm(half)
        f = e * gain
        dv = f - jnp.mean(f, axis=-1, keepdims=True) - xhat * jnp.mean(f * xhat, axis=-1, keepdims=True)
        if half.start:
            out_x.wait()
        dxv[...] = dv * inv
        out_x = pltpu.make_async_copy(dxv, dx_ref.at[half], local.at[6])
        out_x.start()
        dgain = dgain + jnp.sum(e * xhat, axis=0, keepdims=True)
        dshift = dshift + jnp.sum(e, axis=0, keepdims=True)
    ones = jnp.ones((8, BLK), BF)
    db_query = nt(ones, gj[0].reshape(width, BLK))[0:1]
    db_value = nt(ones, gj[2].reshape(width, BLK))[0:1]
    mine = jnp.concatenate([db_query, db_value, dgain, dshift], axis=0)
    mine = shard_rows(mine, step)
    small[...] = packed_ref[...]
    small[:, 0:2] = mine[:, 0:2]
    small[:, 3:5] = mine[:, 2:4]
    tail.begin([1])
    tail.early(2)
    tail.late(2)
    for k in (3, 2, 1):
        for a in range(2):
            z_push(tail, k, a, rz, sz, vz)

    def gather_z(a, out, buf, vsem):
        for k in (1, 2, 3):
            landed(buf.at[k - 1], vsem.at[k, a])

        def add_part(part):
            total = out[part]
            for k in (1, 2, 3):
                total = total + buf[(k - 1,) + part].astype(F32)
            out[part] = total

        in_parts(out.shape, add_part)

    for a in range(count):
        work.column_out(a, outs[a])
        gather_z(a, outs[a], rzp[a], vzp)
    for a in range(2):
        tail.column_out(a, last_outs[a])
        gather_z(a, last_outs[a], rz[a], vz)
    out_x.wait()
    tail.finish()
    for cp in along:
        cp.wait_send()
    work.finish()
    for k in range(1, 8):
        remote(*full(k)).wait_send()
    for b in range(8):
        sent_unless(b == t, stage.at[b], gj.at[0, hf], s_q.at[b], r_q.at[hf], (b, m))
        sent_unless(b == t, stage_kv.at[b], gj.at[pl.ds(1, 2), hf], s_kv.at[b], r_kv.at[hf], (b, m))
    for n in range(2):
        task = role if n == 0 else 3 - role
        for h in range(2):
            b, u = 2 * task + h, 8 + 2 * n + h
            sent_unless((b == t) & own, stage.at[u], gj.at[0, hs], s_q.at[u], r_q.at[hs], (b, owner_m))

    @pl.when(own)
    def _():
        for k in range(8):
            forward(k).wait_send()
        for k in range(1, 8):
            remote(*shared_kv(k)).wait_send()

    @pl.when(jnp.logical_not(own))
    def _():
        for k in range(8):
            part(k).wait_send()


def attend_back(grad_mix, heads, out_full, log_sum, tokens, begins, flat, packed, full_qkv, grads, cid):
    n = len(grads)
    rows, width = tokens.shape
    head = (HD, BLK)
    S, V = jax.ShapeDtypeStruct, pltpu.VMEM
    shards = [(g.shape[1:], BF) for g in grads]
    last = [((width // 32, 3 * width), BF), ((SMALL_ROWS, 128), F32)]
    return pl.pallas_call(
        attend_back_kernel,
        out_shape=(S((rows, width), F32),) + tuple(S(s, F32) for s, d in last + shards),
        in_specs=[ANYS] * 3 + [VMEMS] * 5 + [ANYS] + [ANYS] * n,
        out_specs=(ANYS,) + (VMEMS,) * (2 + n),
        scratch_shapes=sums_scratch(shards, True)
        + [V((32,) + s, d) for s, d in last]
        + [V((3, 12) + head, BF), V((width, 3 * width), BF), V((width, rows), BF)]
        + [V((3,) + s, d) for s, d in shards]
        + sums_scratch(last, False)
        + [V((3,) + s, d) for s, d in last]
        + [
            V((2, 8, 2) + head, BF),
            V((2, 8) + head, BF),
            V((2, 8, BLK, HD), BF),
            V((2, 8, BLK, HD), BF),
            V((10, 2) + head, F32),
            V((12,) + head, F32),
            V((2, 8, 1, BLK), F32),
            V((2, 8, 1, BLK), F32),
            V((12,) + head, BF),
            V((8, 2) + head, BF),
            V((8, 2) + head, F32),
            V((8, 2) + head, BF),
            V((4,) + head, F32),
            V((256, width), F32),
        ]
        + [DMA((8,)), DMA((8,)), DMA((4,)), DMA((8,)), DMA((8,)), DMA((8,)), DMA((12,)), DMA((12,))]
        + [DMA((8,)), DMA((12,)), DMA((8,)), DMA((8,)), DMA((8,))]
        + [DMA((4, n)), DMA((4, n)), DMA((4, 2)), DMA((4, 2)), DMA((7,))],
        name="attend_back",
        compiler_params=pltpu.CompilerParams(collective_id=cid, has_side_effects=True, vmem_limit_bytes=62 << 20),
    )(grad_mix, heads, out_full, log_sum, tokens, begins, flat, packed, full_qkv, *grads)


def by_heads(
    tokens,
    cotangent,
    starts,
    w_qkv,
    b_query,
    b_value,
    w_out,
    b_out,
    gain_one,
    shift_one,
    gain_two,
    shift_two,
    w_expand,
    b_expand,
    w_shrink,
    b_shrink,
):
    rows, width = tokens.shape[1:]
    hidden = b_expand.shape[0] * 32
    vectors = [b_query, b_value, b_out, gain_one, shift_one, gain_two, shift_two, b_shrink, b_expand]
    full_qkv, smalls, rest, (heads, out_full, log_sum, attention, begins) = attend(
        tokens[0], starts, [w_qkv, w_out, w_expand, w_shrink], [v.reshape(1, -1) for v in vectors], 1
    )
    full_out, full_expand, full_shrink = (w.reshape(-1, w.shape[-1]) for w in rest)
    attention = attention.reshape(width, rows)
    step = width // 32
    layer_out, grad_hidden, grad_mix, dw_out, dw_expand, dw_shrink, flat, sums, db_expand = middle(
        tokens[0], cotangent[0], attention, smalls, full_out, full_expand, full_shrink
    )
    pieces = sums.reshape(8, 32, step).transpose(1, 0, 2)
    gap = jnp.zeros((32, 2, step), F32)
    packed = [gap, pieces[:, 0:1], gap, pieces[:, 1:4], db_expand.reshape(32, 4, step), gap, gap]
    packed = jnp.pad(jnp.concatenate(packed, axis=1), [(0, 0), (0, 0), (0, 128 - step)])
    shards = lambda w: w.reshape((32, -1) + w.shape[1:])
    dtokens, dw_qkv, smalls, dw_out, dw_expand, dw_shrink = attend_back(
        grad_mix.reshape(12, HD, rows),
        heads,
        out_full,
        log_sum,
        tokens[0],
        begins,
        flat,
        packed,
        full_qkv,
        [shards(dw_out), shards(dw_expand), shards(dw_shrink)],
        2,
    )
    step = width // 32
    vecs = [smalls[i, :step] for i in range(8)]
    db_query, db_value, db_out, dgain_one, dshift_one, dgain_two, dshift_two, db_shrink = vecs
    db_expand = smalls[8:12, :step].reshape(-1)
    return (
        layer_out.reshape(1, rows, width),
        (grad_hidden + dtokens).reshape(1, rows, width),
        dw_qkv,
        db_query,
        db_value,
        dw_out,
        db_out,
        dgain_one,
        dshift_one,
        dgain_two,
        dshift_two,
        dw_expand,
        db_expand,
        dw_shrink,
        db_shrink,
    )


def solution(mesh):
    rows, vector, seq = P(("tok", "mdl"), None), P(("tok", "mdl")), P("mdl", "tok", None)
    by_name = dict(m=rows, v=vector, s=seq)
    fits = mesh.shape["tok"] == 8 and mesh.shape["mdl"] == 4
    return jax.shard_map(
        by_heads if fits else general,
        mesh=mesh,
        in_specs=(seq, seq, P("mdl", None)) + tuple(by_name[k] for k in "mvvmvvvvvmvmv"),
        out_specs=tuple(by_name[k] for k in "ssmvvmvvvvvmvmv"),
        check_vma=False,
    )
```

```python
import functools
import math

import jax
import jax.numpy as jnp
from jax import lax
from jax.experimental import pallas as pl
from jax.experimental.pallas import tpu as pltpu
from jax.sharding import PartitionSpec as P

HD = 64
PIECE = 256
KEYB = 512


epsilon = 1e-05
masked_score = -1e30
gelu_coeff = 0.7978845608028654


def layer_norm(values, gain_vec, shift_vec):
    center = values - jnp.mean(values, axis=-1, keepdims=True)
    spread = jnp.mean(center * center, axis=-1, keepdims=True)
    return center * lax.rsqrt(spread + epsilon) * gain_vec + shift_vec


def gelu_tanh(inputs):
    return (
        0.5 * inputs * (1.0 + jnp.tanh(gelu_coeff * (inputs + 0.044715 * inputs * inputs * inputs)))
    )


def piece_ids(begins, positions):
    inside = (positions[:, None] >= begins[None, :]) & (
        positions[:, None] < begins[None, :] + PIECE
    )
    labels = jnp.arange(1, begins.shape[0] + 1, dtype=jnp.int32)
    return jnp.sum(jnp.where(inside, labels[None, :], 0), axis=1) - 1


def block_scores(query_heads, key_heads, query_pos, query_lab, begins, block_index, scaling):
    key_block = lax.dynamic_slice_in_dim(key_heads, block_index * KEYB, KEYB, 0)
    key_pos = block_index * KEYB + jnp.arange(KEYB, dtype=jnp.int32)
    key_lab = piece_ids(begins, key_pos)
    scores = (
        jnp.einsum("qhd,khd->hqk", query_heads, key_block, preferred_element_type=jnp.float32)
        * scaling
    )
    allowed = (key_pos[None, :] <= query_pos[:, None]) | (
        key_lab[None, :] == query_lab[:, None]
    ) & (query_lab[:, None] >= 0)
    return jnp.where(allowed[None, :, :], scores, masked_score)


def attend_forward(
    query_heads, key_heads, value_heads, query_pos, query_lab, begins, needed, scaling
):
    local_rows = query_heads.shape[0]
    head_count = query_heads.shape[1]

    def stats_step(block_index, loop_state):
        highest, summed = loop_state
        masked = block_scores(
            query_heads, key_heads, query_pos, query_lab, begins, block_index, scaling
        )
        new_high = jnp.maximum(highest, jnp.max(masked, axis=-1))
        summed = summed * jnp.exp(highest - new_high) + jnp.sum(
            jnp.exp(masked - new_high[:, :, None]), axis=-1
        )
        return (new_high, summed)

    starting = (
        jnp.full((head_count, local_rows), masked_score, jnp.float32),
        jnp.zeros((head_count, local_rows), jnp.float32),
    )
    highest, summed = lax.fori_loop(0, needed, stats_step, starting)

    def mix_step(block_index, running):
        masked = block_scores(
            query_heads, key_heads, query_pos, query_lab, begins, block_index, scaling
        )
        prob_low = (jnp.exp(masked - highest[:, :, None]) / summed[:, :, None]).astype(jnp.bfloat16)
        value_block = lax.dynamic_slice_in_dim(value_heads, block_index * KEYB, KEYB, 0)
        return running + jnp.einsum(
            "hqk,khd->qhd", prob_low, value_block, preferred_element_type=jnp.float32
        )

    mixture = lax.fori_loop(0, needed, mix_step, jnp.zeros(query_heads.shape, jnp.float32))
    return (mixture, highest, summed)


def attend_backward(
    query_heads,
    key_heads,
    value_heads,
    grad_heads,
    mixture,
    query_pos,
    query_lab,
    begins,
    needed,
    highest,
    summed,
    scaling,
):
    row_delta = jnp.einsum("qhd,qhd->hq", grad_heads.astype(jnp.float32), mixture)

    def grad_step(block_index, loop_state):
        grad_query, grad_keys, grad_values = loop_state
        masked = block_scores(
            query_heads, key_heads, query_pos, query_lab, begins, block_index, scaling
        )
        prob_full = jnp.exp(masked - highest[:, :, None]) / summed[:, :, None]
        offset = block_index * KEYB
        value_block = lax.dynamic_slice_in_dim(value_heads, offset, KEYB, 0)
        grad_probs = jnp.einsum(
            "qhd,khd->hqk", grad_heads, value_block, preferred_element_type=jnp.float32
        )
        grad_scores = (prob_full * (grad_probs - row_delta[:, :, None])).astype(jnp.bfloat16)
        key_block = lax.dynamic_slice_in_dim(key_heads, offset, KEYB, 0)
        grad_query = (
            grad_query
            + jnp.einsum("hqk,khd->qhd", grad_scores, key_block, preferred_element_type=jnp.float32)
            * scaling
        )
        key_part = (
            jnp.einsum("hqk,qhd->khd", grad_scores, query_heads, preferred_element_type=jnp.float32)
            * scaling
        )
        value_part = jnp.einsum(
            "hqk,qhd->khd",
            prob_full.astype(jnp.bfloat16),
            grad_heads,
            preferred_element_type=jnp.float32,
        )
        grad_keys = lax.dynamic_update_slice_in_dim(
            grad_keys, lax.dynamic_slice_in_dim(grad_keys, offset, KEYB, 0) + key_part, offset, 0
        )
        grad_values = lax.dynamic_update_slice_in_dim(
            grad_values,
            lax.dynamic_slice_in_dim(grad_values, offset, KEYB, 0) + value_part,
            offset,
            0,
        )
        return (grad_query, grad_keys, grad_values)

    starting = (
        jnp.zeros(query_heads.shape, jnp.float32),
        jnp.zeros(key_heads.shape, jnp.float32),
        jnp.zeros(value_heads.shape, jnp.float32),
    )
    return lax.fori_loop(0, needed, grad_step, starting)


def general(
    tokens,
    cotangent,
    starts,
    w_qkv,
    b_query,
    b_value,
    w_out,
    b_out,
    gain_one,
    shift_one,
    gain_two,
    shift_two,
    w_expand,
    b_expand,
    w_shrink,
    b_shrink,
):
    (
        full_qkv,
        full_bq,
        full_bv,
        full_out,
        full_bo,
        full_gone,
        full_sone,
        full_gtwo,
        full_stwo,
        full_expand,
        full_bexp,
        full_shrink,
        full_bshr,
    ) = (
        lax.all_gather(w_qkv.astype(jnp.bfloat16), ("tok", "mdl"), axis=0, tiled=True),
        lax.all_gather(b_query.astype(jnp.bfloat16), ("tok", "mdl"), axis=0, tiled=True),
        lax.all_gather(b_value.astype(jnp.bfloat16), ("tok", "mdl"), axis=0, tiled=True),
        lax.all_gather(w_out.astype(jnp.bfloat16), ("tok", "mdl"), axis=0, tiled=True),
        lax.all_gather(b_out.astype(jnp.bfloat16), ("tok", "mdl"), axis=0, tiled=True),
        lax.all_gather(gain_one.astype(jnp.bfloat16), ("tok", "mdl"), axis=0, tiled=True),
        lax.all_gather(shift_one.astype(jnp.bfloat16), ("tok", "mdl"), axis=0, tiled=True),
        lax.all_gather(gain_two.astype(jnp.bfloat16), ("tok", "mdl"), axis=0, tiled=True),
        lax.all_gather(shift_two.astype(jnp.bfloat16), ("tok", "mdl"), axis=0, tiled=True),
        lax.all_gather(w_expand.astype(jnp.bfloat16), ("tok", "mdl"), axis=0, tiled=True),
        lax.all_gather(b_expand.astype(jnp.bfloat16), ("tok", "mdl"), axis=0, tiled=True),
        lax.all_gather(w_shrink.astype(jnp.bfloat16), ("tok", "mdl"), axis=0, tiled=True),
        lax.all_gather(b_shrink.astype(jnp.bfloat16), ("tok", "mdl"), axis=0, tiled=True),
    )
    query_bias = full_bq.astype(jnp.float32)
    value_bias = full_bv.astype(jnp.float32)
    out_bias = full_bo.astype(jnp.float32)
    gain_first = full_gone.astype(jnp.float32)
    shift_first = full_sone.astype(jnp.float32)
    gain_second = full_gtwo.astype(jnp.float32)
    shift_second = full_stwo.astype(jnp.float32)
    expand_bias = full_bexp.astype(jnp.float32)
    shrink_bias = full_bshr.astype(jnp.float32)
    local_rows = tokens.shape[1]
    model_width = tokens.shape[2]
    head_count = model_width // HD
    group_size = lax.axis_size("tok")
    member = lax.axis_index("tok")
    seq_len = local_rows * group_size
    scaling = HD ** (-0.5)
    needed = jnp.minimum(
        seq_len // KEYB, ((member + 1) * local_rows + PIECE - 1 + KEYB - 1) // KEYB
    )
    begins = starts[0]
    query_pos = member * local_rows + jnp.arange(local_rows, dtype=jnp.int32)
    query_lab = piece_ids(begins, query_pos)
    token_rows = tokens[0]
    cotangent_rows = cotangent[0]
    inputs = token_rows.astype(jnp.float32)
    normed = layer_norm(inputs, gain_first, shift_first).astype(jnp.bfloat16)
    joined = jnp.dot(normed, full_qkv, preferred_element_type=jnp.float32)
    queries = (joined[:, :model_width] + query_bias).astype(jnp.bfloat16)
    keys_own = joined[:, model_width : 2 * model_width].astype(jnp.bfloat16)
    values_own = (joined[:, 2 * model_width :] + value_bias).astype(jnp.bfloat16)
    key_full, value_full = (
        lax.all_gather(keys_own, "tok", axis=0, tiled=True),
        lax.all_gather(values_own, "tok", axis=0, tiled=True),
    )
    query_heads = queries.reshape(local_rows, head_count, HD)
    mixture, highest, summed = attend_forward(
        query_heads,
        key_full.reshape(seq_len, head_count, HD),
        value_full.reshape(seq_len, head_count, HD),
        query_pos,
        query_lab,
        begins,
        needed,
        scaling,
    )
    attention = mixture.reshape(local_rows, model_width).astype(jnp.bfloat16)
    hidden_one = inputs + (
        jnp.dot(attention, full_out, preferred_element_type=jnp.float32) + out_bias
    )
    normed_two = layer_norm(hidden_one, gain_second, shift_second).astype(jnp.bfloat16)
    expanded = jnp.dot(normed_two, full_expand, preferred_element_type=jnp.float32) + expand_bias
    activated = gelu_tanh(expanded).astype(jnp.bfloat16)
    layer_out = hidden_one + (
        jnp.dot(activated, full_shrink, preferred_element_type=jnp.float32) + shrink_bias
    )
    upstream = cotangent_rows.astype(jnp.float32)
    db_shrink = jnp.sum(upstream, axis=0)
    dw_shrink = jnp.einsum(
        "rf,rd->fd", activated, cotangent_rows, preferred_element_type=jnp.float32
    )
    grad_act = jnp.einsum(
        "rd,fd->rf", cotangent_rows, full_shrink, preferred_element_type=jnp.float32
    )
    gelu_pull = jax.vjp(gelu_tanh, expanded)[1]
    grad_expand = gelu_pull(grad_act)[0].astype(jnp.bfloat16)
    db_expand = jnp.sum(grad_expand.astype(jnp.float32), axis=0)
    dw_expand = jnp.einsum("rd,rf->df", normed_two, grad_expand, preferred_element_type=jnp.float32)
    grad_normed_two = jnp.einsum(
        "rf,df->rd", grad_expand, full_expand, preferred_element_type=jnp.float32
    )
    norm_pull = jax.vjp(layer_norm, hidden_one, gain_second, shift_second)[1]
    grad_hidden_part, dgain_two, dshift_two = norm_pull(grad_normed_two)
    grad_hidden = upstream + grad_hidden_part
    grad_attn = grad_hidden.astype(jnp.bfloat16)
    db_out = jnp.sum(grad_attn.astype(jnp.float32), axis=0)
    dw_out = jnp.einsum("rd,re->de", attention, grad_attn, preferred_element_type=jnp.float32)
    grad_mix = jnp.einsum(
        "re,de->rd", grad_attn, full_out, preferred_element_type=jnp.float32
    ).astype(jnp.bfloat16)
    key_back, value_back = (key_full, value_full)
    grad_query, grad_keys, grad_values = attend_backward(
        query_heads,
        key_back.reshape(seq_len, head_count, HD),
        value_back.reshape(seq_len, head_count, HD),
        grad_mix.reshape(local_rows, head_count, HD),
        mixture,
        query_pos,
        query_lab,
        begins,
        needed,
        highest,
        summed,
        scaling,
    )
    key_share, value_share = (
        lax.psum_scatter(
            grad_keys.reshape(seq_len, model_width).astype(jnp.bfloat16),
            "tok",
            scatter_dimension=0,
            tiled=True,
        ).astype(jnp.float32),
        lax.psum_scatter(
            grad_values.reshape(seq_len, model_width).astype(jnp.bfloat16),
            "tok",
            scatter_dimension=0,
            tiled=True,
        ).astype(jnp.float32),
    )
    grad_joined = jnp.concatenate(
        [
            grad_query.reshape(local_rows, model_width).astype(jnp.bfloat16),
            key_share.astype(jnp.bfloat16),
            value_share.astype(jnp.bfloat16),
        ],
        axis=1,
    )
    db_query = jnp.sum(grad_joined[:, :model_width].astype(jnp.float32), axis=0)
    db_value = jnp.sum(grad_joined[:, 2 * model_width :].astype(jnp.float32), axis=0)
    dw_qkv = jnp.einsum("rd,re->de", normed, grad_joined, preferred_element_type=jnp.float32)
    grad_normed = jnp.einsum("re,de->rd", grad_joined, full_qkv, preferred_element_type=jnp.float32)
    norm_pull_first = jax.vjp(layer_norm, inputs, gain_first, shift_first)[1]
    grad_input_part, dgain_one, dshift_one = norm_pull_first(grad_normed)
    dtokens = grad_hidden + grad_input_part
    (
        dw_qkv,
        db_query,
        db_value,
        dw_out,
        db_out,
        dgain_one,
        dshift_one,
        dgain_two,
        dshift_two,
        dw_expand,
        db_expand,
        dw_shrink,
        db_shrink,
    ) = (
        lax.psum_scatter(dw_qkv, ("tok", "mdl"), scatter_dimension=0, tiled=True),
        lax.psum_scatter(db_query, ("tok", "mdl"), scatter_dimension=0, tiled=True),
        lax.psum_scatter(db_value, ("tok", "mdl"), scatter_dimension=0, tiled=True),
        lax.psum_scatter(dw_out, ("tok", "mdl"), scatter_dimension=0, tiled=True),
        lax.psum_scatter(db_out, ("tok", "mdl"), scatter_dimension=0, tiled=True),
        lax.psum_scatter(dgain_one, ("tok", "mdl"), scatter_dimension=0, tiled=True),
        lax.psum_scatter(dshift_one, ("tok", "mdl"), scatter_dimension=0, tiled=True),
        lax.psum_scatter(dgain_two, ("tok", "mdl"), scatter_dimension=0, tiled=True),
        lax.psum_scatter(dshift_two, ("tok", "mdl"), scatter_dimension=0, tiled=True),
        lax.psum_scatter(dw_expand, ("tok", "mdl"), scatter_dimension=0, tiled=True),
        lax.psum_scatter(db_expand, ("tok", "mdl"), scatter_dimension=0, tiled=True),
        lax.psum_scatter(dw_shrink, ("tok", "mdl"), scatter_dimension=0, tiled=True),
        lax.psum_scatter(db_shrink, ("tok", "mdl"), scatter_dimension=0, tiled=True),
    )
    return (
        layer_out.astype(jnp.bfloat16).reshape(1, local_rows, model_width),
        dtokens.reshape(1, local_rows, model_width),
        dw_qkv,
        db_query,
        db_value,
        dw_out,
        db_out,
        dgain_one,
        dshift_one,
        dgain_two,
        dshift_two,
        dw_expand,
        db_expand,
        dw_shrink,
        db_shrink,
    )


BLK = 512
LOG_SCALE = math.log2(math.e) * HD ** (-0.5)
F32 = jnp.float32
BF = jnp.bfloat16


def nn(a, b):
    return lax.dot_general(a, b, (((1,), (0,)), ((), ())), preferred_element_type=F32)


def nt(a, b):
    return lax.dot_general(a, b, (((1,), (1,)), ((), ())), preferred_element_type=F32)


def diag_units(task):
    return [
        (2 * task, 0, "diag", 0, BLK, 0, BLK),
        (2 * task, 1, None, 0, BLK, 0, BLK),
        (2 * task + 1, 1, "diag", 0, BLK, 0, BLK),
        (2 * task + 1, 0, "piece", 0, PIECE, BLK - PIECE, PIECE),
    ]


def unit_mask(unit, task, begin):
    j, h, kind, k0, nk, q0, nq = unit
    keys = j * BLK + k0
    queries = (2 * task + h) * BLK + q0
    kc = keys + lax.broadcasted_iota(jnp.int32, (nk, 1), 0)
    qr = queries + lax.broadcasted_iota(jnp.int32, (1, nq), 1)
    kin = ((kc >= begin) & (kc < begin + PIECE)).astype(F32)
    qin = ((qr >= begin) & (qr < begin + PIECE)).astype(F32)
    both = (kin * qin) > 0.5
    if kind == "piece":
        return both
    return (kc <= qr) | both


def forward_units(slot, task, units, begin, xv, kn, acc, ms, ls):
    def score(unit):
        j, h, kind, k0, nk, q0, nq = unit
        s = nn(kn[slot, j, k0 : k0 + nk, :], xv[slot, 2 * task + h, 0, :, q0 : q0 + nq]) * LOG_SCALE
        if kind:
            s = jnp.where(unit_mask(unit, task, begin), s, masked_score)
        return s

    ahead = score(units[0])
    for n, unit in enumerate(units):
        j, h, kind, k0, nk, q0, nq = unit
        now = ahead
        if n + 1 < len(units):
            ahead = score(units[n + 1])
        qs = slice(q0, q0 + nq)
        high = jnp.maximum(ms[h, :, qs], jnp.max(now, axis=0, keepdims=True))
        fade = jnp.exp2(ms[h, :, qs] - high)
        p = jnp.exp2(now - high)
        ls[h, :, qs] = ls[h, :, qs] * fade + jnp.sum(p, axis=0, keepdims=True)
        ms[h, :, qs] = high
        acc[h, :, qs] = acc[h, :, qs] * fade + nn(xv[slot, j, 2, :, k0 : k0 + nk], p.astype(BF))


def forward_task(slot, task, begin, xv, kn, acc, ms, ls):
    ms[...] = jnp.full_like(ms, masked_score)
    ls[...] = jnp.zeros_like(ls)
    acc[...] = jnp.zeros_like(acc)

    def step(j, carry):
        forward_units(
            slot, task, [(j, h, None, 0, BLK, 0, BLK) for h in range(2)], begin, xv, kn, acc, ms, ls
        )
        return carry

    lax.fori_loop(0, 2 * task, step, 0)
    forward_units(slot, task, diag_units(task), begin, xv, kn, acc, ms, ls)


def backward_units(slot, task, row, key, units, begin, xv, gv, kn, vn, lsum, delta, dkv, dq):
    def score(unit):
        j, h, kind, k0, nk, q0, nq = unit
        b = 2 * task + h
        s = nn(kn[slot, j, k0 : k0 + nk, :], xv[slot, b, 0, :, q0 : q0 + nq]) * LOG_SCALE
        return s, nn(vn[slot, j, k0 : k0 + nk, :], gv[slot, b, :, q0 : q0 + nq])

    ahead = score(units[0])
    for n, unit in enumerate(units):
        j, h, kind, k0, nk, q0, nq = unit
        b = 2 * task + h
        s, dp = ahead
        if n + 1 < len(units):
            ahead = score(units[n + 1])
        p = jnp.exp2(s - lsum[slot, b, :, q0 : q0 + nq])
        if kind:
            p = jnp.where(unit_mask(unit, task, begin), p, 0.0)
        ds = (p * (dp - delta[slot, b, :, q0 : q0 + nq])).astype(BF)
        dkv[key + j, 1, :, k0 : k0 + nk] += nt(gv[slot, b, :, q0 : q0 + nq], p.astype(BF))
        dkv[key + j, 0, :, k0 : k0 + nk] += nt(xv[slot, b, 0, :, q0 : q0 + nq], ds)
        dq[row + h, :, q0 : q0 + nq] += nn(xv[slot, j, 1, :, k0 : k0 + nk], ds)


MESH_ID = pl.DeviceIdType.MESH
ANYS = pl.BlockSpec(memory_space=pl.ANY)
VMEMS = pl.BlockSpec(memory_space=pltpu.VMEM)
SMEMS = pl.BlockSpec(memory_space=pltpu.SMEM)
DMA = pltpu.SemaphoreType.DMA


def place():
    t = lax.axis_index("tok")
    m = lax.axis_index("mdl")
    return t, m, t // 2, t % 2, m // 2, m % 2


def greet(peers):
    barrier = pltpu.get_barrier_semaphore()
    for peer in peers:
        pl.semaphore_signal(barrier, inc=1, device_id=peer, device_id_type=MESH_ID)
    return lambda: pl.semaphore_wait(barrier, len(peers))


def meet(peers):
    greet(peers)()


def chip_group(t, m):
    return [(t ^ k, m ^ b) for k in range(8) for b in range(2) if (k, b) != (0, 0)]


def column_group(t, m):
    return [(t ^ 2, m), (t ^ 4, m), (t ^ 6, m), (t ^ 1, m), (t, m ^ 2), (t, m ^ 1)]


def remote(src, dst, ssem, rsem, dev):
    return pltpu.make_async_remote_copy(
        src_ref=src, dst_ref=dst, send_sem=ssem, recv_sem=rsem, device_id=dev, device_id_type=MESH_ID
    )


def landed(ref, sem):
    pltpu.make_async_copy(ref, ref, sem).wait()


def send_unless(here, src, dst, ssem, rsem, dev):
    @pl.when(here)
    def _():
        pltpu.make_async_copy(src, dst, rsem).start()

    @pl.when(jnp.logical_not(here))
    def _():
        remote(src, dst, ssem, rsem, dev).start()


def sent_unless(here, src, dst, ssem, rsem, dev):
    @pl.when(jnp.logical_not(here))
    def _():
        remote(src, dst, ssem, rsem, dev).wait_send()


class Pushes:
    def __init__(self, outs, send, recv):
        self.outs, self.send, self.recv, self.started = outs, send, recv, []

    def push(self, shard, dev, src=None):
        e = len(self.started)
        todo = []
        for a, out in enumerate(self.outs):
            cp = remote(
                out.at[shard] if src is None else src[a],
                out.at[shard],
                self.send.at[e, a],
                self.recv.at[a, shard],
                dev,
            )
            cp.start()
            todo.append(cp)
        self.started.append(todo)

    def arrived(self, shard):
        for a, out in enumerate(self.outs):
            landed(out.at[shard], self.recv.at[a, shard])

    def finish(self):
        for todo in self.started:
            for cp in todo:
                cp.wait_send()


class Line:
    def __init__(self, outs, send, recv, fan, beside):
        self.outs, self.send, self.recv, self.fan, self.beside = outs, send, recv, fan, beside
        self.t, self.m = lax.axis_index("tok"), lax.axis_index("mdl")
        self.z = self.t // 2
        self.chips = lax.axis_size("tok") // 2

    def ways(self, hop):
        up = (0, (self.z >= hop) & (self.z < self.chips - 1), self.t - 2 * hop, self.t + 2)
        down = (1, (self.z + hop < self.chips) & (self.z > 0), self.t + 2 * hop, self.t - 2)
        return up, down

    def copies(self, hop, way, shard, to, src=None):
        at = 4 * shard + self.m
        return [
            remote(
                out.at[at] if src is None else src[a],
                out.at[at],
                self.send.at[2 * hop + way, a],
                self.recv.at[a, at],
                (to, self.m),
            )
            for a, out in enumerate(self.outs)
        ]

    def comes(self, hop, way):
        return (self.z >= hop) if way == 0 else (self.z + hop < self.chips)

    def aside(self, hop, way, shard):
        at = 4 * shard + self.m
        return [
            remote(out.at[at], out.at[at], self.fan.at[6 * (hop - 1) + 3 * way + d, a], self.recv.at[a, at], dev)
            for d, dev in enumerate(self.beside)
            for a, out in enumerate(self.outs)
        ]

    def own(self, src):
        for way, there, shard, to in self.ways(0):

            @pl.when(there)
            def _():
                for cp in self.copies(0, way, shard, to, src):
                    cp.start()

    def hop(self, hop):
        for way, there, shard, to in self.ways(hop):
            @pl.when(self.comes(hop, way))
            def _():
                at = 4 * shard + self.m
                for a, out in enumerate(self.outs):
                    landed(out.at[at], self.recv.at[a, at])
                for cp in self.aside(hop, way, shard):
                    cp.start()

            if hop < self.chips - 1:

                @pl.when(there)
                def _():
                    for cp in self.copies(hop, way, shard, to):
                        cp.start()

    def finish(self, src):
        for hop in range(self.chips - 1):
            for way, there, shard, to in self.ways(hop):

                @pl.when(there)
                def _():
                    for cp in self.copies(hop, way, shard, to, src if hop == 0 else None):
                        cp.wait_send()
        for hop in range(1, self.chips):
            for way, there, shard, to in self.ways(hop):

                @pl.when(self.comes(hop, way))
                def _():
                    for cp in self.aside(hop, way, shard):
                        cp.wait_send()


def in_parts(shape, body):
    rows, width = shape
    if rows % 24 or width % 768:
        body((slice(None), slice(None)))
        return
    across = width // 768

    def step(i, carry):
        r = pl.multiple_of(i // across * 24, 8)
        c = pl.multiple_of(i % across * 768, 128)
        body((pl.ds(r, 24), pl.ds(c, 768)))
        return carry

    lax.fori_loop(0, rows // 24 * across, step, 0)


class Sums:
    def __init__(self, ins, acc, r1, rx, ry, rd, s1, v1, ss, vx, vy, vd, own=None):
        self.own = own
        self.t, self.m = lax.axis_index("tok"), lax.axis_index("mdl")
        self.ins, self.acc, self.r1, self.rx, self.ry, self.rd = ins, acc, r1, rx, ry, rd
        self.s1, self.v1, self.ss, self.vx, self.vy, self.vd = s1, v1, ss, vx, vy, vd
        self.count = len(ins)
        self.started = []

    def owner(self, n):
        return self.t ^ (2 * (n // 4) + (n // 2) % 2), self.m ^ (2 * (n % 2))

    def first(self, n, a):
        tt, mm = self.owner(n)
        return remote(
            self.ins[a].at[4 * tt + (mm ^ 1)], self.r1[a].at[n], self.s1.at[n, a], self.v1.at[n, a], (self.t, self.m ^ 1)
        )

    def begin(self, which=None):
        for n in (15, 11, 14, 10, 7, 3, 5, 1, 6, 2, 13, 9, 12, 8, 4, 0):
            for a in range(self.count) if which is None else which:
                self.first(n, a).start()
                if self.own is not None:
                    tt, mm = self.owner(n)
                    pltpu.make_async_copy(self.ins[a].at[4 * tt + mm], self.acc[a].at[n], self.own.at[n, a]).start()

    def hop(self, e, n, dst, slot, vsem, by_x):
        dev = (self.t ^ 1, self.m) if by_x else (self.t, self.m ^ 2)
        return [
            remote(self.acc[a].at[n], dst[a].at[slot], self.ss.at[e, a], vsem.at[slot, a], dev)
            for a in range(self.count)
        ]

    def push(self, *what):
        e = len(self.started)
        self.started.append(what)
        for cp in self.hop(e, *what):
            cp.start()

    def total(self, n, a, more, store):
        tt, mm = self.owner(n)
        self.first(n, a).wait_recv()
        if self.own is not None:
            landed(self.acc[a].at[n], self.own.at[n, a])
        for buf, slot, vsem in more:
            landed(buf[a].at[slot], vsem.at[slot, a])

        def add_part(part):
            out = self.acc[a][(n,) + part] if self.own is not None else self.ins[a][(4 * tt + mm,) + part]
            out = out.astype(F32) + self.r1[a][(n,) + part].astype(F32)
            for buf, slot, vsem in more:
                out = out + buf[a][(slot,) + part].astype(F32)
            store(part, out)

        in_parts(self.acc[a].shape[1:], add_part)

    def add(self, n, more=()):
        for a in range(self.count):
            self.add_one(n, a, more)

    def add_one(self, n, a, more):
        def store(part, out):
            self.acc[a][(n,) + part] = out.astype(self.acc[a].dtype)

        self.total(n, a, more, store)

    def early(self, by_y):
        for k in (3, 2, 1, 0):
            self.add(4 * k + 3)
            self.push(4 * k + 3, self.rd, k, self.vd, k >= by_y)
        for k in (3, 2, 1, 0):
            if k >= by_y:
                self.add(4 * k + 2)
                self.push(4 * k + 2, self.rx, k, self.vx, True)
            else:
                self.add(4 * k + 1)
                self.push(4 * k + 1, self.ry, k, self.vy, False)

    def late(self, by_y):
        for k in (3, 2, 1, 0):
            via = [(self.rd, k, self.vd)]
            if k < by_y:
                self.add(4 * k + 2, via)
                self.push(4 * k + 2, self.rx, k, self.vx, True)
            else:
                self.add(4 * k + 1, via)
                self.push(4 * k + 1, self.ry, k, self.vy, False)

    def column(self, k, a, more=()):
        self.add_one(4 * k, a, [(self.rx, k, self.vx), (self.ry, k, self.vy)] + list(more))

    def column_out(self, a, out):
        def store(part, total):
            out[part] = total

        self.total(0, a, [(self.rx, 0, self.vx), (self.ry, 0, self.vy)], store)

    def finish(self):
        for n in range(16):
            for a in range(self.count):
                self.first(n, a).wait_send()
        for e, what in enumerate(self.started):
            for cp in self.hop(e, *what):
                cp.wait_send()


def sums_scratch(shards, outside):
    n = len(shards)
    bufs = [pltpu.VMEM((k,) + s, d) for k in (16, 16, 4, 4, 4) for s, d in shards]
    sems = [DMA((16, n)), DMA((16, n)), DMA((12, n)), DMA((4, n)), DMA((4, n)), DMA((4, n))]
    return bufs + sems + ([DMA((16, n))] if outside else [])


def take_sums(ins, refs, outside):
    n = len(ins)
    bufs = [refs[i * n : (i + 1) * n] for i in range(5)]
    end = 5 * n + 6 + outside
    return Sums(ins, *bufs, *refs[5 * n : end]), refs[end:]


SMALL_ROWS = 16


def side_by_side(smalls, width):
    step = width // 32
    lane = lax.broadcasted_iota(jnp.int32, (128, width), 0)
    col = lax.broadcasted_iota(jnp.int32, (128, width), 1)
    pick = (lax.rem(col, step) == lane).astype(BF)
    every = lax.dot_general(
        smalls.reshape(32 * SMALL_ROWS, 128).astype(BF), pick, (((1,), (0,)), ((), ())), preferred_element_type=F32
    )
    shard = lax.broadcasted_iota(jnp.int32, (32, SMALL_ROWS, width), 0)
    at = lax.broadcasted_iota(jnp.int32, (32, SMALL_ROWS, width), 2) // step
    return jnp.sum(jnp.where(shard == at, every.reshape(32, SMALL_ROWS, width), 0.0), axis=0)


def attend_kernel(*refs):
    (tokens_ref, starts_ref), masters, vectors = refs[:2], refs[2:6], refs[6:15]
    full_qkv, smalls_out, weights, (heads, of_ref, l_ref, att, begins) = refs[15], refs[16], refs[17:20], refs[20:25]
    (low_qkv, low0, low1, low2, small, smalls, wq, normed, jv, xv, kn, acc, ms, ls, stage) = refs[25:40]
    (s1, v1, local, s_full, r_full, s_sh, r_sh, s_fw, r_fw, s_out, r_out, keep, send, recv, send_z, fan) = refs[40:]
    t, m, z, x, y, c = place()
    xn, yn, sib = (t ^ 1, m), (t, m ^ 2), (t, m ^ 1)
    own = x == c
    role = (x + c) % 2
    hf, hs, owner_m = 3 * z + 2 * x, 3 * z + 1, 2 * y + x
    lows = (low0, low1, low2)
    me = 4 * t + m
    step = low_qkv.shape[0]
    width = 32 * step

    met = greet(chip_group(t, m) + [yn])
    low_qkv[...] = masters[0][...].astype(BF)
    small[...] = jnp.zeros_like(small)
    for v in range(8):
        small[v : v + 1, 0:step] = vectors[v][...].astype(BF).astype(F32)
    for q in range(4):
        small[8 + q : 9 + q, 0:step] = vectors[8][:, q * step : (q + 1) * step].astype(BF).astype(F32)
    small[12:13, 0 : starts_ref.shape[1]] = starts_ref[...].astype(F32)
    smalls[me] = small[...]
    met()

    class Shards:
        def __init__(self, ref):
            self.at = self
            self.ref = ref

        def __getitem__(self, shard):
            return self.ref.at[pl.ds(pl.multiple_of(step * shard, 8), step)]

    first = Pushes((Shards(full_qkv), smalls), s1, v1)
    for dev in [(t ^ 2, m), (t ^ 4, m), (t ^ 6, m), xn, yn, sib]:
        first.push(me, dev, (low_qkv, small))
    work = Pushes(weights, send, recv)
    for low, master in zip(lows, masters[1:]):
        low[...] = master[...].astype(BF)
    column = Line(weights, send_z, recv, fan, (xn, yn, sib))
    own_rows = [pltpu.make_async_copy(low_qkv, Shards(full_qkv)[me], local.at[0])]
    own_rows += [pltpu.make_async_copy(lows[a], weights[a].at[me], local.at[1 + a]) for a in range(3)]
    for cp in own_rows:
        cp.start()

    values = tokens_ref[...].astype(F32)
    center = values - jnp.mean(values, axis=-1, keepdims=True)
    spread = jnp.mean(center * center, axis=-1, keepdims=True)
    xhat = center * lax.rsqrt(spread + epsilon)

    for k in range(1, 4):
        shard = 4 * (t ^ (2 * k)) + m
        first.arrived(shard)
        for dev in (xn, yn, sib):
            first.push(shard, dev)
    column.own(lows)
    for k in range(4):
        col = t ^ (2 * k)
        xi, yi = 4 * (col ^ 1) + m, 4 * col + (m ^ 2)
        first.arrived(xi)
        if k < 2:
            first.push(xi, yn)
        first.push(xi, sib)
        first.arrived(yi)
        if k >= 2:
            first.push(yi, xn)
        first.push(yi, sib)
    for dev in (xn, yn, sib):
        work.push(me, dev, lows)
    column.hop(1)
    for k in range(4):
        di = 4 * (t ^ (2 * k) ^ 1) + (m ^ 2)
        first.arrived(di)
        first.push(di, sib)
    for k in range(4):
        for a in (0, 1):
            for b in (0, 2):
                first.arrived(4 * (t ^ (2 * k) ^ a) + (m ^ b ^ 1))
    column.hop(2)
    for cp in own_rows:
        cp.wait()
    load = pltpu.make_async_copy(full_qkv, wq, local.at[4])
    load.start()
    share = pltpu.make_async_copy(smalls, smalls_out, local.at[5])
    share.start()
    flat = side_by_side(smalls[...], width)
    normed[...] = (xhat * flat[3:4] + flat[4:5]).astype(BF)
    bias = jnp.concatenate([flat[0:1], jnp.zeros_like(flat[0:1]), flat[1:2]], axis=1)
    begins[0] = smalls[m, 12:13, :].astype(jnp.int32)
    begins[1] = smalls[owner_m, 12:13, :].astype(jnp.int32)
    load.wait()
    for n in range(9):
        part = slice(n * 256, (n + 1) * 256)
        block = lax.dot_general(
            normed[...], wq[:, part], (((1,), (0,)), ((), ())), preferred_element_type=F32
        )
        block = (block + bias[:, part]).T.astype(BF)
        for h in range(4):
            g = 4 * n + h
            jv[g // 12, g % 12] = block[h * HD : (h + 1) * HD]

    def full(k):
        d = t ^ k
        return jv.at[:, 3 * (d // 2) + 2 * (d % 2)], xv.at[0, t], s_full.at[k], r_full.at[t], (d, m)

    def shared(k):
        zd = z ^ k
        return jv.at[:, 3 * zd + 1], xv.at[1, t], s_sh.at[k], r_sh.at[t], (2 * zd + c, m)

    for k in (4, 5, 6, 7, 2, 3, 1):
        remote(*full(k)).start()
    loc = full(0)
    pltpu.make_async_copy(loc[0], loc[1], loc[3]).start()
    column.hop(3)
    for k in range(1, 8):
        remote(*full(k)).wait_send()
    for k in (2, 3, 1):
        remote(*shared(k)).start()
    send_unless(own, *shared(0))

    def keep_head(slot):
        cp = pltpu.make_async_copy(xv.at[slot], heads.at[slot], keep.at[slot])
        cp.start()
        return cp

    for b in range(8):
        landed(xv.at[0, b], r_full.at[b])
    kept = [keep_head(0)]
    for b in range(8):
        kn[0, b] = xv[0, b, 1].T

    def begin_of(slot, task):
        lane = lax.broadcasted_iota(jnp.int32, (1, 128), 1)
        return jnp.sum(jnp.where(lane == task, begins[slot], 0), axis=1, keepdims=True)

    def finish_task(slot, task, row, head, mdl, alone):
        for h in range(2):
            b, u = 2 * task + h, 2 * row + h
            out = acc[h] / ls[h]
            of_ref[u] = out
            stage[u] = out.astype(BF)
            l_ref[u] = ms[h] + jnp.log2(ls[h])
            send_unless((b == t) & alone, stage.at[u], att.at[head], s_out.at[u], r_out.at[head], (b, mdl))

    def full_task(w, carry):
        forward_task(0, w, begin_of(0, w), xv, kn, acc, ms, ls)
        finish_task(0, w, w, hf, m, t >= 0)
        return carry

    lax.fori_loop(0, 3, full_task, 0)

    for k in range(4):
        col = t ^ (2 * k)
        xi, yi = 4 * (col ^ 1) + m, 4 * col + (m ^ 2)
        work.arrived(xi)
        if k < 3:
            work.push(xi, yn)
        work.push(xi, sib)
        work.arrived(yi)
        if k == 3:
            work.push(yi, xn)
        work.push(yi, sib)

    def forward(k):
        b = t ^ k
        return remote(xv.at[1, b], xv.at[1, b], s_fw.at[k], r_fw.at[b], sib)

    @pl.when(own)
    def _():
        for k in (0, 1, 2, 3, 6, 7, 4, 5):
            landed(xv.at[1, t ^ k], r_sh.at[t ^ k])
            forward(k).start()

    lax.fori_loop(3, 4, full_task, 0)

    @pl.when(jnp.logical_not(own))
    def _():
        for k in range(8):
            forward(k).wait_recv()

    kept.append(keep_head(1))
    for b in range(8):
        kn[1, b] = xv[1, b, 1].T

    def shared_task(n, carry):
        task = jnp.where(n == 0, role, 3 - role)
        forward_task(1, task, begin_of(1, task), xv, kn, acc, ms, ls)
        finish_task(1, task, 4 + n, hs, owner_m, own)
        return carry

    lax.fori_loop(0, 2, shared_task, 0)

    for k in range(4):
        di = 4 * (t ^ (2 * k) ^ 1) + (m ^ 2)
        work.arrived(di)
        work.push(di, sib)
    for h in range(12):
        landed(att.at[h], r_out.at[h])
    for k in range(4):
        for a in (0, 1):
            for b in (0, 2):
                work.arrived(4 * (t ^ (2 * k) ^ a) + (m ^ b ^ 1))
    first.finish()
    work.finish()
    column.finish(lows)
    for k in (1, 2, 3):
        remote(*shared(k)).wait_send()
    sent_unless(own, *shared(0))

    @pl.when(own)
    def _():
        for k in range(8):
            forward(k).wait_send()

    for w in range(4):
        for h in range(2):
            b, u = 2 * w + h, 2 * w + h
            sent_unless(b == t, stage.at[u], att.at[hf], s_out.at[u], r_out.at[hf], (b, m))
    for n in range(2):
        task = role if n == 0 else 3 - role
        for h in range(2):
            b, u = 2 * task + h, 8 + 2 * n + h
            sent_unless((b == t) & own, stage.at[u], att.at[hs], s_out.at[u], r_out.at[hs], (b, owner_m))
    for cp in kept:
        cp.wait()
    share.wait()


def attend(tokens, starts, masters, vectors, cid):
    rows, width = tokens.shape
    step = width // 32
    head = (HD, BLK)
    S, V = jax.ShapeDtypeStruct, pltpu.VMEM
    outs = pl.pallas_call(
        attend_kernel,
        out_shape=(S((width, 3 * width), BF), S((32, SMALL_ROWS, 128), F32))
        + tuple(S((32,) + w.shape, BF) for w in masters[1:])
        + (S((2, 8, 3) + head, BF), S((12,) + head, F32), S((12, 1, BLK), F32), S((12,) + head, BF), S((2, 1, 128), jnp.int32)),
        in_specs=[VMEMS] * 15,
        out_specs=(ANYS,) * 6 + (VMEMS, VMEMS, ANYS, VMEMS),
        scratch_shapes=[V(w.shape, BF) for w in masters]
        + [
            V((SMALL_ROWS, 128), F32),
            V((32, SMALL_ROWS, 128), F32),
            V((width, 3 * width), BF),
            V((rows, width), BF),
            V((3, 12) + head, BF),
            V((2, 8, 3) + head, BF),
            V((2, 8, BLK, HD), BF),
            V((2,) + head, F32),
            V((2, 1, BLK), F32),
            V((2, 1, BLK), F32),
            V((12,) + head, BF),
        ]
        + [DMA((31, 2)), DMA((2, 32)), DMA((6,))]
        + [DMA((8,)), DMA((8,)), DMA((4,)), DMA((8,)), DMA((8,)), DMA((8,)), DMA((12,)), DMA((12,)), DMA((2,))]
        + [DMA((19, 3)), DMA((3, 32)), DMA((6, 3)), DMA((18, 3))],
        name="attend",
        compiler_params=pltpu.CompilerParams(collective_id=cid, has_side_effects=True, vmem_limit_bytes=62 << 20),
    )(tokens, starts, *masters, *vectors)
    return outs[0], outs[1], outs[2:5], outs[5:]


FF_BLOCK = 512
HBMS = pl.BlockSpec(memory_space=pltpu.HBM)


def shard_rows(rows, step):
    r, n = rows.shape
    count = n // step
    shard = lax.broadcasted_iota(jnp.int32, (count, r, n), 0)
    at = lax.broadcasted_iota(jnp.int32, (count, r, n), 2) // step
    spread = jnp.where(shard == at, rows[None], 0.0).reshape(count * r, n)
    col = lax.broadcasted_iota(jnp.int32, (n, 128), 0)
    lane = lax.broadcasted_iota(jnp.int32, (n, 128), 1)
    pick = (lax.rem(col, step) == lane).astype(F32)
    out = lax.dot_general(
        spread, pick, (((1,), (0,)), ((), ())), precision=lax.Precision.HIGHEST, preferred_element_type=F32
    )
    return out.reshape(count, r, 128)


def expand_row(smalls, hidden):
    step = hidden // 128
    lane = lax.broadcasted_iota(jnp.int32, (128, hidden), 0)
    col = lax.broadcasted_iota(jnp.int32, (128, hidden), 1)
    pick = (lax.rem(col, step) == lane).astype(BF)
    every = nn(smalls[:, 8:12, :].reshape(128, 128).astype(BF), pick)
    return jnp.sum(jnp.where(lane == col // step, every, 0.0), axis=0, keepdims=True)


def middle_kernel(
    x_ref, c_ref, att_any, smalls_any, wo_any, we_ref, ws_ref,
    out_ref, gh_ref, gm_any, dwo_any, dwe_ref, dws_ref, flat, vec_ref, dbe_ref,
    be, hidden, xhat, inv, n2, n2t, out_acc, dn2, att_ref, smalls_ref, wo_ref, gm_ref, dwo_ref, sems,
):
    i = pl.program_id(0)
    last = pl.num_programs(0) - 1
    width = x_ref.shape[1]

    @pl.when(i == 0)
    def _():
        pairs = ((smalls_any, smalls_ref), (att_any, att_ref), (wo_any, wo_ref))
        loads = [pltpu.make_async_copy(a, b, sems.at[n]) for n, (a, b) in enumerate(pairs)]
        for cp in loads:
            cp.start()
        loads[0].wait()
        flat[...] = side_by_side(smalls_ref[...], width)
        row = expand_row(smalls_ref[...], be.shape[0] * FF_BLOCK)
        for n in range(be.shape[0]):
            be[n] = row[:, n * FF_BLOCK : (n + 1) * FF_BLOCK]
        loads[1].wait()
        loads[2].wait()
        branch = nn(att_ref[...].T, wo_ref[...]) + flat[2:3]
        h = x_ref[...].astype(F32) + branch
        hidden[...] = h
        center = h - jnp.mean(h, axis=-1, keepdims=True)
        scale = lax.rsqrt(jnp.mean(center * center, axis=-1, keepdims=True) + epsilon)
        inv[...] = scale
        xhat[...] = center * scale
        low = (xhat[...] * flat[5:6] + flat[6:7]).astype(BF)
        n2[...] = low
        n2t[...] = low.T
        out_acc[...] = jnp.zeros_like(out_acc)
        dn2[...] = jnp.zeros_like(dn2)

    u = nn(n2[...], we_ref[...]) + be[i]
    square = u * u
    th = jnp.tanh(gelu_coeff * (u + 0.044715 * square * u))
    half = 0.5 * (1.0 + th)
    act = (u * half).astype(BF)
    slope = half + 0.5 * u * (1.0 - th * th) * (gelu_coeff * (1.0 + 3.0 * 0.044715 * square))
    out_acc[...] += nn(act, ws_ref[...])
    ge = nt(c_ref[...], ws_ref[...]) * slope
    ge = ge.astype(BF)
    dbe_ref[...] = jnp.sum(ge.astype(F32), axis=0, keepdims=True)
    dws_ref[...] = nn(act.T, c_ref[...]).astype(BF)
    dwe_ref[...] = nn(n2t[...], ge).astype(BF)
    dn2[...] += nt(ge, we_ref[...])

    @pl.when(i == last)
    def _():
        out_ref[...] = (hidden[...] + (out_acc[...] + flat[7:8])).astype(BF)
        up = c_ref[...].astype(F32)
        e = dn2[...]
        f = e * flat[5:6]
        xh = xhat[...]
        dv = f - jnp.mean(f, axis=-1, keepdims=True) - xh * jnp.mean(f * xh, axis=-1, keepdims=True)
        gh = up + dv * inv[...]
        gh_ref[...] = gh
        ga = gh.astype(BF)
        gm_ref[...] = nt(wo_ref[...], ga).astype(BF)
        saves = [pltpu.make_async_copy(gm_ref, gm_any, sems.at[3])]
        saves[0].start()
        dwo_ref[...] = nn(att_ref[...], ga).astype(BF)
        saves.append(pltpu.make_async_copy(dwo_ref, dwo_any, sems.at[4]))
        saves[1].start()
        vec_ref[0:1] = jnp.sum(ga.astype(F32), axis=0, keepdims=True)
        vec_ref[1:2] = jnp.sum(e * xh, axis=0, keepdims=True)
        vec_ref[2:3] = jnp.sum(e, axis=0, keepdims=True)
        vec_ref[3:4] = jnp.sum(up, axis=0, keepdims=True)
        vec_ref[4:8] = jnp.zeros((4, width), F32)
        for cp in saves:
            cp.wait()


def middle(x, c, att, smalls, wo, we, ws):
    rows, width = x.shape
    hidden = we.shape[1]
    S, V = jax.ShapeDtypeStruct, pltpu.VMEM
    n = hidden // FF_BLOCK
    across = pl.BlockSpec((width, FF_BLOCK), lambda i: (0, i))
    down = pl.BlockSpec((FF_BLOCK, width), lambda i: (i, 0))
    whole = lambda a: pl.BlockSpec(a.shape, lambda i: (0,) * len(a.shape), pipeline_mode=pl.Buffered(1))
    outs = (
        S((rows, width), BF),
        S((rows, width), F32),
        S((width, rows), BF),
        S((width, width), BF),
        S((width, hidden), BF),
        S((hidden, width), BF),
        S((SMALL_ROWS, width), F32),
        S((8, width), F32),
        S((1, hidden), F32),
    )
    return pl.pallas_call(
        middle_kernel,
        grid=(n,),
        out_shape=outs,
        in_specs=[whole(x), whole(c), HBMS, HBMS, HBMS, across, down],
        out_specs=(whole(outs[0]), whole(outs[1]), HBMS, HBMS)
        + (across, down, whole(outs[6]), whole(outs[7]), pl.BlockSpec((1, FF_BLOCK), lambda i: (0, i))),
        scratch_shapes=[
            V((n, 1, FF_BLOCK), F32),
            V((rows, width), F32),
            V((rows, width), F32),
            V((rows, 1), F32),
            V((rows, width), BF),
            V((width, rows), BF),
            V((rows, width), F32),
            V((rows, width), F32),
            V(att.shape, BF),
            V(smalls.shape, F32),
            V(wo.shape, BF),
            V((width, rows), BF),
            V((width, width), BF),
            DMA((5,)),
        ],
        name="middle",
        compiler_params=pltpu.CompilerParams(vmem_limit_bytes=62 << 20),
    )(x, c, att, smalls, wo, we, ws)


def attend_back_kernel(*refs):
    g_ref, heads_ref, of_ref, l_ref, tokens_ref, begins, flat_ref, vec_ref, bias_ref, wq_ref = refs[:10]
    ins, dx_ref, last_outs, outs = refs[10:13], refs[13], refs[14:16], refs[16:19]
    work, rest = take_sums(ins, refs[19:], True)
    dwq, small, gj, wq, normed_t, rzp = rest[0], rest[1], rest[2], rest[3], rest[4], rest[5:8]
    tail, rest = take_sums((dwq, small), rest[8:], False)
    rz, rest = rest[:2], rest[2:]
    (xv, gv, kn, vn, dkv, dq, lsum, delta, stage, stage_kv, got, stage_sh, ofv, dxv) = rest[:14]
    (s_full, r_full, s_sh, r_sh, s_fw, r_fw, s_q, r_q, s_kv, r_kv, s_shkv, s_part, r_part) = rest[14:27]
    szp, vzp, sz, vz, local = rest[27:]
    count = len(ins)
    t, m, z, x, y, c = place()
    sib = (t, m ^ 1)
    met = greet(chip_group(t, m) + [(t, m ^ 2)])
    def load_of(first):
        return pltpu.make_async_copy(of_ref.at[pl.ds(first, 4)], ofv, local.at[5])

    loads = [pltpu.make_async_copy(heads_ref.at[s, :, 2], stage_kv.at[:, s], local.at[s]) for s in range(2)]
    loads += [pltpu.make_async_copy(heads_ref.at[s, :, pl.ds(0, 2)], xv.at[s], local.at[2 + s]) for s in range(2)]
    load_of(8).start()
    for cp in loads:
        cp.start()
    met()
    own = x == c
    role = (x + c) % 2
    hf, hs, owner_m = 3 * z + 2 * x, 3 * z + 1, 2 * y + x
    order = (4, 5, 6, 7, 2, 3, 1)

    def full(k):
        d = t ^ k
        return g_ref.at[3 * (d // 2) + 2 * (d % 2)], gv.at[0, t], s_full.at[k], r_full.at[t], (d, m)

    def shared(k):
        zd = z ^ k
        return g_ref.at[3 * zd + 1], gv.at[1, t], s_sh.at[k], r_sh.at[t], (2 * zd + c, m)

    for k in (2, 3, 1):
        remote(*shared(k)).start()
    send_unless(own, *shared(0))
    loc = full(0)
    pltpu.make_async_copy(loc[0], loc[1], loc[3]).start()
    work.begin()
    for cp in loads:
        cp.wait()
    for s in range(2):
        for b in range(8):
            kn[s, b] = xv[s, b, 1].T
            vn[s, b] = stage_kv[b, s].T
    dkv[...] = jnp.zeros_like(dkv)
    dq[...] = jnp.zeros_like(dq)
    for k in (1, 2, 3):
        remote(*shared(k)).wait_send()
    sent_unless(own, *shared(0))
    for k in order:
        remote(*full(k)).start()

    def forward(k):
        b = t ^ k
        return remote(gv.at[1, b], gv.at[1, b], s_fw.at[k], r_fw.at[b], sib)

    @pl.when(own)
    def _():
        for k in (0, 1, 2, 3, 6, 7, 4, 5):
            landed(gv.at[1, t ^ k], r_sh.at[t ^ k])
            forward(k).start()

    work.early(4)

    @pl.when(jnp.logical_not(own))
    def _():
        for k in range(8):
            forward(k).wait_recv()

    def begin_of(slot, task):
        lane = lax.broadcasted_iota(jnp.int32, (1, 128), 1)
        return jnp.sum(jnp.where(lane == task, begins[slot], 0), axis=1, keepdims=True)

    def ready(slot, b, u):
        lsum[slot, b] = l_ref[u]
        delta[slot, b] = jnp.sum(gv[slot, b].astype(F32) * ofv[u % 4], axis=0, keepdims=True)

    def out_q(slot, b, u):
        stage[u] = (dq[u] * HD ** (-0.5)).astype(BF)
        if slot:
            send_unless((b == t) & own, stage.at[u], gj.at[0, hs], s_q.at[u], r_q.at[hs], (b, owner_m))
        else:
            send_unless(b == t, stage.at[u], gj.at[0, hf], s_q.at[u], r_q.at[hf], (b, m))

    args = (xv, gv, kn, vn, lsum, delta, dkv, dq)

    def shared_task(n, carry):
        task = jnp.where(n == 0, role, 3 - role)
        begin = begin_of(1, task)

        def step(j, carry):
            backward_units(1, task, 8 + 2 * n, 0, [(j, h, None, 0, BLK, 0, BLK) for h in range(2)], begin, *args)
            return carry

        lax.fori_loop(0, 2 * task, step, 0)
        backward_units(1, task, 8 + 2 * n, 0, diag_units(task), begin, *args)
        for h in range(2):
            out_q(1, 2 * task + h, 8 + 2 * n + h)
        return carry

    load_of(8).wait()
    for n in range(2):
        task = role if n == 0 else 3 - role
        for h in range(2):
            ready(1, 2 * task + h, 8 + 2 * n + h)
    load_of(0).start()
    lax.fori_loop(0, 2, shared_task, 0)

    def part(k):
        b = t ^ k
        return remote(dkv.at[b], got.at[b], s_part.at[k], r_part.at[b], sib)

    def shared_kv(k):
        b = t ^ k
        return stage_sh.at[b], gj.at[pl.ds(1, 2), hs], s_shkv.at[k], r_kv.at[hs], (b, m)

    @pl.when(jnp.logical_not(own))
    def _():
        for k in order + (0,):
            part(k).start()

    for b in range(8):
        landed(gv.at[0, b], r_full.at[b])
    load_of(0).wait()
    for b in range(4):
        ready(0, b, b)
    load_of(4).start()
    load_of(4).wait()
    for b in range(4, 8):
        ready(0, b, b)

    @pl.when(own)
    def _():
        for k in order + (0,):
            b = t ^ k
            part(k).wait_recv()
            stage_sh[b, 0] = ((dkv[b, 0] + got[b, 0]) * HD ** (-0.5)).astype(BF)
            stage_sh[b, 1] = (dkv[b, 1] + got[b, 1]).astype(BF)
            a = shared_kv(k)
            if k:
                remote(*a).start()
            else:
                pltpu.make_async_copy(a[0], a[1], a[3]).start()

    def full_keys(s, carry):
        keys = z ^ (3 - s)
        dkv[8:10] = jnp.zeros((2,) + dkv.shape[1:], F32)
        backward_units(0, keys, 2 * keys, 8 - 2 * keys, diag_units(keys), begin_of(0, keys), *args)

        def step(n, carry):
            task, j = n // 2, 2 * keys + n % 2
            units = [(j, h, None, 0, BLK, 0, BLK) for h in range(2)]
            backward_units(0, task, 2 * task, 8 - 2 * keys, units, 0, *args)
            return carry

        lax.fori_loop(2 * keys + 2, 8, step, 0)
        for i in range(2):
            b = 2 * keys + i
            stage_kv[b, 0] = (dkv[8 + i, 0] * HD ** (-0.5)).astype(BF)
            stage_kv[b, 1] = dkv[8 + i, 1].astype(BF)
            send_unless(b == t, stage_kv.at[b], gj.at[pl.ds(1, 2), hf], s_kv.at[b], r_kv.at[hf], (b, m))

        @pl.when(s == 1)
        def _():
            work.late(4)

        return carry

    lax.fori_loop(0, 4, full_keys, 0)
    for b in range(8):
        out_q(0, b, b)
    along = []

    def z_push(sums, k, a, buf, slot, ssem, vsem, to, more=()):
        sums.column(k, a, more)
        cp = remote(sums.acc[a].at[4 * k], buf[a].at[slot], ssem.at[slot, a], vsem.at[slot, a], (t ^ (2 * to), m))
        cp.start()
        along.append(cp)

    width = tokens_ref.shape[1]
    step = width // 32
    gain, shift = flat_ref[3:4], flat_ref[4:5]

    def norm(half):
        values = tokens_ref[half].astype(F32)
        center = values - jnp.mean(values, axis=-1, keepdims=True)
        inv = lax.rsqrt(jnp.mean(center * center, axis=-1, keepdims=True) + epsilon)
        return center * inv, inv

    load = pltpu.make_async_copy(wq_ref, wq, local.at[4])
    load.start()
    halves = [slice(n * 256, (n + 1) * 256) for n in range(tokens_ref.shape[0] // 256)]
    for half in halves:
        normed_t[:, half] = (norm(half)[0] * gain + shift).astype(BF).T

    for a in range(count):
        z_push(work, 3, a, rzp, 1, szp, vzp, 1)
        z_push(work, 1, a, rzp, 0, szp, vzp, 1)

    for h in range(12):
        landed(gj.at[0, h], r_q.at[h])
        landed(gj.at[pl.ds(1, 2), h], r_kv.at[h])
    load.wait()
    for n in range(9):
        grads = gj[n // 3, 4 * (n % 3) : 4 * (n % 3) + 4].reshape(256, BLK)
        block = nt(normed_t[...], grads)
        dwq[:, :, n * 256 : (n + 1) * 256] = block.reshape(32, step, 256).astype(BF)
    tail.begin([0])
    dgain, dshift = jnp.zeros((1, width), F32), jnp.zeros((1, width), F32)
    for half in halves:
        e = jnp.zeros((width, 256), F32)
        for n in range(9):
            grads = gj[n // 3, 4 * (n % 3) : 4 * (n % 3) + 4, :, half].reshape(256, 256)
            e = e + nn(wq[:, n * 256 : (n + 1) * 256], grads)
        e = e.T
        xhat, inv = norm(half)
        f = e * gain
        dv = f - jnp.mean(f, axis=-1, keepdims=True) - xhat * jnp.mean(f * xhat, axis=-1, keepdims=True)
        if half.start:
            out_x.wait()
        dxv[...] = dv * inv
        out_x = pltpu.make_async_copy(dxv, dx_ref.at[half], local.at[6])
        out_x.start()
        dgain = dgain + jnp.sum(e * xhat, axis=0, keepdims=True)
        dshift = dshift + jnp.sum(e, axis=0, keepdims=True)
    ones = jnp.ones((8, BLK), BF)
    db_query = nt(ones, gj[0].reshape(width, BLK))[0:1]
    db_value = nt(ones, gj[2].reshape(width, BLK))[0:1]
    rows = [db_query, db_value, vec_ref[0:1], dgain, dshift, vec_ref[1:4]]
    small[:, 0:8] = shard_rows(jnp.concatenate(rows, axis=0), step)
    small[:, 8:12] = bias_ref[...]
    small[:, 12:16] = jnp.zeros((32, 4, 128), F32)
    tail.begin([1])
    for a in range(count):
        z_push(work, 2, a, rzp, 2, szp, vzp, 2, [(rzp, 1, vzp)])
    tail.early(2)
    tail.late(2)
    for k in (3, 2, 1):
        for a in range(2):
            z_push(tail, k, a, rz, k - 1, sz, vz, k)

    def gather_z(a, out, buf, slots, vsem):
        for n in slots:
            landed(buf.at[n], vsem.at[n, a])

        def add_part(part):
            total = out[part]
            for n in slots:
                total = total + buf[(n,) + part].astype(F32)
            out[part] = total

        in_parts(out.shape, add_part)

    for a in range(count):
        work.column_out(a, outs[a])
        gather_z(a, outs[a], rzp[a], (0, 2), vzp)
    for a in range(2):
        tail.column_out(a, last_outs[a])
        gather_z(a, last_outs[a], rz[a], (0, 1, 2), vz)
    out_x.wait()
    tail.finish()
    for cp in along:
        cp.wait_send()
    work.finish()
    for k in range(1, 8):
        remote(*full(k)).wait_send()
    for b in range(8):
        sent_unless(b == t, stage.at[b], gj.at[0, hf], s_q.at[b], r_q.at[hf], (b, m))
        sent_unless(b == t, stage_kv.at[b], gj.at[pl.ds(1, 2), hf], s_kv.at[b], r_kv.at[hf], (b, m))
    for n in range(2):
        task = role if n == 0 else 3 - role
        for h in range(2):
            b, u = 2 * task + h, 8 + 2 * n + h
            sent_unless((b == t) & own, stage.at[u], gj.at[0, hs], s_q.at[u], r_q.at[hs], (b, owner_m))

    @pl.when(own)
    def _():
        for k in range(8):
            forward(k).wait_send()
        for k in range(1, 8):
            remote(*shared_kv(k)).wait_send()

    @pl.when(jnp.logical_not(own))
    def _():
        for k in range(8):
            part(k).wait_send()


def attend_back(grad_mix, heads, out_full, log_sum, tokens, begins, flat, vec, bias, full_qkv, grads, cid):
    n = len(grads)
    rows, width = tokens.shape
    head = (HD, BLK)
    S, V = jax.ShapeDtypeStruct, pltpu.VMEM
    shards = [(g.shape[1:], BF) for g in grads]
    last = [((width // 32, 3 * width), BF), ((SMALL_ROWS, 128), F32)]
    return pl.pallas_call(
        attend_back_kernel,
        out_shape=(S((rows, width), F32),) + tuple(S(s, F32) for s, d in last + shards),
        in_specs=[ANYS] * 3 + [VMEMS] * 6 + [ANYS] + [ANYS] * n,
        out_specs=(ANYS,) + (VMEMS,) * (2 + n),
        scratch_shapes=sums_scratch(shards, True)
        + [V((32,) + s, d) for s, d in last]
        + [V((3, 12) + head, BF), V((width, 3 * width), BF), V((width, rows), BF)]
        + [V((3,) + s, d) for s, d in shards]
        + sums_scratch(last, False)
        + [V((3,) + s, d) for s, d in last]
        + [
            V((2, 8, 2) + head, BF),
            V((2, 8) + head, BF),
            V((2, 8, BLK, HD), BF),
            V((2, 8, BLK, HD), BF),
            V((10, 2) + head, F32),
            V((12,) + head, F32),
            V((2, 8, 1, BLK), F32),
            V((2, 8, 1, BLK), F32),
            V((12,) + head, BF),
            V((8, 2) + head, BF),
            V((8, 2) + head, F32),
            V((8, 2) + head, BF),
            V((4,) + head, F32),
            V((256, width), F32),
        ]
        + [DMA((8,)), DMA((8,)), DMA((4,)), DMA((8,)), DMA((8,)), DMA((8,)), DMA((12,)), DMA((12,))]
        + [DMA((8,)), DMA((12,)), DMA((8,)), DMA((8,)), DMA((8,))]
        + [DMA((4, n)), DMA((4, n)), DMA((4, 2)), DMA((4, 2)), DMA((7,))],
        name="attend_back",
        compiler_params=pltpu.CompilerParams(collective_id=cid, has_side_effects=True, vmem_limit_bytes=62 << 20),
    )(grad_mix, heads, out_full, log_sum, tokens, begins, flat, vec, bias, full_qkv, *grads)


def by_heads(
    tokens,
    cotangent,
    starts,
    w_qkv,
    b_query,
    b_value,
    w_out,
    b_out,
    gain_one,
    shift_one,
    gain_two,
    shift_two,
    w_expand,
    b_expand,
    w_shrink,
    b_shrink,
):
    rows, width = tokens.shape[1:]
    hidden = b_expand.shape[0] * 32
    vectors = [b_query, b_value, b_out, gain_one, shift_one, gain_two, shift_two, b_shrink, b_expand]
    full_qkv, smalls, rest, (heads, out_full, log_sum, attention, begins) = attend(
        tokens[0], starts, [w_qkv, w_out, w_expand, w_shrink], [v.reshape(1, -1) for v in vectors], 1
    )
    full_out, full_expand, full_shrink = (w.reshape(-1, w.shape[-1]) for w in rest)
    attention = attention.reshape(width, rows)
    step = width // 32
    layer_out, grad_hidden, grad_mix, dw_out, dw_expand, dw_shrink, flat, sums, db_expand = middle(
        tokens[0], cotangent[0], attention, smalls, full_out, full_expand, full_shrink
    )
    bias = jnp.pad(db_expand.reshape(32, 4, step), [(0, 0), (0, 0), (0, 128 - step)])
    shards = lambda w: w.reshape((32, -1) + w.shape[1:])
    dtokens, dw_qkv, smalls, dw_out, dw_expand, dw_shrink = attend_back(
        grad_mix.reshape(12, HD, rows),
        heads,
        out_full,
        log_sum,
        tokens[0],
        begins,
        flat,
        sums,
        bias,
        full_qkv,
        [shards(dw_out), shards(dw_expand), shards(dw_shrink)],
        2,
    )
    step = width // 32
    vecs = [smalls[i, :step] for i in range(8)]
    db_query, db_value, db_out, dgain_one, dshift_one, dgain_two, dshift_two, db_shrink = vecs
    db_expand = smalls[8:12, :step].reshape(-1)
    return (
        layer_out.reshape(1, rows, width),
        (grad_hidden + dtokens).reshape(1, rows, width),
        dw_qkv,
        db_query,
        db_value,
        dw_out,
        db_out,
        dgain_one,
        dshift_one,
        dgain_two,
        dshift_two,
        dw_expand,
        db_expand,
        dw_shrink,
        db_shrink,
    )


def solution(mesh):
    rows, vector, seq = P(("tok", "mdl"), None), P(("tok", "mdl")), P("mdl", "tok", None)
    by_name = dict(m=rows, v=vector, s=seq)
    fits = mesh.shape["tok"] == 8 and mesh.shape["mdl"] == 4
    return jax.shard_map(
        by_heads if fits else general,
        mesh=mesh,
        in_specs=(seq, seq, P("mdl", None)) + tuple(by_name[k] for k in "mvvmvvvvvmvmv"),
        out_specs=tuple(by_name[k] for k in "ssmvvmvvvvvmvmv"),
        check_vma=False,
    )
```

```python
import functools
import math

import jax
import jax.numpy as jnp
from jax import lax
from jax.experimental import pallas as pl
from jax.experimental.pallas import tpu as pltpu
from jax.sharding import PartitionSpec as P

HD = 64
PIECE = 256
KEYB = 512


epsilon = 1e-05
masked_score = -1e30
gelu_coeff = 0.7978845608028654


def layer_norm(values, gain_vec, shift_vec):
    center = values - jnp.mean(values, axis=-1, keepdims=True)
    spread = jnp.mean(center * center, axis=-1, keepdims=True)
    return center * lax.rsqrt(spread + epsilon) * gain_vec + shift_vec


def gelu_tanh(inputs):
    return (
        0.5 * inputs * (1.0 + jnp.tanh(gelu_coeff * (inputs + 0.044715 * inputs * inputs * inputs)))
    )


def piece_ids(begins, positions):
    inside = (positions[:, None] >= begins[None, :]) & (
        positions[:, None] < begins[None, :] + PIECE
    )
    labels = jnp.arange(1, begins.shape[0] + 1, dtype=jnp.int32)
    return jnp.sum(jnp.where(inside, labels[None, :], 0), axis=1) - 1


def block_scores(query_heads, key_heads, query_pos, query_lab, begins, block_index, scaling):
    key_block = lax.dynamic_slice_in_dim(key_heads, block_index * KEYB, KEYB, 0)
    key_pos = block_index * KEYB + jnp.arange(KEYB, dtype=jnp.int32)
    key_lab = piece_ids(begins, key_pos)
    scores = (
        jnp.einsum("qhd,khd->hqk", query_heads, key_block, preferred_element_type=jnp.float32)
        * scaling
    )
    allowed = (key_pos[None, :] <= query_pos[:, None]) | (
        key_lab[None, :] == query_lab[:, None]
    ) & (query_lab[:, None] >= 0)
    return jnp.where(allowed[None, :, :], scores, masked_score)


def attend_forward(
    query_heads, key_heads, value_heads, query_pos, query_lab, begins, needed, scaling
):
    local_rows = query_heads.shape[0]
    head_count = query_heads.shape[1]

    def stats_step(block_index, loop_state):
        highest, summed = loop_state
        masked = block_scores(
            query_heads, key_heads, query_pos, query_lab, begins, block_index, scaling
        )
        new_high = jnp.maximum(highest, jnp.max(masked, axis=-1))
        summed = summed * jnp.exp(highest - new_high) + jnp.sum(
            jnp.exp(masked - new_high[:, :, None]), axis=-1
        )
        return (new_high, summed)

    starting = (
        jnp.full((head_count, local_rows), masked_score, jnp.float32),
        jnp.zeros((head_count, local_rows), jnp.float32),
    )
    highest, summed = lax.fori_loop(0, needed, stats_step, starting)

    def mix_step(block_index, running):
        masked = block_scores(
            query_heads, key_heads, query_pos, query_lab, begins, block_index, scaling
        )
        prob_low = (jnp.exp(masked - highest[:, :, None]) / summed[:, :, None]).astype(jnp.bfloat16)
        value_block = lax.dynamic_slice_in_dim(value_heads, block_index * KEYB, KEYB, 0)
        return running + jnp.einsum(
            "hqk,khd->qhd", prob_low, value_block, preferred_element_type=jnp.float32
        )

    mixture = lax.fori_loop(0, needed, mix_step, jnp.zeros(query_heads.shape, jnp.float32))
    return (mixture, highest, summed)


def attend_backward(
    query_heads,
    key_heads,
    value_heads,
    grad_heads,
    mixture,
    query_pos,
    query_lab,
    begins,
    needed,
    highest,
    summed,
    scaling,
):
    row_delta = jnp.einsum("qhd,qhd->hq", grad_heads.astype(jnp.float32), mixture)

    def grad_step(block_index, loop_state):
        grad_query, grad_keys, grad_values = loop_state
        masked = block_scores(
            query_heads, key_heads, query_pos, query_lab, begins, block_index, scaling
        )
        prob_full = jnp.exp(masked - highest[:, :, None]) / summed[:, :, None]
        offset = block_index * KEYB
        value_block = lax.dynamic_slice_in_dim(value_heads, offset, KEYB, 0)
        grad_probs = jnp.einsum(
            "qhd,khd->hqk", grad_heads, value_block, preferred_element_type=jnp.float32
        )
        grad_scores = (prob_full * (grad_probs - row_delta[:, :, None])).astype(jnp.bfloat16)
        key_block = lax.dynamic_slice_in_dim(key_heads, offset, KEYB, 0)
        grad_query = (
            grad_query
            + jnp.einsum("hqk,khd->qhd", grad_scores, key_block, preferred_element_type=jnp.float32)
            * scaling
        )
        key_part = (
            jnp.einsum("hqk,qhd->khd", grad_scores, query_heads, preferred_element_type=jnp.float32)
            * scaling
        )
        value_part = jnp.einsum(
            "hqk,qhd->khd",
            prob_full.astype(jnp.bfloat16),
            grad_heads,
            preferred_element_type=jnp.float32,
        )
        grad_keys = lax.dynamic_update_slice_in_dim(
            grad_keys, lax.dynamic_slice_in_dim(grad_keys, offset, KEYB, 0) + key_part, offset, 0
        )
        grad_values = lax.dynamic_update_slice_in_dim(
            grad_values,
            lax.dynamic_slice_in_dim(grad_values, offset, KEYB, 0) + value_part,
            offset,
            0,
        )
        return (grad_query, grad_keys, grad_values)

    starting = (
        jnp.zeros(query_heads.shape, jnp.float32),
        jnp.zeros(key_heads.shape, jnp.float32),
        jnp.zeros(value_heads.shape, jnp.float32),
    )
    return lax.fori_loop(0, needed, grad_step, starting)


def general(
    tokens,
    cotangent,
    starts,
    w_qkv,
    b_query,
    b_value,
    w_out,
    b_out,
    gain_one,
    shift_one,
    gain_two,
    shift_two,
    w_expand,
    b_expand,
    w_shrink,
    b_shrink,
):
    (
        full_qkv,
        full_bq,
        full_bv,
        full_out,
        full_bo,
        full_gone,
        full_sone,
        full_gtwo,
        full_stwo,
        full_expand,
        full_bexp,
        full_shrink,
        full_bshr,
    ) = (
        lax.all_gather(w_qkv.astype(jnp.bfloat16), ("tok", "mdl"), axis=0, tiled=True),
        lax.all_gather(b_query.astype(jnp.bfloat16), ("tok", "mdl"), axis=0, tiled=True),
        lax.all_gather(b_value.astype(jnp.bfloat16), ("tok", "mdl"), axis=0, tiled=True),
        lax.all_gather(w_out.astype(jnp.bfloat16), ("tok", "mdl"), axis=0, tiled=True),
        lax.all_gather(b_out.astype(jnp.bfloat16), ("tok", "mdl"), axis=0, tiled=True),
        lax.all_gather(gain_one.astype(jnp.bfloat16), ("tok", "mdl"), axis=0, tiled=True),
        lax.all_gather(shift_one.astype(jnp.bfloat16), ("tok", "mdl"), axis=0, tiled=True),
        lax.all_gather(gain_two.astype(jnp.bfloat16), ("tok", "mdl"), axis=0, tiled=True),
        lax.all_gather(shift_two.astype(jnp.bfloat16), ("tok", "mdl"), axis=0, tiled=True),
        lax.all_gather(w_expand.astype(jnp.bfloat16), ("tok", "mdl"), axis=0, tiled=True),
        lax.all_gather(b_expand.astype(jnp.bfloat16), ("tok", "mdl"), axis=0, tiled=True),
        lax.all_gather(w_shrink.astype(jnp.bfloat16), ("tok", "mdl"), axis=0, tiled=True),
        lax.all_gather(b_shrink.astype(jnp.bfloat16), ("tok", "mdl"), axis=0, tiled=True),
    )
    query_bias = full_bq.astype(jnp.float32)
    value_bias = full_bv.astype(jnp.float32)
    out_bias = full_bo.astype(jnp.float32)
    gain_first = full_gone.astype(jnp.float32)
    shift_first = full_sone.astype(jnp.float32)
    gain_second = full_gtwo.astype(jnp.float32)
    shift_second = full_stwo.astype(jnp.float32)
    expand_bias = full_bexp.astype(jnp.float32)
    shrink_bias = full_bshr.astype(jnp.float32)
    local_rows = tokens.shape[1]
    model_width = tokens.shape[2]
    head_count = model_width // HD
    group_size = lax.axis_size("tok")
    member = lax.axis_index("tok")
    seq_len = local_rows * group_size
    scaling = HD ** (-0.5)
    needed = jnp.minimum(
        seq_len // KEYB, ((member + 1) * local_rows + PIECE - 1 + KEYB - 1) // KEYB
    )
    begins = starts[0]
    query_pos = member * local_rows + jnp.arange(local_rows, dtype=jnp.int32)
    query_lab = piece_ids(begins, query_pos)
    token_rows = tokens[0]
    cotangent_rows = cotangent[0]
    inputs = token_rows.astype(jnp.float32)
    normed = layer_norm(inputs, gain_first, shift_first).astype(jnp.bfloat16)
    joined = jnp.dot(normed, full_qkv, preferred_element_type=jnp.float32)
    queries = (joined[:, :model_width] + query_bias).astype(jnp.bfloat16)
    keys_own = joined[:, model_width : 2 * model_width].astype(jnp.bfloat16)
    values_own = (joined[:, 2 * model_width :] + value_bias).astype(jnp.bfloat16)
    key_full, value_full = (
        lax.all_gather(keys_own, "tok", axis=0, tiled=True),
        lax.all_gather(values_own, "tok", axis=0, tiled=True),
    )
    query_heads = queries.reshape(local_rows, head_count, HD)
    mixture, highest, summed = attend_forward(
        query_heads,
        key_full.reshape(seq_len, head_count, HD),
        value_full.reshape(seq_len, head_count, HD),
        query_pos,
        query_lab,
        begins,
        needed,
        scaling,
    )
    attention = mixture.reshape(local_rows, model_width).astype(jnp.bfloat16)
    hidden_one = inputs + (
        jnp.dot(attention, full_out, preferred_element_type=jnp.float32) + out_bias
    )
    normed_two = layer_norm(hidden_one, gain_second, shift_second).astype(jnp.bfloat16)
    expanded = jnp.dot(normed_two, full_expand, preferred_element_type=jnp.float32) + expand_bias
    activated = gelu_tanh(expanded).astype(jnp.bfloat16)
    layer_out = hidden_one + (
        jnp.dot(activated, full_shrink, preferred_element_type=jnp.float32) + shrink_bias
    )
    upstream = cotangent_rows.astype(jnp.float32)
    db_shrink = jnp.sum(upstream, axis=0)
    dw_shrink = jnp.einsum(
        "rf,rd->fd", activated, cotangent_rows, preferred_element_type=jnp.float32
    )
    grad_act = jnp.einsum(
        "rd,fd->rf", cotangent_rows, full_shrink, preferred_element_type=jnp.float32
    )
    gelu_pull = jax.vjp(gelu_tanh, expanded)[1]
    grad_expand = gelu_pull(grad_act)[0].astype(jnp.bfloat16)
    db_expand = jnp.sum(grad_expand.astype(jnp.float32), axis=0)
    dw_expand = jnp.einsum("rd,rf->df", normed_two, grad_expand, preferred_element_type=jnp.float32)
    grad_normed_two = jnp.einsum(
        "rf,df->rd", grad_expand, full_expand, preferred_element_type=jnp.float32
    )
    norm_pull = jax.vjp(layer_norm, hidden_one, gain_second, shift_second)[1]
    grad_hidden_part, dgain_two, dshift_two = norm_pull(grad_normed_two)
    grad_hidden = upstream + grad_hidden_part
    grad_attn = grad_hidden.astype(jnp.bfloat16)
    db_out = jnp.sum(grad_attn.astype(jnp.float32), axis=0)
    dw_out = jnp.einsum("rd,re->de", attention, grad_attn, preferred_element_type=jnp.float32)
    grad_mix = jnp.einsum(
        "re,de->rd", grad_attn, full_out, preferred_element_type=jnp.float32
    ).astype(jnp.bfloat16)
    key_back, value_back = (key_full, value_full)
    grad_query, grad_keys, grad_values = attend_backward(
        query_heads,
        key_back.reshape(seq_len, head_count, HD),
        value_back.reshape(seq_len, head_count, HD),
        grad_mix.reshape(local_rows, head_count, HD),
        mixture,
        query_pos,
        query_lab,
        begins,
        needed,
        highest,
        summed,
        scaling,
    )
    key_share, value_share = (
        lax.psum_scatter(
            grad_keys.reshape(seq_len, model_width).astype(jnp.bfloat16),
            "tok",
            scatter_dimension=0,
            tiled=True,
        ).astype(jnp.float32),
        lax.psum_scatter(
            grad_values.reshape(seq_len, model_width).astype(jnp.bfloat16),
            "tok",
            scatter_dimension=0,
            tiled=True,
        ).astype(jnp.float32),
    )
    grad_joined = jnp.concatenate(
        [
            grad_query.reshape(local_rows, model_width).astype(jnp.bfloat16),
            key_share.astype(jnp.bfloat16),
            value_share.astype(jnp.bfloat16),
        ],
        axis=1,
    )
    db_query = jnp.sum(grad_joined[:, :model_width].astype(jnp.float32), axis=0)
    db_value = jnp.sum(grad_joined[:, 2 * model_width :].astype(jnp.float32), axis=0)
    dw_qkv = jnp.einsum("rd,re->de", normed, grad_joined, preferred_element_type=jnp.float32)
    grad_normed = jnp.einsum("re,de->rd", grad_joined, full_qkv, preferred_element_type=jnp.float32)
    norm_pull_first = jax.vjp(layer_norm, inputs, gain_first, shift_first)[1]
    grad_input_part, dgain_one, dshift_one = norm_pull_first(grad_normed)
    dtokens = grad_hidden + grad_input_part
    (
        dw_qkv,
        db_query,
        db_value,
        dw_out,
        db_out,
        dgain_one,
        dshift_one,
        dgain_two,
        dshift_two,
        dw_expand,
        db_expand,
        dw_shrink,
        db_shrink,
    ) = (
        lax.psum_scatter(dw_qkv, ("tok", "mdl"), scatter_dimension=0, tiled=True),
        lax.psum_scatter(db_query, ("tok", "mdl"), scatter_dimension=0, tiled=True),
        lax.psum_scatter(db_value, ("tok", "mdl"), scatter_dimension=0, tiled=True),
        lax.psum_scatter(dw_out, ("tok", "mdl"), scatter_dimension=0, tiled=True),
        lax.psum_scatter(db_out, ("tok", "mdl"), scatter_dimension=0, tiled=True),
        lax.psum_scatter(dgain_one, ("tok", "mdl"), scatter_dimension=0, tiled=True),
        lax.psum_scatter(dshift_one, ("tok", "mdl"), scatter_dimension=0, tiled=True),
        lax.psum_scatter(dgain_two, ("tok", "mdl"), scatter_dimension=0, tiled=True),
        lax.psum_scatter(dshift_two, ("tok", "mdl"), scatter_dimension=0, tiled=True),
        lax.psum_scatter(dw_expand, ("tok", "mdl"), scatter_dimension=0, tiled=True),
        lax.psum_scatter(db_expand, ("tok", "mdl"), scatter_dimension=0, tiled=True),
        lax.psum_scatter(dw_shrink, ("tok", "mdl"), scatter_dimension=0, tiled=True),
        lax.psum_scatter(db_shrink, ("tok", "mdl"), scatter_dimension=0, tiled=True),
    )
    return (
        layer_out.astype(jnp.bfloat16).reshape(1, local_rows, model_width),
        dtokens.reshape(1, local_rows, model_width),
        dw_qkv,
        db_query,
        db_value,
        dw_out,
        db_out,
        dgain_one,
        dshift_one,
        dgain_two,
        dshift_two,
        dw_expand,
        db_expand,
        dw_shrink,
        db_shrink,
    )


BLK = 512
LOG_SCALE = math.log2(math.e) * HD ** (-0.5)
F32 = jnp.float32
BF = jnp.bfloat16


def nn(a, b):
    return lax.dot_general(a, b, (((1,), (0,)), ((), ())), preferred_element_type=F32)


def nt(a, b):
    return lax.dot_general(a, b, (((1,), (1,)), ((), ())), preferred_element_type=F32)


def diag_units(task):
    return [
        (2 * task, 0, "diag", 0, BLK, 0, BLK),
        (2 * task, 1, None, 0, BLK, 0, BLK),
        (2 * task + 1, 1, "diag", 0, BLK, 0, BLK),
        (2 * task + 1, 0, "piece", 0, PIECE, BLK - PIECE, PIECE),
    ]


def unit_mask(unit, task, begin):
    j, h, kind, k0, nk, q0, nq = unit
    keys = j * BLK + k0
    queries = (2 * task + h) * BLK + q0
    kc = keys + lax.broadcasted_iota(jnp.int32, (nk, 1), 0)
    qr = queries + lax.broadcasted_iota(jnp.int32, (1, nq), 1)
    kin = ((kc >= begin) & (kc < begin + PIECE)).astype(F32)
    qin = ((qr >= begin) & (qr < begin + PIECE)).astype(F32)
    both = (kin * qin) > 0.5
    if kind == "piece":
        return both
    return (kc <= qr) | both


def forward_units(slot, task, units, begin, xv, kn, acc, ms, ls):
    def score(unit):
        j, h, kind, k0, nk, q0, nq = unit
        s = nn(kn[slot, j, k0 : k0 + nk, :], xv[slot, 2 * task + h, 0, :, q0 : q0 + nq]) * LOG_SCALE
        if kind:
            s = jnp.where(unit_mask(unit, task, begin), s, masked_score)
        return s

    ahead = score(units[0])
    for n, unit in enumerate(units):
        j, h, kind, k0, nk, q0, nq = unit
        now = ahead
        if n + 1 < len(units):
            ahead = score(units[n + 1])
        qs = slice(q0, q0 + nq)
        high = jnp.maximum(ms[h, :, qs], jnp.max(now, axis=0, keepdims=True))
        fade = jnp.exp2(ms[h, :, qs] - high)
        p = jnp.exp2(now - high)
        ls[h, :, qs] = ls[h, :, qs] * fade + jnp.sum(p, axis=0, keepdims=True)
        ms[h, :, qs] = high
        acc[h, :, qs] = acc[h, :, qs] * fade + nn(xv[slot, j, 2, :, k0 : k0 + nk], p.astype(BF))


def forward_task(slot, task, begin, xv, kn, acc, ms, ls):
    ms[...] = jnp.full_like(ms, masked_score)
    ls[...] = jnp.zeros_like(ls)
    acc[...] = jnp.zeros_like(acc)

    def step(j, carry):
        forward_units(
            slot, task, [(j, h, None, 0, BLK, 0, BLK) for h in range(2)], begin, xv, kn, acc, ms, ls
        )
        return carry

    lax.fori_loop(0, 2 * task, step, 0)
    forward_units(slot, task, diag_units(task), begin, xv, kn, acc, ms, ls)


def backward_units(slot, task, row, key, units, begin, xv, gv, kn, vn, lsum, delta, dkv, dq):
    def score(unit):
        j, h, kind, k0, nk, q0, nq = unit
        b = 2 * task + h
        s = nn(kn[slot, j, k0 : k0 + nk, :], xv[slot, b, 0, :, q0 : q0 + nq]) * LOG_SCALE
        return s, nn(vn[slot, j, k0 : k0 + nk, :], gv[slot, b, :, q0 : q0 + nq])

    ahead = score(units[0])
    for n, unit in enumerate(units):
        j, h, kind, k0, nk, q0, nq = unit
        b = 2 * task + h
        s, dp = ahead
        if n + 1 < len(units):
            ahead = score(units[n + 1])
        p = jnp.exp2(s - lsum[slot, b, :, q0 : q0 + nq])
        if kind:
            p = jnp.where(unit_mask(unit, task, begin), p, 0.0)
        ds = (p * (dp - delta[slot, b, :, q0 : q0 + nq])).astype(BF)
        dkv[key + j, 1, :, k0 : k0 + nk] += nt(gv[slot, b, :, q0 : q0 + nq], p.astype(BF))
        dkv[key + j, 0, :, k0 : k0 + nk] += nt(xv[slot, b, 0, :, q0 : q0 + nq], ds)
        dq[row + h, :, q0 : q0 + nq] += nn(xv[slot, j, 1, :, k0 : k0 + nk], ds)


MESH_ID = pl.DeviceIdType.MESH
ANYS = pl.BlockSpec(memory_space=pl.ANY)
VMEMS = pl.BlockSpec(memory_space=pltpu.VMEM)
SMEMS = pl.BlockSpec(memory_space=pltpu.SMEM)
DMA = pltpu.SemaphoreType.DMA


def place():
    t = lax.axis_index("tok")
    m = lax.axis_index("mdl")
    return t, m, t // 2, t % 2, m // 2, m % 2


def greet(peers):
    barrier = pltpu.get_barrier_semaphore()
    for peer in peers:
        pl.semaphore_signal(barrier, inc=1, device_id=peer, device_id_type=MESH_ID)
    return lambda: pl.semaphore_wait(barrier, len(peers))


def meet(peers):
    greet(peers)()


def chip_group(t, m):
    return [(t ^ k, m ^ b) for k in range(8) for b in range(2) if (k, b) != (0, 0)]


def column_group(t, m):
    return [(t ^ 2, m), (t ^ 4, m), (t ^ 6, m), (t ^ 1, m), (t, m ^ 2), (t, m ^ 1)]


def remote(src, dst, ssem, rsem, dev):
    return pltpu.make_async_remote_copy(
        src_ref=src, dst_ref=dst, send_sem=ssem, recv_sem=rsem, device_id=dev, device_id_type=MESH_ID
    )


def landed(ref, sem):
    pltpu.make_async_copy(ref, ref, sem).wait()


def send_unless(here, src, dst, ssem, rsem, dev):
    @pl.when(here)
    def _():
        pltpu.make_async_copy(src, dst, rsem).start()

    @pl.when(jnp.logical_not(here))
    def _():
        remote(src, dst, ssem, rsem, dev).start()


def sent_unless(here, src, dst, ssem, rsem, dev):
    @pl.when(jnp.logical_not(here))
    def _():
        remote(src, dst, ssem, rsem, dev).wait_send()


class Pushes:
    def __init__(self, outs, send, recv):
        self.outs, self.send, self.recv, self.started = outs, send, recv, []

    def push(self, shard, dev, src=None):
        e = len(self.started)
        todo = []
        for a, out in enumerate(self.outs):
            cp = remote(
                out.at[shard] if src is None else src[a],
                out.at[shard],
                self.send.at[e, a],
                self.recv.at[a, shard],
                dev,
            )
            cp.start()
            todo.append(cp)
        self.started.append(todo)

    def arrived(self, shard):
        for a, out in enumerate(self.outs):
            landed(out.at[shard], self.recv.at[a, shard])

    def finish(self):
        for todo in self.started:
            for cp in todo:
                cp.wait_send()


class Line:
    def __init__(self, outs, send, recv, fan, beside):
        self.outs, self.send, self.recv, self.fan, self.beside = outs, send, recv, fan, beside
        self.t, self.m = lax.axis_index("tok"), lax.axis_index("mdl")
        self.z = self.t // 2
        self.chips = lax.axis_size("tok") // 2

    def ways(self, hop):
        up = (0, (self.z >= hop) & (self.z < self.chips - 1), self.t - 2 * hop, self.t + 2)
        down = (1, (self.z + hop < self.chips) & (self.z > 0), self.t + 2 * hop, self.t - 2)
        return up, down

    def copies(self, hop, way, shard, to, src=None):
        at = 4 * shard + self.m
        return [
            remote(
                out.at[at] if src is None else src[a],
                out.at[at],
                self.send.at[2 * hop + way, a],
                self.recv.at[a, at],
                (to, self.m),
            )
            for a, out in enumerate(self.outs)
        ]

    def comes(self, hop, way):
        return (self.z >= hop) if way == 0 else (self.z + hop < self.chips)

    def aside(self, hop, way, shard):
        at = 4 * shard + self.m
        return [
            remote(out.at[at], out.at[at], self.fan.at[6 * (hop - 1) + 3 * way + d, a], self.recv.at[a, at], dev)
            for d, dev in enumerate(self.beside)
            for a, out in enumerate(self.outs)
        ]

    def own(self, src):
        for way, there, shard, to in self.ways(0):

            @pl.when(there)
            def _():
                for cp in self.copies(0, way, shard, to, src):
                    cp.start()

    def hop(self, hop):
        for way, there, shard, to in self.ways(hop):
            @pl.when(self.comes(hop, way))
            def _():
                at = 4 * shard + self.m
                for a, out in enumerate(self.outs):
                    landed(out.at[at], self.recv.at[a, at])
                for cp in self.aside(hop, way, shard):
                    cp.start()

            if hop < self.chips - 1:

                @pl.when(there)
                def _():
                    for cp in self.copies(hop, way, shard, to):
                        cp.start()

    def finish(self, src):
        for hop in range(self.chips - 1):
            for way, there, shard, to in self.ways(hop):

                @pl.when(there)
                def _():
                    for cp in self.copies(hop, way, shard, to, src if hop == 0 else None):
                        cp.wait_send()
        for hop in range(1, self.chips):
            for way, there, shard, to in self.ways(hop):

                @pl.when(self.comes(hop, way))
                def _():
                    for cp in self.aside(hop, way, shard):
                        cp.wait_send()


def in_parts(shape, body):
    rows, width = shape
    if rows % 24 or width % 768:
        body((slice(None), slice(None)))
        return
    across = width // 768

    def step(i, carry):
        r = pl.multiple_of(i // across * 24, 8)
        c = pl.multiple_of(i % across * 768, 128)
        body((pl.ds(r, 24), pl.ds(c, 768)))
        return carry

    lax.fori_loop(0, rows // 24 * across, step, 0)


class Sums:
    def __init__(self, ins, acc, r1, rx, ry, rd, s1, v1, ss, vx, vy, vd, own=None):
        self.own = own
        self.t, self.m = lax.axis_index("tok"), lax.axis_index("mdl")
        self.ins, self.acc, self.r1, self.rx, self.ry, self.rd = ins, acc, r1, rx, ry, rd
        self.s1, self.v1, self.ss, self.vx, self.vy, self.vd = s1, v1, ss, vx, vy, vd
        self.count = len(ins)
        self.started = []

    def owner(self, n):
        return self.t ^ (2 * (n // 4) + (n // 2) % 2), self.m ^ (2 * (n % 2))

    def first(self, n, a):
        tt, mm = self.owner(n)
        return remote(
            self.ins[a].at[4 * tt + (mm ^ 1)], self.r1[a].at[n], self.s1.at[n, a], self.v1.at[n, a], (self.t, self.m ^ 1)
        )

    def begin(self, which=None):
        for n in (15, 11, 14, 10, 7, 3, 5, 1, 6, 2, 13, 9, 12, 8, 4, 0):
            for a in range(self.count) if which is None else which:
                self.first(n, a).start()
                if self.own is not None:
                    tt, mm = self.owner(n)
                    pltpu.make_async_copy(self.ins[a].at[4 * tt + mm], self.acc[a].at[n], self.own.at[n, a]).start()

    def hop(self, e, n, dst, slot, vsem, by_x):
        dev = (self.t ^ 1, self.m) if by_x else (self.t, self.m ^ 2)
        return [
            remote(self.acc[a].at[n], dst[a].at[slot], self.ss.at[e, a], vsem.at[slot, a], dev)
            for a in range(self.count)
        ]

    def push(self, *what):
        e = len(self.started)
        self.started.append(what)
        for cp in self.hop(e, *what):
            cp.start()

    def total(self, n, a, more, store):
        tt, mm = self.owner(n)
        self.first(n, a).wait_recv()
        if self.own is not None:
            landed(self.acc[a].at[n], self.own.at[n, a])
        for buf, slot, vsem in more:
            landed(buf[a].at[slot], vsem.at[slot, a])

        def add_part(part):
            out = self.acc[a][(n,) + part] if self.own is not None else self.ins[a][(4 * tt + mm,) + part]
            out = out.astype(F32) + self.r1[a][(n,) + part].astype(F32)
            for buf, slot, vsem in more:
                out = out + buf[a][(slot,) + part].astype(F32)
            store(part, out)

        in_parts(self.acc[a].shape[1:], add_part)

    def add(self, n, more=()):
        for a in range(self.count):
            self.add_one(n, a, more)

    def add_one(self, n, a, more):
        def store(part, out):
            self.acc[a][(n,) + part] = out.astype(self.acc[a].dtype)

        self.total(n, a, more, store)

    def early(self, by_y):
        for k in (3, 2, 1, 0):
            self.add(4 * k + 3)
            self.push(4 * k + 3, self.rd, k, self.vd, k >= by_y)
        for k in (3, 2, 1, 0):
            if k >= by_y:
                self.add(4 * k + 2)
                self.push(4 * k + 2, self.rx, k, self.vx, True)
            else:
                self.add(4 * k + 1)
                self.push(4 * k + 1, self.ry, k, self.vy, False)

    def late(self, by_y):
        for k in (3, 2, 1, 0):
            via = [(self.rd, k, self.vd)]
            if k < by_y:
                self.add(4 * k + 2, via)
                self.push(4 * k + 2, self.rx, k, self.vx, True)
            else:
                self.add(4 * k + 1, via)
                self.push(4 * k + 1, self.ry, k, self.vy, False)

    def column(self, k, a, more=()):
        self.add_one(4 * k, a, [(self.rx, k, self.vx), (self.ry, k, self.vy)] + list(more))

    def column_out(self, a, out):
        def store(part, total):
            out[part] = total

        self.total(0, a, [(self.rx, 0, self.vx), (self.ry, 0, self.vy)], store)

    def finish(self):
        for n in range(16):
            for a in range(self.count):
                self.first(n, a).wait_send()
        for e, what in enumerate(self.started):
            for cp in self.hop(e, *what):
                cp.wait_send()


def sums_scratch(shards, outside):
    n = len(shards)
    bufs = [pltpu.VMEM((k,) + s, d) for k in (16, 16, 4, 4, 4) for s, d in shards]
    sems = [DMA((16, n)), DMA((16, n)), DMA((12, n)), DMA((4, n)), DMA((4, n)), DMA((4, n))]
    return bufs + sems + ([DMA((16, n))] if outside else [])


def take_sums(ins, refs, outside):
    n = len(ins)
    bufs = [refs[i * n : (i + 1) * n] for i in range(5)]
    end = 5 * n + 6 + outside
    return Sums(ins, *bufs, *refs[5 * n : end]), refs[end:]


SMALL_ROWS = 16


def side_by_side(smalls, width):
    step = width // 32
    lane = lax.broadcasted_iota(jnp.int32, (128, width), 0)
    col = lax.broadcasted_iota(jnp.int32, (128, width), 1)
    pick = (lax.rem(col, step) == lane).astype(BF)
    every = lax.dot_general(
        smalls.reshape(32 * SMALL_ROWS, 128).astype(BF), pick, (((1,), (0,)), ((), ())), preferred_element_type=F32
    )
    shard = lax.broadcasted_iota(jnp.int32, (32, SMALL_ROWS, width), 0)
    at = lax.broadcasted_iota(jnp.int32, (32, SMALL_ROWS, width), 2) // step
    return jnp.sum(jnp.where(shard == at, every.reshape(32, SMALL_ROWS, width), 0.0), axis=0)


def attend_kernel(*refs):
    (tokens_ref, starts_ref), masters, vectors = refs[:2], refs[2:6], refs[6:15]
    full_qkv, smalls_out, weights, (heads, of_ref, l_ref, att, begins) = refs[15], refs[16], refs[17:20], refs[20:25]
    (low_qkv, low0, low1, low2, small, smalls, wq, normed, jv, xv, kn, acc, ms, ls, stage) = refs[25:40]
    (s1, v1, local, s_full, r_full, s_sh, r_sh, s_fw, r_fw, s_out, r_out, keep, send, recv, send_z, fan) = refs[40:]
    t, m, z, x, y, c = place()
    xn, yn, sib = (t ^ 1, m), (t, m ^ 2), (t, m ^ 1)
    own = x == c
    role = (x + c) % 2
    hf, hs, owner_m = 3 * z + 2 * x, 3 * z + 1, 2 * y + x
    lows = (low0, low1, low2)
    me = 4 * t + m
    step = low_qkv.shape[0]
    width = 32 * step

    met = greet(chip_group(t, m) + [yn])
    low_qkv[...] = masters[0][...].astype(BF)
    small[...] = jnp.zeros_like(small)
    for v in range(8):
        small[v : v + 1, 0:step] = vectors[v][...].astype(BF).astype(F32)
    for q in range(4):
        small[8 + q : 9 + q, 0:step] = vectors[8][:, q * step : (q + 1) * step].astype(BF).astype(F32)
    small[12:13, 0 : starts_ref.shape[1]] = starts_ref[...].astype(F32)
    smalls[me] = small[...]
    met()

    class Shards:
        def __init__(self, ref):
            self.at = self
            self.ref = ref

        def __getitem__(self, shard):
            return self.ref.at[pl.ds(pl.multiple_of(step * shard, 8), step)]

    first = Pushes((Shards(full_qkv), smalls), s1, v1)
    for dev in [(t ^ 2, m), (t ^ 4, m), (t ^ 6, m), xn, yn, sib]:
        first.push(me, dev, (low_qkv, small))
    work = Pushes(weights, send, recv)
    for low, master in zip(lows, masters[1:]):
        low[...] = master[...].astype(BF)
    column = Line(weights, send_z, recv, fan, (xn, yn, sib))
    own_rows = [pltpu.make_async_copy(low_qkv, Shards(full_qkv)[me], local.at[0])]
    own_rows += [pltpu.make_async_copy(lows[a], weights[a].at[me], local.at[1 + a]) for a in range(3)]
    for cp in own_rows:
        cp.start()

    values = tokens_ref[...].astype(F32)
    center = values - jnp.mean(values, axis=-1, keepdims=True)
    spread = jnp.mean(center * center, axis=-1, keepdims=True)
    xhat = center * lax.rsqrt(spread + epsilon)

    for k in range(1, 4):
        shard = 4 * (t ^ (2 * k)) + m
        first.arrived(shard)
        for dev in (xn, yn, sib):
            first.push(shard, dev)
    column.own(lows)
    for k in range(4):
        col = t ^ (2 * k)
        xi, yi = 4 * (col ^ 1) + m, 4 * col + (m ^ 2)
        first.arrived(xi)
        if k < 2:
            first.push(xi, yn)
        first.push(xi, sib)
        first.arrived(yi)
        if k >= 2:
            first.push(yi, xn)
        first.push(yi, sib)
    for dev in (xn, yn, sib):
        work.push(me, dev, lows)
    column.hop(1)
    for k in range(4):
        di = 4 * (t ^ (2 * k) ^ 1) + (m ^ 2)
        first.arrived(di)
        first.push(di, sib)
    for k in range(4):
        for a in (0, 1):
            for b in (0, 2):
                first.arrived(4 * (t ^ (2 * k) ^ a) + (m ^ b ^ 1))
    column.hop(2)
    for cp in own_rows:
        cp.wait()
    load = pltpu.make_async_copy(full_qkv, wq, local.at[4])
    load.start()
    share = pltpu.make_async_copy(smalls, smalls_out, local.at[5])
    share.start()
    flat = side_by_side(smalls[...], width)
    normed[...] = (xhat * flat[3:4] + flat[4:5]).astype(BF)
    bias = jnp.concatenate([flat[0:1], jnp.zeros_like(flat[0:1]), flat[1:2]], axis=1)
    begins[0] = smalls[m, 12:13, :].astype(jnp.int32)
    begins[1] = smalls[owner_m, 12:13, :].astype(jnp.int32)
    load.wait()
    for n in range(9):
        part = slice(n * 256, (n + 1) * 256)
        block = lax.dot_general(
            normed[...], wq[:, part], (((1,), (0,)), ((), ())), preferred_element_type=F32
        )
        block = (block + bias[:, part]).T.astype(BF)
        for h in range(4):
            g = 4 * n + h
            jv[g // 12, g % 12] = block[h * HD : (h + 1) * HD]

    def full(k):
        d = t ^ k
        return jv.at[:, 3 * (d // 2) + 2 * (d % 2)], xv.at[0, t], s_full.at[k], r_full.at[t], (d, m)

    def shared(k):
        zd = z ^ k
        return jv.at[:, 3 * zd + 1], xv.at[1, t], s_sh.at[k], r_sh.at[t], (2 * zd + c, m)

    for k in (4, 5, 6, 7, 2, 3, 1):
        remote(*full(k)).start()
    loc = full(0)
    pltpu.make_async_copy(loc[0], loc[1], loc[3]).start()
    column.hop(3)
    for k in range(1, 8):
        remote(*full(k)).wait_send()
    for k in (2, 3, 1):
        remote(*shared(k)).start()
    send_unless(own, *shared(0))

    def keep_head(slot):
        cp = pltpu.make_async_copy(xv.at[slot], heads.at[slot], keep.at[slot])
        cp.start()
        return cp

    for b in range(8):
        landed(xv.at[0, b], r_full.at[b])
    kept = [keep_head(0)]
    for b in range(8):
        kn[0, b] = xv[0, b, 1].T

    def begin_of(slot, task):
        lane = lax.broadcasted_iota(jnp.int32, (1, 128), 1)
        return jnp.sum(jnp.where(lane == task, begins[slot], 0), axis=1, keepdims=True)

    def finish_task(slot, task, row, head, mdl, alone):
        for h in range(2):
            b, u = 2 * task + h, 2 * row + h
            out = acc[h] / ls[h]
            of_ref[u] = out
            stage[u] = out.astype(BF)
            l_ref[u] = ms[h] + jnp.log2(ls[h])
            send_unless((b == t) & alone, stage.at[u], att.at[head], s_out.at[u], r_out.at[head], (b, mdl))

    def full_task(w, carry):
        forward_task(0, w, begin_of(0, w), xv, kn, acc, ms, ls)
        finish_task(0, w, w, hf, m, t >= 0)
        return carry

    lax.fori_loop(0, 3, full_task, 0)

    for k in range(4):
        col = t ^ (2 * k)
        xi, yi = 4 * (col ^ 1) + m, 4 * col + (m ^ 2)
        work.arrived(xi)
        if k < 3:
            work.push(xi, yn)
        work.push(xi, sib)
        work.arrived(yi)
        if k == 3:
            work.push(yi, xn)
        work.push(yi, sib)

    def forward(k):
        b = t ^ k
        return remote(xv.at[1, b], xv.at[1, b], s_fw.at[k], r_fw.at[b], sib)

    @pl.when(own)
    def _():
        for k in (0, 1, 2, 3, 6, 7, 4, 5):
            landed(xv.at[1, t ^ k], r_sh.at[t ^ k])
            forward(k).start()

    lax.fori_loop(3, 4, full_task, 0)

    @pl.when(jnp.logical_not(own))
    def _():
        for k in range(8):
            forward(k).wait_recv()

    kept.append(keep_head(1))
    for b in range(8):
        kn[1, b] = xv[1, b, 1].T

    def shared_task(n, carry):
        task = jnp.where(n == 0, role, 3 - role)
        forward_task(1, task, begin_of(1, task), xv, kn, acc, ms, ls)
        finish_task(1, task, 4 + n, hs, owner_m, own)
        return carry

    lax.fori_loop(0, 2, shared_task, 0)

    for k in range(4):
        di = 4 * (t ^ (2 * k) ^ 1) + (m ^ 2)
        work.arrived(di)
        work.push(di, sib)
    for h in range(12):
        landed(att.at[h], r_out.at[h])
    for k in range(4):
        for a in (0, 1):
            for b in (0, 2):
                work.arrived(4 * (t ^ (2 * k) ^ a) + (m ^ b ^ 1))
    first.finish()
    work.finish()
    column.finish(lows)
    for k in (1, 2, 3):
        remote(*shared(k)).wait_send()
    sent_unless(own, *shared(0))

    @pl.when(own)
    def _():
        for k in range(8):
            forward(k).wait_send()

    for w in range(4):
        for h in range(2):
            b, u = 2 * w + h, 2 * w + h
            sent_unless(b == t, stage.at[u], att.at[hf], s_out.at[u], r_out.at[hf], (b, m))
    for n in range(2):
        task = role if n == 0 else 3 - role
        for h in range(2):
            b, u = 2 * task + h, 8 + 2 * n + h
            sent_unless((b == t) & own, stage.at[u], att.at[hs], s_out.at[u], r_out.at[hs], (b, owner_m))
    for cp in kept:
        cp.wait()
    share.wait()


def attend(tokens, starts, masters, vectors, cid):
    rows, width = tokens.shape
    step = width // 32
    head = (HD, BLK)
    S, V = jax.ShapeDtypeStruct, pltpu.VMEM
    outs = pl.pallas_call(
        attend_kernel,
        out_shape=(S((width, 3 * width), BF), S((32, SMALL_ROWS, 128), F32))
        + tuple(S((32,) + w.shape, BF) for w in masters[1:])
        + (S((2, 8, 3) + head, BF), S((12,) + head, F32), S((12, 1, BLK), F32), S((12,) + head, BF), S((2, 1, 128), jnp.int32)),
        in_specs=[VMEMS] * 15,
        out_specs=(ANYS,) * 6 + (VMEMS, VMEMS, ANYS, VMEMS),
        scratch_shapes=[V(w.shape, BF) for w in masters]
        + [
            V((SMALL_ROWS, 128), F32),
            V((32, SMALL_ROWS, 128), F32),
            V((width, 3 * width), BF),
            V((rows, width), BF),
            V((3, 12) + head, BF),
            V((2, 8, 3) + head, BF),
            V((2, 8, BLK, HD), BF),
            V((2,) + head, F32),
            V((2, 1, BLK), F32),
            V((2, 1, BLK), F32),
            V((12,) + head, BF),
        ]
        + [DMA((31, 2)), DMA((2, 32)), DMA((6,))]
        + [DMA((8,)), DMA((8,)), DMA((4,)), DMA((8,)), DMA((8,)), DMA((8,)), DMA((12,)), DMA((12,)), DMA((2,))]
        + [DMA((19, 3)), DMA((3, 32)), DMA((6, 3)), DMA((18, 3))],
        name="attend",
        compiler_params=pltpu.CompilerParams(collective_id=cid, has_side_effects=True, vmem_limit_bytes=62 << 20),
    )(tokens, starts, *masters, *vectors)
    return outs[0], outs[1], outs[2:5], outs[5:]


FF_BLOCK = 512
HBMS = pl.BlockSpec(memory_space=pltpu.HBM)


def shard_rows(rows, step):
    r, n = rows.shape
    count = n // step
    shard = lax.broadcasted_iota(jnp.int32, (count, r, n), 0)
    at = lax.broadcasted_iota(jnp.int32, (count, r, n), 2) // step
    spread = jnp.where(shard == at, rows[None], 0.0).reshape(count * r, n)
    col = lax.broadcasted_iota(jnp.int32, (n, 128), 0)
    lane = lax.broadcasted_iota(jnp.int32, (n, 128), 1)
    pick = (lax.rem(col, step) == lane).astype(F32)
    out = lax.dot_general(
        spread, pick, (((1,), (0,)), ((), ())), precision=lax.Precision.HIGHEST, preferred_element_type=F32
    )
    return out.reshape(count, r, 128)


def expand_row(smalls, hidden):
    step = hidden // 128
    lane = lax.broadcasted_iota(jnp.int32, (128, hidden), 0)
    col = lax.broadcasted_iota(jnp.int32, (128, hidden), 1)
    pick = (lax.rem(col, step) == lane).astype(BF)
    every = nn(smalls[:, 8:12, :].reshape(128, 128).astype(BF), pick)
    return jnp.sum(jnp.where(lane == col // step, every, 0.0), axis=0, keepdims=True)


def middle_kernel(
    x_ref, c_ref, att_any, smalls_any, wo_any, we_ref, ws_ref,
    out_ref, gh_ref, gm_any, dwo_any, dwe_ref, dws_ref, flat, vec_ref, dbe_ref,
    be, hidden, xhat, inv, n2, n2t, out_acc, dn2, att_ref, smalls_ref, wo_ref, gm_ref, dwo_ref, sems,
):
    i = pl.program_id(0)
    last = pl.num_programs(0) - 1
    width = x_ref.shape[1]

    @pl.when(i == 0)
    def _():
        pairs = ((smalls_any, smalls_ref), (att_any, att_ref), (wo_any, wo_ref))
        loads = [pltpu.make_async_copy(a, b, sems.at[n]) for n, (a, b) in enumerate(pairs)]
        for cp in loads:
            cp.start()
        loads[0].wait()
        flat[...] = side_by_side(smalls_ref[...], width)
        row = expand_row(smalls_ref[...], be.shape[0] * FF_BLOCK)
        for n in range(be.shape[0]):
            be[n] = row[:, n * FF_BLOCK : (n + 1) * FF_BLOCK]
        loads[1].wait()
        loads[2].wait()
        branch = nn(att_ref[...].T, wo_ref[...]) + flat[2:3]
        h = x_ref[...].astype(F32) + branch
        hidden[...] = h
        center = h - jnp.mean(h, axis=-1, keepdims=True)
        scale = lax.rsqrt(jnp.mean(center * center, axis=-1, keepdims=True) + epsilon)
        inv[...] = scale
        xhat[...] = center * scale
        low = (xhat[...] * flat[5:6] + flat[6:7]).astype(BF)
        n2[...] = low
        n2t[...] = low.T
        out_acc[...] = jnp.zeros_like(out_acc)
        dn2[...] = jnp.zeros_like(dn2)

    u = nn(n2[...], we_ref[...]) + be[i]
    square = u * u
    th = jnp.tanh(gelu_coeff * (u + 0.044715 * square * u))
    half = 0.5 * (1.0 + th)
    act = (u * half).astype(BF)
    slope = half + 0.5 * u * (1.0 - th * th) * (gelu_coeff * (1.0 + 3.0 * 0.044715 * square))
    out_acc[...] += nn(act, ws_ref[...])
    ge = nt(c_ref[...], ws_ref[...]) * slope
    ge = ge.astype(BF)
    dbe_ref[...] = jnp.sum(ge.astype(F32), axis=0, keepdims=True)
    dws_ref[...] = nn(act.T, c_ref[...]).astype(BF)
    dwe_ref[...] = nn(n2t[...], ge).astype(BF)
    dn2[...] += nt(ge, we_ref[...])

    @pl.when(i == last)
    def _():
        out_ref[...] = (hidden[...] + (out_acc[...] + flat[7:8])).astype(BF)
        up = c_ref[...].astype(F32)
        e = dn2[...]
        f = e * flat[5:6]
        xh = xhat[...]
        dv = f - jnp.mean(f, axis=-1, keepdims=True) - xh * jnp.mean(f * xh, axis=-1, keepdims=True)
        gh = up + dv * inv[...]
        gh_ref[...] = gh
        ga = gh.astype(BF)
        gm_ref[...] = nt(wo_ref[...], ga).astype(BF)
        saves = [pltpu.make_async_copy(gm_ref, gm_any, sems.at[3])]
        saves[0].start()
        dwo_ref[...] = nn(att_ref[...], ga).astype(BF)
        saves.append(pltpu.make_async_copy(dwo_ref, dwo_any, sems.at[4]))
        saves[1].start()
        vec_ref[0:1] = jnp.sum(ga.astype(F32), axis=0, keepdims=True)
        vec_ref[1:2] = jnp.sum(e * xh, axis=0, keepdims=True)
        vec_ref[2:3] = jnp.sum(e, axis=0, keepdims=True)
        vec_ref[3:4] = jnp.sum(up, axis=0, keepdims=True)
        vec_ref[4:8] = jnp.zeros((4, width), F32)
        for cp in saves:
            cp.wait()


def middle(x, c, att, smalls, wo, we, ws):
    rows, width = x.shape
    hidden = we.shape[1]
    S, V = jax.ShapeDtypeStruct, pltpu.VMEM
    n = hidden // FF_BLOCK
    across = pl.BlockSpec((width, FF_BLOCK), lambda i: (0, i))
    down = pl.BlockSpec((FF_BLOCK, width), lambda i: (i, 0))
    whole = lambda a: pl.BlockSpec(a.shape, lambda i: (0,) * len(a.shape), pipeline_mode=pl.Buffered(1))
    outs = (
        S((rows, width), BF),
        S((rows, width), F32),
        S((width, rows), BF),
        S((width, width), BF),
        S((width, hidden), BF),
        S((hidden, width), BF),
        S((SMALL_ROWS, width), F32),
        S((8, width), F32),
        S((1, hidden), F32),
    )
    return pl.pallas_call(
        middle_kernel,
        grid=(n,),
        out_shape=outs,
        in_specs=[whole(x), whole(c), HBMS, HBMS, HBMS, across, down],
        out_specs=(whole(outs[0]), whole(outs[1]), HBMS, HBMS)
        + (across, down, whole(outs[6]), whole(outs[7]), pl.BlockSpec((1, FF_BLOCK), lambda i: (0, i))),
        scratch_shapes=[
            V((n, 1, FF_BLOCK), F32),
            V((rows, width), F32),
            V((rows, width), F32),
            V((rows, 1), F32),
            V((rows, width), BF),
            V((width, rows), BF),
            V((rows, width), F32),
            V((rows, width), F32),
            V(att.shape, BF),
            V(smalls.shape, F32),
            V(wo.shape, BF),
            V((width, rows), BF),
            V((width, width), BF),
            DMA((5,)),
        ],
        name="middle",
        compiler_params=pltpu.CompilerParams(vmem_limit_bytes=62 << 20),
    )(x, c, att, smalls, wo, we, ws)


def attend_back_kernel(*refs):
    g_ref, heads_ref, of_ref, l_ref, tokens_ref, begins, flat_ref, vec_ref, bias_ref, wq_ref = refs[:10]
    ins, dx_ref, last_outs, outs = refs[10:13], refs[13], refs[14:16], refs[16:19]
    work, rest = take_sums(ins, refs[19:], True)
    dwq, small, dwkv, gj, wq, normed_t, rzp = rest[0], rest[1], rest[2], rest[3], rest[4], rest[5], rest[6:9]
    tail, rest = take_sums((dwq, small), rest[9:], False)
    rz, rest = rest[:2], rest[2:]
    tail_kv, rest = take_sums((dwkv,), rest, False)
    rzk, rest = rest[:1], rest[1:]
    (xv, gv, kn, vn, dkv, dq, lsum, delta, stage, stage_kv, got, stage_sh, ofv, dxv) = rest[:14]
    (s_full, r_full, s_sh, r_sh, s_fw, r_fw, s_q, r_q, s_kv, r_kv, s_shkv, s_part, r_part) = rest[14:27]
    szp, vzp, sz, vz, szk, vzk, local = rest[27:]
    count = len(ins)
    t, m, z, x, y, c = place()
    sib = (t, m ^ 1)
    met = greet(chip_group(t, m) + [(t, m ^ 2)])
    def load_of(first):
        return pltpu.make_async_copy(of_ref.at[pl.ds(first, 4)], ofv, local.at[5])

    loads = [pltpu.make_async_copy(heads_ref.at[s, :, 2], stage_kv.at[:, s], local.at[s]) for s in range(2)]
    loads += [pltpu.make_async_copy(heads_ref.at[s, :, pl.ds(0, 2)], xv.at[s], local.at[2 + s]) for s in range(2)]
    load_of(8).start()
    for cp in loads:
        cp.start()
    met()
    own = x == c
    role = (x + c) % 2
    hf, hs, owner_m = 3 * z + 2 * x, 3 * z + 1, 2 * y + x
    order = (4, 5, 6, 7, 2, 3, 1)

    def full(k):
        d = t ^ k
        return g_ref.at[3 * (d // 2) + 2 * (d % 2)], gv.at[0, t], s_full.at[k], r_full.at[t], (d, m)

    def shared(k):
        zd = z ^ k
        return g_ref.at[3 * zd + 1], gv.at[1, t], s_sh.at[k], r_sh.at[t], (2 * zd + c, m)

    for k in (2, 3, 1):
        remote(*shared(k)).start()
    send_unless(own, *shared(0))
    loc = full(0)
    pltpu.make_async_copy(loc[0], loc[1], loc[3]).start()
    work.begin()
    for cp in loads:
        cp.wait()
    for s in range(2):
        for b in range(8):
            kn[s, b] = xv[s, b, 1].T
            vn[s, b] = stage_kv[b, s].T
    dkv[...] = jnp.zeros_like(dkv)
    dq[...] = jnp.zeros_like(dq)
    for k in (1, 2, 3):
        remote(*shared(k)).wait_send()
    sent_unless(own, *shared(0))
    for k in order:
        remote(*full(k)).start()

    def forward(k):
        b = t ^ k
        return remote(gv.at[1, b], gv.at[1, b], s_fw.at[k], r_fw.at[b], sib)

    @pl.when(own)
    def _():
        for k in (0, 1, 2, 3, 6, 7, 4, 5):
            landed(gv.at[1, t ^ k], r_sh.at[t ^ k])
            forward(k).start()

    work.early(4)

    @pl.when(jnp.logical_not(own))
    def _():
        for k in range(8):
            forward(k).wait_recv()

    def begin_of(slot, task):
        lane = lax.broadcasted_iota(jnp.int32, (1, 128), 1)
        return jnp.sum(jnp.where(lane == task, begins[slot], 0), axis=1, keepdims=True)

    def ready(slot, b, u):
        lsum[slot, b] = l_ref[u]
        delta[slot, b] = jnp.sum(gv[slot, b].astype(F32) * ofv[u % 4], axis=0, keepdims=True)

    def out_q(slot, b, u):
        stage[u] = (dq[u] * HD ** (-0.5)).astype(BF)
        if slot:
            send_unless((b == t) & own, stage.at[u], gj.at[0, hs], s_q.at[u], r_q.at[hs], (b, owner_m))
        else:
            send_unless(b == t, stage.at[u], gj.at[0, hf], s_q.at[u], r_q.at[hf], (b, m))

    args = (xv, gv, kn, vn, lsum, delta, dkv, dq)

    def shared_task(n, carry):
        task = jnp.where(n == 0, role, 3 - role)
        begin = begin_of(1, task)

        def step(j, carry):
            backward_units(1, task, 8 + 2 * n, 0, [(j, h, None, 0, BLK, 0, BLK) for h in range(2)], begin, *args)
            return carry

        lax.fori_loop(0, 2 * task, step, 0)
        backward_units(1, task, 8 + 2 * n, 0, diag_units(task), begin, *args)
        for h in range(2):
            out_q(1, 2 * task + h, 8 + 2 * n + h)
        return carry

    load_of(8).wait()
    for n in range(2):
        task = role if n == 0 else 3 - role
        for h in range(2):
            ready(1, 2 * task + h, 8 + 2 * n + h)
    load_of(0).start()
    lax.fori_loop(0, 2, shared_task, 0)

    def part(k):
        b = t ^ k
        return remote(dkv.at[b], got.at[b], s_part.at[k], r_part.at[b], sib)

    def shared_kv(k):
        b = t ^ k
        return stage_sh.at[b], gj.at[pl.ds(1, 2), hs], s_shkv.at[k], r_kv.at[hs], (b, m)

    @pl.when(jnp.logical_not(own))
    def _():
        for k in order + (0,):
            part(k).start()

    for b in range(8):
        landed(gv.at[0, b], r_full.at[b])
    load_of(0).wait()
    for b in range(4):
        ready(0, b, b)
    load_of(4).start()
    load_of(4).wait()
    for b in range(4, 8):
        ready(0, b, b)

    @pl.when(own)
    def _():
        for k in order + (0,):
            b = t ^ k
            part(k).wait_recv()
            stage_sh[b, 0] = ((dkv[b, 0] + got[b, 0]) * HD ** (-0.5)).astype(BF)
            stage_sh[b, 1] = (dkv[b, 1] + got[b, 1]).astype(BF)
            a = shared_kv(k)
            if k:
                remote(*a).start()
            else:
                pltpu.make_async_copy(a[0], a[1], a[3]).start()

    def full_keys(s, carry):
        keys = z ^ (3 - s)
        dkv[8:10] = jnp.zeros((2,) + dkv.shape[1:], F32)
        backward_units(0, keys, 2 * keys, 8 - 2 * keys, diag_units(keys), begin_of(0, keys), *args)

        def step(n, carry):
            task, j = n // 2, 2 * keys + n % 2
            units = [(j, h, None, 0, BLK, 0, BLK) for h in range(2)]
            backward_units(0, task, 2 * task, 8 - 2 * keys, units, 0, *args)
            return carry

        lax.fori_loop(2 * keys + 2, 8, step, 0)
        for i in range(2):
            b = 2 * keys + i
            stage_kv[b, 0] = (dkv[8 + i, 0] * HD ** (-0.5)).astype(BF)
            stage_kv[b, 1] = dkv[8 + i, 1].astype(BF)
            send_unless(b == t, stage_kv.at[b], gj.at[pl.ds(1, 2), hf], s_kv.at[b], r_kv.at[hf], (b, m))

        @pl.when(s == jnp.where(z == 0, 1, 0))
        def _():
            work.late(4)

        return carry

    lax.fori_loop(0, 4, full_keys, 0)
    for b in range(8):
        out_q(0, b, b)
    along = []

    def z_push(sums, k, a, buf, slot, ssem, vsem, to, more=()):
        sums.column(k, a, more)
        cp = remote(sums.acc[a].at[4 * k], buf[a].at[slot], ssem.at[slot, a], vsem.at[slot, a], (t ^ (2 * to), m))
        cp.start()
        along.append(cp)

    width = tokens_ref.shape[1]
    step = width // 32
    gain, shift = flat_ref[3:4], flat_ref[4:5]

    def norm(half):
        values = tokens_ref[half].astype(F32)
        center = values - jnp.mean(values, axis=-1, keepdims=True)
        inv = lax.rsqrt(jnp.mean(center * center, axis=-1, keepdims=True) + epsilon)
        return center * inv, inv

    load = pltpu.make_async_copy(wq_ref, wq, local.at[4])
    load.start()
    halves = [slice(n * 256, (n + 1) * 256) for n in range(tokens_ref.shape[0] // 256)]
    for half in halves:
        normed_t[:, half] = (norm(half)[0] * gain + shift).astype(BF).T

    for a in range(count):
        z_push(work, 3, a, rzp, 1, szp, vzp, 1)
        z_push(work, 1, a, rzp, 0, szp, vzp, 1)

    def weight_grads(first, last, out):
        for n in range(first, last):
            grads = gj[n // 3, 4 * (n % 3) : 4 * (n % 3) + 4].reshape(256, BLK)
            block = nt(normed_t[...], grads).reshape(32, step, 256)
            out[:, :, (n - first) * 256 : (n - first + 1) * 256] = block.astype(BF)

    for h in range(12):
        landed(gj.at[pl.ds(1, 2), h], r_kv.at[h])
    weight_grads(3, 9, dwkv)
    tail_kv.begin()
    for h in range(12):
        landed(gj.at[0, h], r_q.at[h])
    weight_grads(0, 3, dwq)
    tail.begin([0])
    load.wait()
    tail_kv.early(2)
    for a in range(count):
        z_push(work, 2, a, rzp, 2, szp, vzp, 2, [(rzp, 1, vzp)])
    dgain, dshift = jnp.zeros((1, width), F32), jnp.zeros((1, width), F32)
    for half in halves:
        e = jnp.zeros((width, 256), F32)
        for n in range(9):
            grads = gj[n // 3, 4 * (n % 3) : 4 * (n % 3) + 4, :, half].reshape(256, 256)
            e = e + nn(wq[:, n * 256 : (n + 1) * 256], grads)
        e = e.T
        xhat, inv = norm(half)
        f = e * gain
        dv = f - jnp.mean(f, axis=-1, keepdims=True) - xhat * jnp.mean(f * xhat, axis=-1, keepdims=True)
        if half.start:
            out_x.wait()
        dxv[...] = dv * inv
        out_x = pltpu.make_async_copy(dxv, dx_ref.at[half], local.at[6])
        out_x.start()
        dgain = dgain + jnp.sum(e * xhat, axis=0, keepdims=True)
        dshift = dshift + jnp.sum(e, axis=0, keepdims=True)
    ones = jnp.ones((8, BLK), BF)
    db_query = nt(ones, gj[0].reshape(width, BLK))[0:1]
    db_value = nt(ones, gj[2].reshape(width, BLK))[0:1]
    rows = [db_query, db_value, vec_ref[0:1], dgain, dshift, vec_ref[1:4]]
    small[:, 0:8] = shard_rows(jnp.concatenate(rows, axis=0), step)
    small[:, 8:12] = bias_ref[...]
    small[:, 12:16] = jnp.zeros((32, 4, 128), F32)
    tail.begin([1])
    tail_kv.late(2)
    tail.early(2)
    for k in (3, 2, 1):
        z_push(tail_kv, k, 0, rzk, k - 1, szk, vzk, k)
    tail.late(2)
    for k in (3, 2, 1):
        for a in range(2):
            z_push(tail, k, a, rz, k - 1, sz, vz, k)

    def gather_z(a, out, buf, slots, vsem):
        for n in slots:
            landed(buf.at[n], vsem.at[n, a])

        def add_part(part):
            total = out[part]
            for n in slots:
                total = total + buf[(n,) + part].astype(F32)
            out[part] = total

        in_parts(out.shape, add_part)

    for a in range(count):
        work.column_out(a, outs[a])
        gather_z(a, outs[a], rzp[a], (0, 2), vzp)
    ends = last_outs[0].at[:, pl.ds(0, width)], last_outs[1]
    end_kv = last_outs[0].at[:, pl.ds(width, 2 * width)]
    tail_kv.column_out(0, end_kv)
    gather_z(0, end_kv, rzk[0], (0, 1, 2), vzk)
    for a in range(2):
        tail.column_out(a, ends[a])
        gather_z(a, ends[a], rz[a], (0, 1, 2), vz)
    out_x.wait()
    tail.finish()
    tail_kv.finish()
    for cp in along:
        cp.wait_send()
    work.finish()
    for k in range(1, 8):
        remote(*full(k)).wait_send()
    for b in range(8):
        sent_unless(b == t, stage.at[b], gj.at[0, hf], s_q.at[b], r_q.at[hf], (b, m))
        sent_unless(b == t, stage_kv.at[b], gj.at[pl.ds(1, 2), hf], s_kv.at[b], r_kv.at[hf], (b, m))
    for n in range(2):
        task = role if n == 0 else 3 - role
        for h in range(2):
            b, u = 2 * task + h, 8 + 2 * n + h
            sent_unless((b == t) & own, stage.at[u], gj.at[0, hs], s_q.at[u], r_q.at[hs], (b, owner_m))

    @pl.when(own)
    def _():
        for k in range(8):
            forward(k).wait_send()
        for k in range(1, 8):
            remote(*shared_kv(k)).wait_send()

    @pl.when(jnp.logical_not(own))
    def _():
        for k in range(8):
            part(k).wait_send()


def attend_back(grad_mix, heads, out_full, log_sum, tokens, begins, flat, vec, bias, full_qkv, grads, cid):
    n = len(grads)
    rows, width = tokens.shape
    head = (HD, BLK)
    S, V = jax.ShapeDtypeStruct, pltpu.VMEM
    shards = [(g.shape[1:], BF) for g in grads]
    last = [((width // 32, width), BF), ((SMALL_ROWS, 128), F32)]
    keyed = [((width // 32, 2 * width), BF)]
    ends = [(width // 32, 3 * width), (SMALL_ROWS, 128)] + [s for s, d in shards]
    return pl.pallas_call(
        attend_back_kernel,
        out_shape=(S((rows, width), F32),) + tuple(S(s, F32) for s in ends),
        in_specs=[ANYS] * 3 + [VMEMS] * 6 + [ANYS] + [ANYS] * n,
        out_specs=(ANYS,) + (VMEMS,) * (2 + n),
        scratch_shapes=sums_scratch(shards, True)
        + [V((32,) + s, d) for s, d in last + keyed]
        + [V((3, 12) + head, BF), V((width, 3 * width), BF), V((width, rows), BF)]
        + [V((3,) + s, d) for s, d in shards]
        + sums_scratch(last, False)
        + [V((3,) + s, d) for s, d in last]
        + sums_scratch(keyed, False)
        + [V((3,) + s, d) for s, d in keyed]
        + [
            V((2, 8, 2) + head, BF),
            V((2, 8) + head, BF),
            V((2, 8, BLK, HD), BF),
            V((2, 8, BLK, HD), BF),
            V((10, 2) + head, F32),
            V((12,) + head, F32),
            V((2, 8, 1, BLK), F32),
            V((2, 8, 1, BLK), F32),
            V((12,) + head, BF),
            V((8, 2) + head, BF),
            V((8, 2) + head, F32),
            V((8, 2) + head, BF),
            V((4,) + head, F32),
            V((256, width), F32),
        ]
        + [DMA((8,)), DMA((8,)), DMA((4,)), DMA((8,)), DMA((8,)), DMA((8,)), DMA((12,)), DMA((12,))]
        + [DMA((8,)), DMA((12,)), DMA((8,)), DMA((8,)), DMA((8,))]
        + [DMA((4, n)), DMA((4, n)), DMA((4, 2)), DMA((4, 2)), DMA((4, 1)), DMA((4, 1)), DMA((7,))],
        name="attend_back",
        compiler_params=pltpu.CompilerParams(collective_id=cid, has_side_effects=True, vmem_limit_bytes=62 << 20),
    )(grad_mix, heads, out_full, log_sum, tokens, begins, flat, vec, bias, full_qkv, *grads)


def by_heads(
    tokens,
    cotangent,
    starts,
    w_qkv,
    b_query,
    b_value,
    w_out,
    b_out,
    gain_one,
    shift_one,
    gain_two,
    shift_two,
    w_expand,
    b_expand,
    w_shrink,
    b_shrink,
):
    rows, width = tokens.shape[1:]
    hidden = b_expand.shape[0] * 32
    vectors = [b_query, b_value, b_out, gain_one, shift_one, gain_two, shift_two, b_shrink, b_expand]
    full_qkv, smalls, rest, (heads, out_full, log_sum, attention, begins) = attend(
        tokens[0], starts, [w_qkv, w_out, w_expand, w_shrink], [v.reshape(1, -1) for v in vectors], 1
    )
    full_out, full_expand, full_shrink = (w.reshape(-1, w.shape[-1]) for w in rest)
    attention = attention.reshape(width, rows)
    step = width // 32
    layer_out, grad_hidden, grad_mix, dw_out, dw_expand, dw_shrink, flat, sums, db_expand = middle(
        tokens[0], cotangent[0], attention, smalls, full_out, full_expand, full_shrink
    )
    bias = jnp.pad(db_expand.reshape(32, 4, step), [(0, 0), (0, 0), (0, 128 - step)])
    shards = lambda w: w.reshape((32, -1) + w.shape[1:])
    dtokens, dw_qkv, smalls, dw_out, dw_expand, dw_shrink = attend_back(
        grad_mix.reshape(12, HD, rows),
        heads,
        out_full,
        log_sum,
        tokens[0],
        begins,
        flat,
        sums,
        bias,
        full_qkv,
        [shards(dw_out), shards(dw_expand), shards(dw_shrink)],
        2,
    )
    step = width // 32
    vecs = [smalls[i, :step] for i in range(8)]
    db_query, db_value, db_out, dgain_one, dshift_one, dgain_two, dshift_two, db_shrink = vecs
    db_expand = smalls[8:12, :step].reshape(-1)
    return (
        layer_out.reshape(1, rows, width),
        (grad_hidden + dtokens).reshape(1, rows, width),
        dw_qkv,
        db_query,
        db_value,
        dw_out,
        db_out,
        dgain_one,
        dshift_one,
        dgain_two,
        dshift_two,
        dw_expand,
        db_expand,
        dw_shrink,
        db_shrink,
    )


def solution(mesh):
    rows, vector, seq = P(("tok", "mdl"), None), P(("tok", "mdl")), P("mdl", "tok", None)
    by_name = dict(m=rows, v=vector, s=seq)
    fits = mesh.shape["tok"] == 8 and mesh.shape["mdl"] == 4
    return jax.shard_map(
        by_heads if fits else general,
        mesh=mesh,
        in_specs=(seq, seq, P("mdl", None)) + tuple(by_name[k] for k in "mvvmvvvvvmvmv"),
        out_specs=tuple(by_name[k] for k in "ssmvvmvvvvvmvmv"),
        check_vma=False,
    )
```

```python
import functools
import math

import jax
import jax.numpy as jnp
from jax import lax
from jax.experimental import pallas as pl
from jax.experimental.pallas import tpu as pltpu
from jax.sharding import PartitionSpec as P

HD = 64
PIECE = 256
KEYB = 512


epsilon = 1e-05
masked_score = -1e30
gelu_coeff = 0.7978845608028654


def layer_norm(values, gain_vec, shift_vec):
    center = values - jnp.mean(values, axis=-1, keepdims=True)
    spread = jnp.mean(center * center, axis=-1, keepdims=True)
    return center * lax.rsqrt(spread + epsilon) * gain_vec + shift_vec


def gelu_tanh(inputs):
    return (
        0.5 * inputs * (1.0 + jnp.tanh(gelu_coeff * (inputs + 0.044715 * inputs * inputs * inputs)))
    )


def piece_ids(begins, positions):
    inside = (positions[:, None] >= begins[None, :]) & (
        positions[:, None] < begins[None, :] + PIECE
    )
    labels = jnp.arange(1, begins.shape[0] + 1, dtype=jnp.int32)
    return jnp.sum(jnp.where(inside, labels[None, :], 0), axis=1) - 1


def block_scores(query_heads, key_heads, query_pos, query_lab, begins, block_index, scaling):
    key_block = lax.dynamic_slice_in_dim(key_heads, block_index * KEYB, KEYB, 0)
    key_pos = block_index * KEYB + jnp.arange(KEYB, dtype=jnp.int32)
    key_lab = piece_ids(begins, key_pos)
    scores = (
        jnp.einsum("qhd,khd->hqk", query_heads, key_block, preferred_element_type=jnp.float32)
        * scaling
    )
    allowed = (key_pos[None, :] <= query_pos[:, None]) | (
        key_lab[None, :] == query_lab[:, None]
    ) & (query_lab[:, None] >= 0)
    return jnp.where(allowed[None, :, :], scores, masked_score)


def attend_forward(
    query_heads, key_heads, value_heads, query_pos, query_lab, begins, needed, scaling
):
    local_rows = query_heads.shape[0]
    head_count = query_heads.shape[1]

    def stats_step(block_index, loop_state):
        highest, summed = loop_state
        masked = block_scores(
            query_heads, key_heads, query_pos, query_lab, begins, block_index, scaling
        )
        new_high = jnp.maximum(highest, jnp.max(masked, axis=-1))
        summed = summed * jnp.exp(highest - new_high) + jnp.sum(
            jnp.exp(masked - new_high[:, :, None]), axis=-1
        )
        return (new_high, summed)

    starting = (
        jnp.full((head_count, local_rows), masked_score, jnp.float32),
        jnp.zeros((head_count, local_rows), jnp.float32),
    )
    highest, summed = lax.fori_loop(0, needed, stats_step, starting)

    def mix_step(block_index, running):
        masked = block_scores(
            query_heads, key_heads, query_pos, query_lab, begins, block_index, scaling
        )
        prob_low = (jnp.exp(masked - highest[:, :, None]) / summed[:, :, None]).astype(jnp.bfloat16)
        value_block = lax.dynamic_slice_in_dim(value_heads, block_index * KEYB, KEYB, 0)
        return running + jnp.einsum(
            "hqk,khd->qhd", prob_low, value_block, preferred_element_type=jnp.float32
        )

    mixture = lax.fori_loop(0, needed, mix_step, jnp.zeros(query_heads.shape, jnp.float32))
    return (mixture, highest, summed)


def attend_backward(
    query_heads,
    key_heads,
    value_heads,
    grad_heads,
    mixture,
    query_pos,
    query_lab,
    begins,
    needed,
    highest,
    summed,
    scaling,
):
    row_delta = jnp.einsum("qhd,qhd->hq", grad_heads.astype(jnp.float32), mixture)

    def grad_step(block_index, loop_state):
        grad_query, grad_keys, grad_values = loop_state
        masked = block_scores(
            query_heads, key_heads, query_pos, query_lab, begins, block_index, scaling
        )
        prob_full = jnp.exp(masked - highest[:, :, None]) / summed[:, :, None]
        offset = block_index * KEYB
        value_block = lax.dynamic_slice_in_dim(value_heads, offset, KEYB, 0)
        grad_probs = jnp.einsum(
            "qhd,khd->hqk", grad_heads, value_block, preferred_element_type=jnp.float32
        )
        grad_scores = (prob_full * (grad_probs - row_delta[:, :, None])).astype(jnp.bfloat16)
        key_block = lax.dynamic_slice_in_dim(key_heads, offset, KEYB, 0)
        grad_query = (
            grad_query
            + jnp.einsum("hqk,khd->qhd", grad_scores, key_block, preferred_element_type=jnp.float32)
            * scaling
        )
        key_part = (
            jnp.einsum("hqk,qhd->khd", grad_scores, query_heads, preferred_element_type=jnp.float32)
            * scaling
        )
        value_part = jnp.einsum(
            "hqk,qhd->khd",
            prob_full.astype(jnp.bfloat16),
            grad_heads,
            preferred_element_type=jnp.float32,
        )
        grad_keys = lax.dynamic_update_slice_in_dim(
            grad_keys, lax.dynamic_slice_in_dim(grad_keys, offset, KEYB, 0) + key_part, offset, 0
        )
        grad_values = lax.dynamic_update_slice_in_dim(
            grad_values,
            lax.dynamic_slice_in_dim(grad_values, offset, KEYB, 0) + value_part,
            offset,
            0,
        )
        return (grad_query, grad_keys, grad_values)

    starting = (
        jnp.zeros(query_heads.shape, jnp.float32),
        jnp.zeros(key_heads.shape, jnp.float32),
        jnp.zeros(value_heads.shape, jnp.float32),
    )
    return lax.fori_loop(0, needed, grad_step, starting)


def general(
    tokens,
    cotangent,
    starts,
    w_qkv,
    b_query,
    b_value,
    w_out,
    b_out,
    gain_one,
    shift_one,
    gain_two,
    shift_two,
    w_expand,
    b_expand,
    w_shrink,
    b_shrink,
):
    (
        full_qkv,
        full_bq,
        full_bv,
        full_out,
        full_bo,
        full_gone,
        full_sone,
        full_gtwo,
        full_stwo,
        full_expand,
        full_bexp,
        full_shrink,
        full_bshr,
    ) = (
        lax.all_gather(w_qkv.astype(jnp.bfloat16), ("tok", "mdl"), axis=0, tiled=True),
        lax.all_gather(b_query.astype(jnp.bfloat16), ("tok", "mdl"), axis=0, tiled=True),
        lax.all_gather(b_value.astype(jnp.bfloat16), ("tok", "mdl"), axis=0, tiled=True),
        lax.all_gather(w_out.astype(jnp.bfloat16), ("tok", "mdl"), axis=0, tiled=True),
        lax.all_gather(b_out.astype(jnp.bfloat16), ("tok", "mdl"), axis=0, tiled=True),
        lax.all_gather(gain_one.astype(jnp.bfloat16), ("tok", "mdl"), axis=0, tiled=True),
        lax.all_gather(shift_one.astype(jnp.bfloat16), ("tok", "mdl"), axis=0, tiled=True),
        lax.all_gather(gain_two.astype(jnp.bfloat16), ("tok", "mdl"), axis=0, tiled=True),
        lax.all_gather(shift_two.astype(jnp.bfloat16), ("tok", "mdl"), axis=0, tiled=True),
        lax.all_gather(w_expand.astype(jnp.bfloat16), ("tok", "mdl"), axis=0, tiled=True),
        lax.all_gather(b_expand.astype(jnp.bfloat16), ("tok", "mdl"), axis=0, tiled=True),
        lax.all_gather(w_shrink.astype(jnp.bfloat16), ("tok", "mdl"), axis=0, tiled=True),
        lax.all_gather(b_shrink.astype(jnp.bfloat16), ("tok", "mdl"), axis=0, tiled=True),
    )
    query_bias = full_bq.astype(jnp.float32)
    value_bias = full_bv.astype(jnp.float32)
    out_bias = full_bo.astype(jnp.float32)
    gain_first = full_gone.astype(jnp.float32)
    shift_first = full_sone.astype(jnp.float32)
    gain_second = full_gtwo.astype(jnp.float32)
    shift_second = full_stwo.astype(jnp.float32)
    expand_bias = full_bexp.astype(jnp.float32)
    shrink_bias = full_bshr.astype(jnp.float32)
    local_rows = tokens.shape[1]
    model_width = tokens.shape[2]
    head_count = model_width // HD
    group_size = lax.axis_size("tok")
    member = lax.axis_index("tok")
    seq_len = local_rows * group_size
    scaling = HD ** (-0.5)
    needed = jnp.minimum(
        seq_len // KEYB, ((member + 1) * local_rows + PIECE - 1 + KEYB - 1) // KEYB
    )
    begins = starts[0]
    query_pos = member * local_rows + jnp.arange(local_rows, dtype=jnp.int32)
    query_lab = piece_ids(begins, query_pos)
    token_rows = tokens[0]
    cotangent_rows = cotangent[0]
    inputs = token_rows.astype(jnp.float32)
    normed = layer_norm(inputs, gain_first, shift_first).astype(jnp.bfloat16)
    joined = jnp.dot(normed, full_qkv, preferred_element_type=jnp.float32)
    queries = (joined[:, :model_width] + query_bias).astype(jnp.bfloat16)
    keys_own = joined[:, model_width : 2 * model_width].astype(jnp.bfloat16)
    values_own = (joined[:, 2 * model_width :] + value_bias).astype(jnp.bfloat16)
    key_full, value_full = (
        lax.all_gather(keys_own, "tok", axis=0, tiled=True),
        lax.all_gather(values_own, "tok", axis=0, tiled=True),
    )
    query_heads = queries.reshape(local_rows, head_count, HD)
    mixture, highest, summed = attend_forward(
        query_heads,
        key_full.reshape(seq_len, head_count, HD),
        value_full.reshape(seq_len, head_count, HD),
        query_pos,
        query_lab,
        begins,
        needed,
        scaling,
    )
    attention = mixture.reshape(local_rows, model_width).astype(jnp.bfloat16)
    hidden_one = inputs + (
        jnp.dot(attention, full_out, preferred_element_type=jnp.float32) + out_bias
    )
    normed_two = layer_norm(hidden_one, gain_second, shift_second).astype(jnp.bfloat16)
    expanded = jnp.dot(normed_two, full_expand, preferred_element_type=jnp.float32) + expand_bias
    activated = gelu_tanh(expanded).astype(jnp.bfloat16)
    layer_out = hidden_one + (
        jnp.dot(activated, full_shrink, preferred_element_type=jnp.float32) + shrink_bias
    )
    upstream = cotangent_rows.astype(jnp.float32)
    db_shrink = jnp.sum(upstream, axis=0)
    dw_shrink = jnp.einsum(
        "rf,rd->fd", activated, cotangent_rows, preferred_element_type=jnp.float32
    )
    grad_act = jnp.einsum(
        "rd,fd->rf", cotangent_rows, full_shrink, preferred_element_type=jnp.float32
    )
    gelu_pull = jax.vjp(gelu_tanh, expanded)[1]
    grad_expand = gelu_pull(grad_act)[0].astype(jnp.bfloat16)
    db_expand = jnp.sum(grad_expand.astype(jnp.float32), axis=0)
    dw_expand = jnp.einsum("rd,rf->df", normed_two, grad_expand, preferred_element_type=jnp.float32)
    grad_normed_two = jnp.einsum(
        "rf,df->rd", grad_expand, full_expand, preferred_element_type=jnp.float32
    )
    norm_pull = jax.vjp(layer_norm, hidden_one, gain_second, shift_second)[1]
    grad_hidden_part, dgain_two, dshift_two = norm_pull(grad_normed_two)
    grad_hidden = upstream + grad_hidden_part
    grad_attn = grad_hidden.astype(jnp.bfloat16)
    db_out = jnp.sum(grad_attn.astype(jnp.float32), axis=0)
    dw_out = jnp.einsum("rd,re->de", attention, grad_attn, preferred_element_type=jnp.float32)
    grad_mix = jnp.einsum(
        "re,de->rd", grad_attn, full_out, preferred_element_type=jnp.float32
    ).astype(jnp.bfloat16)
    key_back, value_back = (key_full, value_full)
    grad_query, grad_keys, grad_values = attend_backward(
        query_heads,
        key_back.reshape(seq_len, head_count, HD),
        value_back.reshape(seq_len, head_count, HD),
        grad_mix.reshape(local_rows, head_count, HD),
        mixture,
        query_pos,
        query_lab,
        begins,
        needed,
        highest,
        summed,
        scaling,
    )
    key_share, value_share = (
        lax.psum_scatter(
            grad_keys.reshape(seq_len, model_width).astype(jnp.bfloat16),
            "tok",
            scatter_dimension=0,
            tiled=True,
        ).astype(jnp.float32),
        lax.psum_scatter(
            grad_values.reshape(seq_len, model_width).astype(jnp.bfloat16),
            "tok",
            scatter_dimension=0,
            tiled=True,
        ).astype(jnp.float32),
    )
    grad_joined = jnp.concatenate(
        [
            grad_query.reshape(local_rows, model_width).astype(jnp.bfloat16),
            key_share.astype(jnp.bfloat16),
            value_share.astype(jnp.bfloat16),
        ],
        axis=1,
    )
    db_query = jnp.sum(grad_joined[:, :model_width].astype(jnp.float32), axis=0)
    db_value = jnp.sum(grad_joined[:, 2 * model_width :].astype(jnp.float32), axis=0)
    dw_qkv = jnp.einsum("rd,re->de", normed, grad_joined, preferred_element_type=jnp.float32)
    grad_normed = jnp.einsum("re,de->rd", grad_joined, full_qkv, preferred_element_type=jnp.float32)
    norm_pull_first = jax.vjp(layer_norm, inputs, gain_first, shift_first)[1]
    grad_input_part, dgain_one, dshift_one = norm_pull_first(grad_normed)
    dtokens = grad_hidden + grad_input_part
    (
        dw_qkv,
        db_query,
        db_value,
        dw_out,
        db_out,
        dgain_one,
        dshift_one,
        dgain_two,
        dshift_two,
        dw_expand,
        db_expand,
        dw_shrink,
        db_shrink,
    ) = (
        lax.psum_scatter(dw_qkv, ("tok", "mdl"), scatter_dimension=0, tiled=True),
        lax.psum_scatter(db_query, ("tok", "mdl"), scatter_dimension=0, tiled=True),
        lax.psum_scatter(db_value, ("tok", "mdl"), scatter_dimension=0, tiled=True),
        lax.psum_scatter(dw_out, ("tok", "mdl"), scatter_dimension=0, tiled=True),
        lax.psum_scatter(db_out, ("tok", "mdl"), scatter_dimension=0, tiled=True),
        lax.psum_scatter(dgain_one, ("tok", "mdl"), scatter_dimension=0, tiled=True),
        lax.psum_scatter(dshift_one, ("tok", "mdl"), scatter_dimension=0, tiled=True),
        lax.psum_scatter(dgain_two, ("tok", "mdl"), scatter_dimension=0, tiled=True),
        lax.psum_scatter(dshift_two, ("tok", "mdl"), scatter_dimension=0, tiled=True),
        lax.psum_scatter(dw_expand, ("tok", "mdl"), scatter_dimension=0, tiled=True),
        lax.psum_scatter(db_expand, ("tok", "mdl"), scatter_dimension=0, tiled=True),
        lax.psum_scatter(dw_shrink, ("tok", "mdl"), scatter_dimension=0, tiled=True),
        lax.psum_scatter(db_shrink, ("tok", "mdl"), scatter_dimension=0, tiled=True),
    )
    return (
        layer_out.astype(jnp.bfloat16).reshape(1, local_rows, model_width),
        dtokens.reshape(1, local_rows, model_width),
        dw_qkv,
        db_query,
        db_value,
        dw_out,
        db_out,
        dgain_one,
        dshift_one,
        dgain_two,
        dshift_two,
        dw_expand,
        db_expand,
        dw_shrink,
        db_shrink,
    )


BLK = 512
LOG_SCALE = math.log2(math.e) * HD ** (-0.5)
F32 = jnp.float32
BF = jnp.bfloat16


def nn(a, b):
    return lax.dot_general(a, b, (((1,), (0,)), ((), ())), preferred_element_type=F32)


def nt(a, b):
    return lax.dot_general(a, b, (((1,), (1,)), ((), ())), preferred_element_type=F32)


def diag_units(task):
    return [
        (2 * task, 0, "diag", 0, BLK, 0, BLK),
        (2 * task, 1, None, 0, BLK, 0, BLK),
        (2 * task + 1, 1, "diag", 0, BLK, 0, BLK),
        (2 * task + 1, 0, "piece", 0, PIECE, BLK - PIECE, PIECE),
    ]


def unit_mask(unit, task, begin):
    j, h, kind, k0, nk, q0, nq = unit
    keys = j * BLK + k0
    queries = (2 * task + h) * BLK + q0
    kc = keys + lax.broadcasted_iota(jnp.int32, (nk, 1), 0)
    qr = queries + lax.broadcasted_iota(jnp.int32, (1, nq), 1)
    kin = ((kc >= begin) & (kc < begin + PIECE)).astype(F32)
    qin = ((qr >= begin) & (qr < begin + PIECE)).astype(F32)
    both = (kin * qin) > 0.5
    if kind == "piece":
        return both
    return (kc <= qr) | both


def forward_units(slot, task, units, begin, xv, kn, acc, ms, ls):
    def score(unit):
        j, h, kind, k0, nk, q0, nq = unit
        s = nn(kn[slot, j, k0 : k0 + nk, :], xv[slot, 2 * task + h, 0, :, q0 : q0 + nq]) * LOG_SCALE
        if kind:
            s = jnp.where(unit_mask(unit, task, begin), s, masked_score)
        return s

    ahead = score(units[0])
    for n, unit in enumerate(units):
        j, h, kind, k0, nk, q0, nq = unit
        now = ahead
        if n + 1 < len(units):
            ahead = score(units[n + 1])
        qs = slice(q0, q0 + nq)
        high = jnp.maximum(ms[h, :, qs], jnp.max(now, axis=0, keepdims=True))
        fade = jnp.exp2(ms[h, :, qs] - high)
        p = jnp.exp2(now - high)
        ls[h, :, qs] = ls[h, :, qs] * fade + jnp.sum(p, axis=0, keepdims=True)
        ms[h, :, qs] = high
        acc[h, :, qs] = acc[h, :, qs] * fade + nn(xv[slot, j, 2, :, k0 : k0 + nk], p.astype(BF))


def forward_task(slot, task, begin, xv, kn, acc, ms, ls):
    ms[...] = jnp.full_like(ms, masked_score)
    ls[...] = jnp.zeros_like(ls)
    acc[...] = jnp.zeros_like(acc)

    def step(j, carry):
        forward_units(
            slot, task, [(j, h, None, 0, BLK, 0, BLK) for h in range(2)], begin, xv, kn, acc, ms, ls
        )
        return carry

    lax.fori_loop(0, 2 * task, step, 0)
    forward_units(slot, task, diag_units(task), begin, xv, kn, acc, ms, ls)


def backward_units(slot, task, row, key, units, begin, xv, gv, kn, vn, lsum, delta, dkv, dq):
    def score(unit):
        j, h, kind, k0, nk, q0, nq = unit
        b = 2 * task + h
        s = nn(kn[slot, j, k0 : k0 + nk, :], xv[slot, b, 0, :, q0 : q0 + nq]) * LOG_SCALE
        return s, nn(vn[slot, j, k0 : k0 + nk, :], gv[slot, b, :, q0 : q0 + nq])

    ahead = score(units[0])
    for n, unit in enumerate(units):
        j, h, kind, k0, nk, q0, nq = unit
        b = 2 * task + h
        s, dp = ahead
        if n + 1 < len(units):
            ahead = score(units[n + 1])
        p = jnp.exp2(s - lsum[slot, b, :, q0 : q0 + nq])
        if kind:
            p = jnp.where(unit_mask(unit, task, begin), p, 0.0)
        ds = (p * (dp - delta[slot, b, :, q0 : q0 + nq])).astype(BF)
        dkv[key + j, 1, :, k0 : k0 + nk] += nt(gv[slot, b, :, q0 : q0 + nq], p.astype(BF))
        dkv[key + j, 0, :, k0 : k0 + nk] += nt(xv[slot, b, 0, :, q0 : q0 + nq], ds)
        dq[row + h, :, q0 : q0 + nq] += nn(xv[slot, j, 1, :, k0 : k0 + nk], ds)


MESH_ID = pl.DeviceIdType.MESH
ANYS = pl.BlockSpec(memory_space=pl.ANY)
VMEMS = pl.BlockSpec(memory_space=pltpu.VMEM)
SMEMS = pl.BlockSpec(memory_space=pltpu.SMEM)
DMA = pltpu.SemaphoreType.DMA


def place():
    t = lax.axis_index("tok")
    m = lax.axis_index("mdl")
    return t, m, t // 2, t % 2, m // 2, m % 2


def greet(peers):
    barrier = pltpu.get_barrier_semaphore()
    for peer in peers:
        pl.semaphore_signal(barrier, inc=1, device_id=peer, device_id_type=MESH_ID)
    return lambda: pl.semaphore_wait(barrier, len(peers))


def meet(peers):
    greet(peers)()


def chip_group(t, m):
    return [(t ^ k, m ^ b) for k in range(8) for b in range(2) if (k, b) != (0, 0)]


def column_group(t, m):
    return [(t ^ 2, m), (t ^ 4, m), (t ^ 6, m), (t ^ 1, m), (t, m ^ 2), (t, m ^ 1)]


def remote(src, dst, ssem, rsem, dev):
    return pltpu.make_async_remote_copy(
        src_ref=src, dst_ref=dst, send_sem=ssem, recv_sem=rsem, device_id=dev, device_id_type=MESH_ID
    )


def landed(ref, sem):
    pltpu.make_async_copy(ref, ref, sem).wait()


def send_unless(here, src, dst, ssem, rsem, dev):
    @pl.when(here)
    def _():
        pltpu.make_async_copy(src, dst, rsem).start()

    @pl.when(jnp.logical_not(here))
    def _():
        remote(src, dst, ssem, rsem, dev).start()


def sent_unless(here, src, dst, ssem, rsem, dev):
    @pl.when(jnp.logical_not(here))
    def _():
        remote(src, dst, ssem, rsem, dev).wait_send()


class Pushes:
    def __init__(self, outs, send, recv):
        self.outs, self.send, self.recv, self.started = outs, send, recv, []

    def push(self, shard, dev, src=None):
        e = len(self.started)
        todo = []
        for a, out in enumerate(self.outs):
            cp = remote(
                out.at[shard] if src is None else src[a],
                out.at[shard],
                self.send.at[e, a],
                self.recv.at[a, shard],
                dev,
            )
            cp.start()
            todo.append(cp)
        self.started.append(todo)

    def arrived(self, shard):
        for a, out in enumerate(self.outs):
            landed(out.at[shard], self.recv.at[a, shard])

    def finish(self):
        for todo in self.started:
            for cp in todo:
                cp.wait_send()


class Line:
    def __init__(self, outs, send, recv, fan, beside):
        self.outs, self.send, self.recv, self.fan, self.beside = outs, send, recv, fan, beside
        self.t, self.m = lax.axis_index("tok"), lax.axis_index("mdl")
        self.z = self.t // 2
        self.chips = lax.axis_size("tok") // 2

    def ways(self, hop):
        up = (0, (self.z >= hop) & (self.z < self.chips - 1), self.t - 2 * hop, self.t + 2)
        down = (1, (self.z + hop < self.chips) & (self.z > 0), self.t + 2 * hop, self.t - 2)
        return up, down

    def copies(self, hop, way, shard, to, src=None):
        at = 4 * shard + self.m
        return [
            remote(
                out.at[at] if src is None else src[a],
                out.at[at],
                self.send.at[2 * hop + way, a],
                self.recv.at[a, at],
                (to, self.m),
            )
            for a, out in enumerate(self.outs)
        ]

    def comes(self, hop, way):
        return (self.z >= hop) if way == 0 else (self.z + hop < self.chips)

    def aside(self, hop, way, shard):
        at = 4 * shard + self.m
        return [
            remote(out.at[at], out.at[at], self.fan.at[6 * (hop - 1) + 3 * way + d, a], self.recv.at[a, at], dev)
            for d, dev in enumerate(self.beside)
            for a, out in enumerate(self.outs)
        ]

    def own(self, src):
        for way, there, shard, to in self.ways(0):

            @pl.when(there)
            def _():
                for cp in self.copies(0, way, shard, to, src):
                    cp.start()

    def hop(self, hop):
        for way, there, shard, to in self.ways(hop):
            @pl.when(self.comes(hop, way))
            def _():
                at = 4 * shard + self.m
                for a, out in enumerate(self.outs):
                    landed(out.at[at], self.recv.at[a, at])
                for cp in self.aside(hop, way, shard):
                    cp.start()

            if hop < self.chips - 1:

                @pl.when(there)
                def _():
                    for cp in self.copies(hop, way, shard, to):
                        cp.start()

    def finish(self, src):
        for hop in range(self.chips - 1):
            for way, there, shard, to in self.ways(hop):

                @pl.when(there)
                def _():
                    for cp in self.copies(hop, way, shard, to, src if hop == 0 else None):
                        cp.wait_send()
        for hop in range(1, self.chips):
            for way, there, shard, to in self.ways(hop):

                @pl.when(self.comes(hop, way))
                def _():
                    for cp in self.aside(hop, way, shard):
                        cp.wait_send()


def in_parts(shape, body):
    rows, width = shape
    if rows % 24 or width % 768:
        body((slice(None), slice(None)))
        return
    across = width // 768

    def step(i, carry):
        r = pl.multiple_of(i // across * 24, 8)
        c = pl.multiple_of(i % across * 768, 128)
        body((pl.ds(r, 24), pl.ds(c, 768)))
        return carry

    lax.fori_loop(0, rows // 24 * across, step, 0)


class Sums:
    def __init__(self, ins, acc, r1, rx, ry, rd, s1, v1, ss, vx, vy, vd, own=None):
        self.own = own
        self.t, self.m = lax.axis_index("tok"), lax.axis_index("mdl")
        self.ins, self.acc, self.r1, self.rx, self.ry, self.rd = ins, acc, r1, rx, ry, rd
        self.s1, self.v1, self.ss, self.vx, self.vy, self.vd = s1, v1, ss, vx, vy, vd
        self.count = len(ins)
        self.started = []

    def owner(self, n):
        return self.t ^ (2 * (n // 4) + (n // 2) % 2), self.m ^ (2 * (n % 2))

    def first(self, n, a):
        tt, mm = self.owner(n)
        return remote(
            self.ins[a].at[4 * tt + (mm ^ 1)], self.r1[a].at[n], self.s1.at[n, a], self.v1.at[n, a], (self.t, self.m ^ 1)
        )

    def begin(self, which=None):
        for n in (15, 11, 14, 10, 7, 3, 5, 1, 6, 2, 13, 9, 12, 8, 4, 0):
            for a in range(self.count) if which is None else which:
                self.first(n, a).start()
                if self.own is not None:
                    tt, mm = self.owner(n)
                    pltpu.make_async_copy(self.ins[a].at[4 * tt + mm], self.acc[a].at[n], self.own.at[n, a]).start()

    def hop(self, e, n, dst, slot, vsem, by_x):
        dev = (self.t ^ 1, self.m) if by_x else (self.t, self.m ^ 2)
        return [
            remote(self.acc[a].at[n], dst[a].at[slot], self.ss.at[e, a], vsem.at[slot, a], dev)
            for a in range(self.count)
        ]

    def push(self, *what):
        e = len(self.started)
        self.started.append(what)
        for cp in self.hop(e, *what):
            cp.start()

    def total(self, n, a, more, store):
        tt, mm = self.owner(n)
        self.first(n, a).wait_recv()
        if self.own is not None:
            landed(self.acc[a].at[n], self.own.at[n, a])
        for buf, slot, vsem in more:
            landed(buf[a].at[slot], vsem.at[slot, a])

        def add_part(part):
            out = self.acc[a][(n,) + part] if self.own is not None else self.ins[a][(4 * tt + mm,) + part]
            out = out.astype(F32) + self.r1[a][(n,) + part].astype(F32)
            for buf, slot, vsem in more:
                out = out + buf[a][(slot,) + part].astype(F32)
            store(part, out)

        in_parts(self.acc[a].shape[1:], add_part)

    def add(self, n, more=()):
        for a in range(self.count):
            self.add_one(n, a, more)

    def add_one(self, n, a, more):
        def store(part, out):
            self.acc[a][(n,) + part] = out.astype(self.acc[a].dtype)

        self.total(n, a, more, store)

    def early(self, by_y):
        for k in (3, 2, 1, 0):
            self.add(4 * k + 3)
            self.push(4 * k + 3, self.rd, k, self.vd, k >= by_y)
        for k in (3, 2, 1, 0):
            if k >= by_y:
                self.add(4 * k + 2)
                self.push(4 * k + 2, self.rx, k, self.vx, True)
            else:
                self.add(4 * k + 1)
                self.push(4 * k + 1, self.ry, k, self.vy, False)

    def late(self, by_y):
        for k in (3, 2, 1, 0):
            via = [(self.rd, k, self.vd)]
            if k < by_y:
                self.add(4 * k + 2, via)
                self.push(4 * k + 2, self.rx, k, self.vx, True)
            else:
                self.add(4 * k + 1, via)
                self.push(4 * k + 1, self.ry, k, self.vy, False)

    def column(self, k, a, more=()):
        self.add_one(4 * k, a, [(self.rx, k, self.vx), (self.ry, k, self.vy)] + list(more))

    def column_out(self, a, out):
        def store(part, total):
            out[part] = total

        self.total(0, a, [(self.rx, 0, self.vx), (self.ry, 0, self.vy)], store)

    def finish(self):
        for n in range(16):
            for a in range(self.count):
                self.first(n, a).wait_send()
        for e, what in enumerate(self.started):
            for cp in self.hop(e, *what):
                cp.wait_send()


def sums_scratch(shards, outside):
    n = len(shards)
    bufs = [pltpu.VMEM((k,) + s, d) for k in (16, 16, 4, 4, 4) for s, d in shards]
    sems = [DMA((16, n)), DMA((16, n)), DMA((12, n)), DMA((4, n)), DMA((4, n)), DMA((4, n))]
    return bufs + sems + ([DMA((16, n))] if outside else [])


def take_sums(ins, refs, outside):
    n = len(ins)
    bufs = [refs[i * n : (i + 1) * n] for i in range(5)]
    end = 5 * n + 6 + outside
    return Sums(ins, *bufs, *refs[5 * n : end]), refs[end:]


SMALL_ROWS = 16


def side_by_side(smalls, width):
    step = width // 32
    lane = lax.broadcasted_iota(jnp.int32, (128, width), 0)
    col = lax.broadcasted_iota(jnp.int32, (128, width), 1)
    pick = (lax.rem(col, step) == lane).astype(BF)
    every = lax.dot_general(
        smalls.reshape(32 * SMALL_ROWS, 128).astype(BF), pick, (((1,), (0,)), ((), ())), preferred_element_type=F32
    )
    shard = lax.broadcasted_iota(jnp.int32, (32, SMALL_ROWS, width), 0)
    at = lax.broadcasted_iota(jnp.int32, (32, SMALL_ROWS, width), 2) // step
    return jnp.sum(jnp.where(shard == at, every.reshape(32, SMALL_ROWS, width), 0.0), axis=0)


def attend_kernel(*refs):
    (tokens_ref, starts_ref), masters, vectors = refs[:2], refs[2:6], refs[6:15]
    full_qkv, smalls_out, weights, (heads, of_ref, l_ref, att, begins) = refs[15], refs[16], refs[17:20], refs[20:25]
    (low_qkv, low0, low1, low2, small, smalls, wq, normed, jv, xv, kn, acc, ms, ls, stage) = refs[25:40]
    (s1, v1, local, s_full, r_full, s_sh, r_sh, s_fw, r_fw, s_out, r_out, keep, send, recv, send_z, fan, pass_sem) = refs[40:]
    t, m, z, x, y, c = place()
    xn, yn, sib = (t ^ 1, m), (t, m ^ 2), (t, m ^ 1)
    own = x == c
    role = (x + c) % 2
    hf, hs, owner_m = 3 * z + 2 * x, 3 * z + 1, 2 * y + x
    lows = (low0, low1, low2)
    me = 4 * t + m
    step = low_qkv.shape[0]
    width = 32 * step

    met = greet(chip_group(t, m) + [yn])
    low_qkv[...] = masters[0][...].astype(BF)
    small[...] = jnp.zeros_like(small)
    for v in range(8):
        small[v : v + 1, 0:step] = vectors[v][...].astype(BF).astype(F32)
    for q in range(4):
        small[8 + q : 9 + q, 0:step] = vectors[8][:, q * step : (q + 1) * step].astype(BF).astype(F32)
    small[12:13, 0 : starts_ref.shape[1]] = starts_ref[...].astype(F32)
    smalls[me] = small[...]
    met()

    class Shards:
        def __init__(self, ref):
            self.at = self
            self.ref = ref

        def __getitem__(self, shard):
            return self.ref.at[pl.ds(pl.multiple_of(step * shard, 8), step)]

    first = Pushes((Shards(full_qkv), smalls), s1, v1)
    for dev in [(t ^ 2, m), (t ^ 4, m), (t ^ 6, m), xn, yn, sib]:
        first.push(me, dev, (low_qkv, small))
    work = Pushes(weights, send, recv)
    for low, master in zip(lows, masters[1:]):
        low[...] = master[...].astype(BF)
    column = Line(weights, send_z, recv, fan, (xn, yn, sib))
    own_rows = [pltpu.make_async_copy(low_qkv, Shards(full_qkv)[me], local.at[0])]
    own_rows += [pltpu.make_async_copy(lows[a], weights[a].at[me], local.at[1 + a]) for a in range(3)]
    for cp in own_rows:
        cp.start()

    values = tokens_ref[...].astype(F32)
    center = values - jnp.mean(values, axis=-1, keepdims=True)
    spread = jnp.mean(center * center, axis=-1, keepdims=True)
    xhat = center * lax.rsqrt(spread + epsilon)

    for k in range(1, 4):
        shard = 4 * (t ^ (2 * k)) + m
        first.arrived(shard)
        for dev in (xn, yn, sib):
            first.push(shard, dev)
    column.own(lows)
    for k in range(4):
        col = t ^ (2 * k)
        xi, yi = 4 * (col ^ 1) + m, 4 * col + (m ^ 2)
        first.arrived(xi)
        if k < 2:
            first.push(xi, yn)
        first.push(xi, sib)
        first.arrived(yi)
        if k >= 2:
            first.push(yi, xn)
        first.push(yi, sib)
    for dev in (xn, yn, sib):
        work.push(me, dev, lows)
    column.hop(1)
    for k in range(4):
        di = 4 * (t ^ (2 * k) ^ 1) + (m ^ 2)
        first.arrived(di)
        first.push(di, sib)
    for k in range(4):
        for a in (0, 1):
            for b in (0, 2):
                first.arrived(4 * (t ^ (2 * k) ^ a) + (m ^ b ^ 1))
    column.hop(2)
    for cp in own_rows:
        cp.wait()
    load = pltpu.make_async_copy(full_qkv, wq, local.at[4])
    load.start()
    share = pltpu.make_async_copy(smalls, smalls_out, local.at[5])
    share.start()
    flat = side_by_side(smalls[...], width)
    normed[...] = (xhat * flat[3:4] + flat[4:5]).astype(BF)
    bias = jnp.concatenate([flat[0:1], jnp.zeros_like(flat[0:1]), flat[1:2]], axis=1)
    begins[0] = smalls[m, 12:13, :].astype(jnp.int32)
    begins[1] = smalls[owner_m, 12:13, :].astype(jnp.int32)
    load.wait()
    for n in range(9):
        part = slice(n * 256, (n + 1) * 256)
        block = lax.dot_general(
            normed[...], wq[:, part], (((1,), (0,)), ((), ())), preferred_element_type=F32
        )
        block = (block + bias[:, part]).T.astype(BF)
        for h in range(4):
            g = 4 * n + h
            jv[g // 12, g % 12] = block[h * HD : (h + 1) * HD]

    def full(k):
        d = t ^ k
        return jv.at[:, 3 * (d // 2) + 2 * (d % 2)], xv.at[0, t], s_full.at[k], r_full.at[t], (d, m)

    def shared(k):
        zd = z ^ k
        return jv.at[:, 3 * zd + 1], xv.at[1, t], s_sh.at[k], r_sh.at[t], (2 * zd + c, m)

    for k in (4, 5, 6, 7, 2, 3, 1):
        remote(*full(k)).start()
    loc = full(0)
    pltpu.make_async_copy(loc[0], loc[1], loc[3]).start()
    column.hop(3)
    for k in range(1, 8):
        remote(*full(k)).wait_send()
    for k in (2, 3, 1):
        remote(*shared(k)).start()
    send_unless(own, *shared(0))

    def keep_head(slot):
        cp = pltpu.make_async_copy(xv.at[slot], heads.at[slot], keep.at[slot])
        cp.start()
        return cp

    for b in range(8):
        landed(xv.at[0, b], r_full.at[b])
    kept = [keep_head(0)]
    for b in range(8):
        kn[0, b] = xv[0, b, 1].T

    def begin_of(slot, task):
        lane = lax.broadcasted_iota(jnp.int32, (1, 128), 1)
        return jnp.sum(jnp.where(lane == task, begins[slot], 0), axis=1, keepdims=True)

    def finish_task(slot, task, row, head, mdl, alone):
        for h in range(2):
            b, u = 2 * task + h, 2 * row + h
            out = acc[h] / ls[h]
            of_ref[u] = out
            stage[u] = out.astype(BF)
            l_ref[u] = ms[h] + jnp.log2(ls[h])
            send_unless((b == t) & alone, stage.at[u], att.at[head], s_out.at[u], r_out.at[head], (b, mdl))

    def full_task(w, carry):
        forward_task(0, w, begin_of(0, w), xv, kn, acc, ms, ls)
        finish_task(0, w, w, hf, m, t >= 0)
        return carry

    def pass_on(begin):
        e = 0
        for k in range(4):
            col = t ^ (2 * k)
            xi, yi = 4 * (col ^ 1) + m, 4 * col + (m ^ 2)
            for shard, devs in ((xi, [yn, sib] if k < 3 else [sib]), (yi, [xn, sib] if k == 3 else [sib])):
                if begin:
                    work.arrived(shard)
                for dev in devs:
                    for n, out in enumerate(weights):
                        cp = remote(out.at[shard], out.at[shard], pass_sem.at[e, n], recv.at[n, shard], dev)
                        if begin:
                            cp.start()
                        else:
                            cp.wait_send()
                    e += 1

    inner = (z == 1) | (z == 2)

    @pl.when(inner)
    def _():
        pass_on(True)

    lax.fori_loop(0, 3, full_task, 0)

    @pl.when(jnp.logical_not(inner))
    def _():
        pass_on(True)

    def forward(k):
        b = t ^ k
        return remote(xv.at[1, b], xv.at[1, b], s_fw.at[k], r_fw.at[b], sib)

    @pl.when(own)
    def _():
        for k in (0, 1, 2, 3, 6, 7, 4, 5):
            landed(xv.at[1, t ^ k], r_sh.at[t ^ k])
            forward(k).start()

    lax.fori_loop(3, 4, full_task, 0)

    @pl.when(jnp.logical_not(own))
    def _():
        for k in range(8):
            forward(k).wait_recv()

    kept.append(keep_head(1))
    for b in range(8):
        kn[1, b] = xv[1, b, 1].T

    def shared_task(n, carry):
        task = jnp.where(n == 0, role, 3 - role)
        forward_task(1, task, begin_of(1, task), xv, kn, acc, ms, ls)
        finish_task(1, task, 4 + n, hs, owner_m, own)
        return carry

    lax.fori_loop(0, 2, shared_task, 0)

    for k in range(4):
        di = 4 * (t ^ (2 * k) ^ 1) + (m ^ 2)
        work.arrived(di)
        work.push(di, sib)
    for h in range(12):
        landed(att.at[h], r_out.at[h])
    for k in range(4):
        for a in (0, 1):
            for b in (0, 2):
                work.arrived(4 * (t ^ (2 * k) ^ a) + (m ^ b ^ 1))
    first.finish()
    work.finish()
    pass_on(False)
    column.finish(lows)
    for k in (1, 2, 3):
        remote(*shared(k)).wait_send()
    sent_unless(own, *shared(0))

    @pl.when(own)
    def _():
        for k in range(8):
            forward(k).wait_send()

    for w in range(4):
        for h in range(2):
            b, u = 2 * w + h, 2 * w + h
            sent_unless(b == t, stage.at[u], att.at[hf], s_out.at[u], r_out.at[hf], (b, m))
    for n in range(2):
        task = role if n == 0 else 3 - role
        for h in range(2):
            b, u = 2 * task + h, 8 + 2 * n + h
            sent_unless((b == t) & own, stage.at[u], att.at[hs], s_out.at[u], r_out.at[hs], (b, owner_m))
    for cp in kept:
        cp.wait()
    share.wait()


def attend(tokens, starts, masters, vectors, cid):
    rows, width = tokens.shape
    step = width // 32
    head = (HD, BLK)
    S, V = jax.ShapeDtypeStruct, pltpu.VMEM
    outs = pl.pallas_call(
        attend_kernel,
        out_shape=(S((width, 3 * width), BF), S((32, SMALL_ROWS, 128), F32))
        + tuple(S((32,) + w.shape, BF) for w in masters[1:])
        + (S((2, 8, 3) + head, BF), S((12,) + head, F32), S((12, 1, BLK), F32), S((12,) + head, BF), S((2, 1, 128), jnp.int32)),
        in_specs=[VMEMS] * 15,
        out_specs=(ANYS,) * 6 + (VMEMS, VMEMS, ANYS, VMEMS),
        scratch_shapes=[V(w.shape, BF) for w in masters]
        + [
            V((SMALL_ROWS, 128), F32),
            V((32, SMALL_ROWS, 128), F32),
            V((width, 3 * width), BF),
            V((rows, width), BF),
            V((3, 12) + head, BF),
            V((2, 8, 3) + head, BF),
            V((2, 8, BLK, HD), BF),
            V((2,) + head, F32),
            V((2, 1, BLK), F32),
            V((2, 1, BLK), F32),
            V((12,) + head, BF),
        ]
        + [DMA((31, 2)), DMA((2, 32)), DMA((6,))]
        + [DMA((8,)), DMA((8,)), DMA((4,)), DMA((8,)), DMA((8,)), DMA((8,)), DMA((12,)), DMA((12,)), DMA((2,))]
        + [DMA((7, 3)), DMA((3, 32)), DMA((6, 3)), DMA((18, 3)), DMA((12, 3))],
        name="attend",
        compiler_params=pltpu.CompilerParams(collective_id=cid, has_side_effects=True, vmem_limit_bytes=62 << 20),
    )(tokens, starts, *masters, *vectors)
    return outs[0], outs[1], outs[2:5], outs[5:]


FF_BLOCK = 512
HBMS = pl.BlockSpec(memory_space=pltpu.HBM)


def shard_rows(rows, step):
    r, n = rows.shape
    count = n // step
    shard = lax.broadcasted_iota(jnp.int32, (count, r, n), 0)
    at = lax.broadcasted_iota(jnp.int32, (count, r, n), 2) // step
    spread = jnp.where(shard == at, rows[None], 0.0).reshape(count * r, n)
    col = lax.broadcasted_iota(jnp.int32, (n, 128), 0)
    lane = lax.broadcasted_iota(jnp.int32, (n, 128), 1)
    pick = (lax.rem(col, step) == lane).astype(F32)
    out = lax.dot_general(
        spread, pick, (((1,), (0,)), ((), ())), precision=lax.Precision.HIGHEST, preferred_element_type=F32
    )
    return out.reshape(count, r, 128)


def expand_row(smalls, hidden):
    step = hidden // 128
    lane = lax.broadcasted_iota(jnp.int32, (128, hidden), 0)
    col = lax.broadcasted_iota(jnp.int32, (128, hidden), 1)
    pick = (lax.rem(col, step) == lane).astype(BF)
    every = nn(smalls[:, 8:12, :].reshape(128, 128).astype(BF), pick)
    return jnp.sum(jnp.where(lane == col // step, every, 0.0), axis=0, keepdims=True)


def middle_kernel(
    x_ref, c_ref, att_any, smalls_any, wo_any, we_ref, ws_ref,
    out_ref, gh_ref, gm_any, dwo_any, dwe_ref, dws_ref, flat, vec_ref, dbe_ref,
    be, hidden, xhat, inv, n2, n2t, out_acc, dn2, att_ref, smalls_ref, wo_ref, gm_ref, dwo_ref, sems,
):
    i = pl.program_id(0)
    last = pl.num_programs(0) - 1
    width = x_ref.shape[1]

    @pl.when(i == 0)
    def _():
        pairs = ((smalls_any, smalls_ref), (att_any, att_ref), (wo_any, wo_ref))
        loads = [pltpu.make_async_copy(a, b, sems.at[n]) for n, (a, b) in enumerate(pairs)]
        for cp in loads:
            cp.start()
        loads[0].wait()
        flat[...] = side_by_side(smalls_ref[...], width)
        row = expand_row(smalls_ref[...], be.shape[0] * FF_BLOCK)
        for n in range(be.shape[0]):
            be[n] = row[:, n * FF_BLOCK : (n + 1) * FF_BLOCK]
        loads[1].wait()
        loads[2].wait()
        branch = nn(att_ref[...].T, wo_ref[...]) + flat[2:3]
        h = x_ref[...].astype(F32) + branch
        hidden[...] = h
        center = h - jnp.mean(h, axis=-1, keepdims=True)
        scale = lax.rsqrt(jnp.mean(center * center, axis=-1, keepdims=True) + epsilon)
        inv[...] = scale
        xhat[...] = center * scale
        low = (xhat[...] * flat[5:6] + flat[6:7]).astype(BF)
        n2[...] = low
        n2t[...] = low.T
        out_acc[...] = jnp.zeros_like(out_acc)
        dn2[...] = jnp.zeros_like(dn2)

    u = nn(n2[...], we_ref[...]) + be[i]
    square = u * u
    th = jnp.tanh(gelu_coeff * (u + 0.044715 * square * u))
    half = 0.5 * (1.0 + th)
    act = (u * half).astype(BF)
    slope = half + 0.5 * u * (1.0 - th * th) * (gelu_coeff * (1.0 + 3.0 * 0.044715 * square))
    out_acc[...] += nn(act, ws_ref[...])
    ge = nt(c_ref[...], ws_ref[...]) * slope
    ge = ge.astype(BF)
    dbe_ref[...] = jnp.sum(ge.astype(F32), axis=0, keepdims=True)
    dws_ref[...] = nn(act.T, c_ref[...]).astype(BF)
    dwe_ref[...] = nn(n2t[...], ge).astype(BF)
    dn2[...] += nt(ge, we_ref[...])

    @pl.when(i == last)
    def _():
        out_ref[...] = (hidden[...] + (out_acc[...] + flat[7:8])).astype(BF)
        up = c_ref[...].astype(F32)
        e = dn2[...]
        f = e * flat[5:6]
        xh = xhat[...]
        dv = f - jnp.mean(f, axis=-1, keepdims=True) - xh * jnp.mean(f * xh, axis=-1, keepdims=True)
        gh = up + dv * inv[...]
        gh_ref[...] = gh
        ga = gh.astype(BF)
        gm_ref[...] = nt(wo_ref[...], ga).astype(BF)
        saves = [pltpu.make_async_copy(gm_ref, gm_any, sems.at[3])]
        saves[0].start()
        dwo_ref[...] = nn(att_ref[...], ga).astype(BF)
        saves.append(pltpu.make_async_copy(dwo_ref, dwo_any, sems.at[4]))
        saves[1].start()
        vec_ref[0:1] = jnp.sum(ga.astype(F32), axis=0, keepdims=True)
        vec_ref[1:2] = jnp.sum(e * xh, axis=0, keepdims=True)
        vec_ref[2:3] = jnp.sum(e, axis=0, keepdims=True)
        vec_ref[3:4] = jnp.sum(up, axis=0, keepdims=True)
        vec_ref[4:8] = jnp.zeros((4, width), F32)
        for cp in saves:
            cp.wait()


def middle(x, c, att, smalls, wo, we, ws):
    rows, width = x.shape
    hidden = we.shape[1]
    S, V = jax.ShapeDtypeStruct, pltpu.VMEM
    n = hidden // FF_BLOCK
    across = pl.BlockSpec((width, FF_BLOCK), lambda i: (0, i))
    down = pl.BlockSpec((FF_BLOCK, width), lambda i: (i, 0))
    whole = lambda a: pl.BlockSpec(a.shape, lambda i: (0,) * len(a.shape), pipeline_mode=pl.Buffered(1))
    outs = (
        S((rows, width), BF),
        S((rows, width), F32),
        S((width, rows), BF),
        S((width, width), BF),
        S((width, hidden), BF),
        S((hidden, width), BF),
        S((SMALL_ROWS, width), F32),
        S((8, width), F32),
        S((1, hidden), F32),
    )
    return pl.pallas_call(
        middle_kernel,
        grid=(n,),
        out_shape=outs,
        in_specs=[whole(x), whole(c), HBMS, HBMS, HBMS, across, down],
        out_specs=(whole(outs[0]), whole(outs[1]), HBMS, HBMS)
        + (across, down, whole(outs[6]), whole(outs[7]), pl.BlockSpec((1, FF_BLOCK), lambda i: (0, i))),
        scratch_shapes=[
            V((n, 1, FF_BLOCK), F32),
            V((rows, width), F32),
            V((rows, width), F32),
            V((rows, 1), F32),
            V((rows, width), BF),
            V((width, rows), BF),
            V((rows, width), F32),
            V((rows, width), F32),
            V(att.shape, BF),
            V(smalls.shape, F32),
            V(wo.shape, BF),
            V((width, rows), BF),
            V((width, width), BF),
            DMA((5,)),
        ],
        name="middle",
        compiler_params=pltpu.CompilerParams(vmem_limit_bytes=62 << 20),
    )(x, c, att, smalls, wo, we, ws)


def attend_back_kernel(*refs):
    g_ref, heads_ref, of_ref, l_ref, tokens_ref, begins, flat_ref, vec_ref, bias_ref, wq_ref = refs[:10]
    ins, dx_ref, last_outs, outs = refs[10:13], refs[13], refs[14:16], refs[16:19]
    work, rest = take_sums(ins, refs[19:], True)
    dwq, small, dwkv, gj, wq, normed_t, rzp = rest[0], rest[1], rest[2], rest[3], rest[4], rest[5], rest[6:9]
    tail, rest = take_sums((dwq, small), rest[9:], False)
    rz, rest = rest[:2], rest[2:]
    tail_kv, rest = take_sums((dwkv,), rest, False)
    rzk, rest = rest[:1], rest[1:]
    (xv, gv, kn, vn, dkv, dq, lsum, delta, stage, stage_kv, got, stage_sh, ofv, dxv) = rest[:14]
    (s_full, r_full, s_sh, r_sh, s_fw, r_fw, s_q, r_q, s_kv, r_kv, s_shkv, s_part, r_part) = rest[14:27]
    szp, vzp, sz, vz, szk, vzk, local = rest[27:]
    count = len(ins)
    t, m, z, x, y, c = place()
    sib = (t, m ^ 1)
    met = greet(chip_group(t, m) + [(t, m ^ 2)])
    def load_of(first):
        return pltpu.make_async_copy(of_ref.at[pl.ds(first, 4)], ofv, local.at[5])

    loads = [pltpu.make_async_copy(heads_ref.at[s, :, 2], stage_kv.at[:, s], local.at[s]) for s in range(2)]
    loads += [pltpu.make_async_copy(heads_ref.at[s, :, pl.ds(0, 2)], xv.at[s], local.at[2 + s]) for s in range(2)]
    load_of(8).start()
    for cp in loads:
        cp.start()
    met()
    own = x == c
    role = (x + c) % 2
    hf, hs, owner_m = 3 * z + 2 * x, 3 * z + 1, 2 * y + x
    order = (4, 5, 6, 7, 2, 3, 1)

    def full(k):
        d = t ^ k
        return g_ref.at[3 * (d // 2) + 2 * (d % 2)], gv.at[0, t], s_full.at[k], r_full.at[t], (d, m)

    def shared(k):
        zd = z ^ k
        return g_ref.at[3 * zd + 1], gv.at[1, t], s_sh.at[k], r_sh.at[t], (2 * zd + c, m)

    for k in (2, 3, 1):
        remote(*shared(k)).start()
    send_unless(own, *shared(0))
    loc = full(0)
    pltpu.make_async_copy(loc[0], loc[1], loc[3]).start()
    work.begin()
    for cp in loads:
        cp.wait()
    for s in range(2):
        for b in range(8):
            kn[s, b] = xv[s, b, 1].T
            vn[s, b] = stage_kv[b, s].T
    dkv[...] = jnp.zeros_like(dkv)
    dq[...] = jnp.zeros_like(dq)
    for k in (1, 2, 3):
        remote(*shared(k)).wait_send()
    sent_unless(own, *shared(0))
    for k in order:
        remote(*full(k)).start()

    def forward(k):
        b = t ^ k
        return remote(gv.at[1, b], gv.at[1, b], s_fw.at[k], r_fw.at[b], sib)

    @pl.when(own)
    def _():
        for k in (0, 1, 2, 3, 6, 7, 4, 5):
            landed(gv.at[1, t ^ k], r_sh.at[t ^ k])
            forward(k).start()

    work.early(4)

    @pl.when(jnp.logical_not(own))
    def _():
        for k in range(8):
            forward(k).wait_recv()

    def begin_of(slot, task):
        lane = lax.broadcasted_iota(jnp.int32, (1, 128), 1)
        return jnp.sum(jnp.where(lane == task, begins[slot], 0), axis=1, keepdims=True)

    def ready(slot, b, u):
        lsum[slot, b] = l_ref[u]
        delta[slot, b] = jnp.sum(gv[slot, b].astype(F32) * ofv[u % 4], axis=0, keepdims=True)

    def out_q(slot, b, u):
        stage[u] = (dq[u] * HD ** (-0.5)).astype(BF)
        if slot:
            send_unless((b == t) & own, stage.at[u], gj.at[0, hs], s_q.at[u], r_q.at[hs], (b, owner_m))
        else:
            send_unless(b == t, stage.at[u], gj.at[0, hf], s_q.at[u], r_q.at[hf], (b, m))

    args = (xv, gv, kn, vn, lsum, delta, dkv, dq)

    def shared_task(n, carry):
        task = jnp.where(n == 0, role, 3 - role)
        begin = begin_of(1, task)

        def step(j, carry):
            backward_units(1, task, 8 + 2 * n, 0, [(j, h, None, 0, BLK, 0, BLK) for h in range(2)], begin, *args)
            return carry

        lax.fori_loop(0, 2 * task, step, 0)
        backward_units(1, task, 8 + 2 * n, 0, diag_units(task), begin, *args)
        for h in range(2):
            out_q(1, 2 * task + h, 8 + 2 * n + h)
        return carry

    load_of(8).wait()
    for n in range(2):
        task = role if n == 0 else 3 - role
        for h in range(2):
            ready(1, 2 * task + h, 8 + 2 * n + h)
    load_of(0).start()
    lax.fori_loop(0, 2, shared_task, 0)

    def part(k):
        b = t ^ k
        return remote(dkv.at[b], got.at[b], s_part.at[k], r_part.at[b], sib)

    def shared_kv(k):
        b = t ^ k
        return stage_sh.at[b], gj.at[pl.ds(1, 2), hs], s_shkv.at[k], r_kv.at[hs], (b, m)

    @pl.when(jnp.logical_not(own))
    def _():
        for k in order + (0,):
            part(k).start()

    for b in range(8):
        landed(gv.at[0, b], r_full.at[b])
    load_of(0).wait()
    for b in range(4):
        ready(0, b, b)
    load_of(4).start()
    load_of(4).wait()
    for b in range(4, 8):
        ready(0, b, b)

    @pl.when(own)
    def _():
        for k in order + (0,):
            b = t ^ k
            part(k).wait_recv()
            stage_sh[b, 0] = ((dkv[b, 0] + got[b, 0]) * HD ** (-0.5)).astype(BF)
            stage_sh[b, 1] = (dkv[b, 1] + got[b, 1]).astype(BF)
            a = shared_kv(k)
            if k:
                remote(*a).start()
            else:
                pltpu.make_async_copy(a[0], a[1], a[3]).start()

    def full_keys(s, carry):
        keys = z ^ (3 - s)
        dkv[8:10] = jnp.zeros((2,) + dkv.shape[1:], F32)
        backward_units(0, keys, 2 * keys, 8 - 2 * keys, diag_units(keys), begin_of(0, keys), *args)

        def step(n, carry):
            task, j = n // 2, 2 * keys + n % 2
            units = [(j, h, None, 0, BLK, 0, BLK) for h in range(2)]
            backward_units(0, task, 2 * task, 8 - 2 * keys, units, 0, *args)
            return carry

        lax.fori_loop(2 * keys + 2, 8, step, 0)
        for i in range(2):
            b = 2 * keys + i
            stage_kv[b, 0] = (dkv[8 + i, 0] * HD ** (-0.5)).astype(BF)
            stage_kv[b, 1] = dkv[8 + i, 1].astype(BF)
            send_unless(b == t, stage_kv.at[b], gj.at[pl.ds(1, 2), hf], s_kv.at[b], r_kv.at[hf], (b, m))

        @pl.when(s == jnp.where(z == 0, 1, 0))
        def _():
            work.late(4)

        return carry

    lax.fori_loop(0, 4, full_keys, 0)
    for b in range(8):
        out_q(0, b, b)
    along = []

    def z_push(sums, k, a, buf, slot, ssem, vsem, to, more=()):
        sums.column(k, a, more)
        cp = remote(sums.acc[a].at[4 * k], buf[a].at[slot], ssem.at[slot, a], vsem.at[slot, a], (t ^ (2 * to), m))
        cp.start()
        along.append(cp)

    width = tokens_ref.shape[1]
    step = width // 32
    gain, shift = flat_ref[3:4], flat_ref[4:5]

    def norm(half):
        values = tokens_ref[half].astype(F32)
        center = values - jnp.mean(values, axis=-1, keepdims=True)
        inv = lax.rsqrt(jnp.mean(center * center, axis=-1, keepdims=True) + epsilon)
        return center * inv, inv

    load = pltpu.make_async_copy(wq_ref, wq, local.at[4])
    load.start()
    halves = [slice(n * 256, (n + 1) * 256) for n in range(tokens_ref.shape[0] // 256)]
    for half in halves:
        normed_t[:, half] = (norm(half)[0] * gain + shift).astype(BF).T

    for a in range(count):
        z_push(work, 3, a, rzp, 1, szp, vzp, 1)
        z_push(work, 1, a, rzp, 0, szp, vzp, 1)

    def weight_grads(first, last, out):
        for n in range(first, last):
            grads = gj[n // 3, 4 * (n % 3) : 4 * (n % 3) + 4].reshape(256, BLK)
            block = nt(normed_t[...], grads).reshape(32, step, 256)
            out[:, :, (n - first) * 256 : (n - first + 1) * 256] = block.astype(BF)

    for h in range(12):
        landed(gj.at[pl.ds(1, 2), h], r_kv.at[h])
    weight_grads(3, 9, dwkv)
    tail_kv.begin()
    for h in range(12):
        landed(gj.at[0, h], r_q.at[h])
    weight_grads(0, 3, dwq)
    tail.begin([0])
    load.wait()
    tail_kv.early(2)
    for a in range(count):
        z_push(work, 2, a, rzp, 2, szp, vzp, 2, [(rzp, 1, vzp)])
    dgain, dshift = jnp.zeros((1, width), F32), jnp.zeros((1, width), F32)
    for half in halves:
        e = jnp.zeros((width, 256), F32)
        for n in range(9):
            grads = gj[n // 3, 4 * (n % 3) : 4 * (n % 3) + 4, :, half].reshape(256, 256)
            e = e + nn(wq[:, n * 256 : (n + 1) * 256], grads)
        e = e.T
        xhat, inv = norm(half)
        f = e * gain
        dv = f - jnp.mean(f, axis=-1, keepdims=True) - xhat * jnp.mean(f * xhat, axis=-1, keepdims=True)
        if half.start:
            out_x.wait()
        dxv[...] = dv * inv
        out_x = pltpu.make_async_copy(dxv, dx_ref.at[half], local.at[6])
        out_x.start()
        dgain = dgain + jnp.sum(e * xhat, axis=0, keepdims=True)
        dshift = dshift + jnp.sum(e, axis=0, keepdims=True)
    ones = jnp.ones((8, BLK), BF)
    db_query = nt(ones, gj[0].reshape(width, BLK))[0:1]
    db_value = nt(ones, gj[2].reshape(width, BLK))[0:1]
    rows = [db_query, db_value, vec_ref[0:1], dgain, dshift, vec_ref[1:4]]
    small[:, 0:8] = shard_rows(jnp.concatenate(rows, axis=0), step)
    small[:, 8:12] = bias_ref[...]
    small[:, 12:16] = jnp.zeros((32, 4, 128), F32)
    tail.begin([1])
    tail_kv.late(2)
    tail.early(2)
    for k in (3, 2, 1):
        z_push(tail_kv, k, 0, rzk, k - 1, szk, vzk, k)
    tail.late(2)
    for k in (3, 2, 1):
        for a in range(2):
            z_push(tail, k, a, rz, k - 1, sz, vz, k)

    def gather_z(a, out, buf, slots, vsem):
        for n in slots:
            landed(buf.at[n], vsem.at[n, a])

        def add_part(part):
            total = out[part]
            for n in slots:
                total = total + buf[(n,) + part].astype(F32)
            out[part] = total

        in_parts(out.shape, add_part)

    for a in range(count):
        work.column_out(a, outs[a])
        gather_z(a, outs[a], rzp[a], (0, 2), vzp)
    ends = last_outs[0].at[:, pl.ds(0, width)], last_outs[1]
    end_kv = last_outs[0].at[:, pl.ds(width, 2 * width)]
    tail_kv.column_out(0, end_kv)
    gather_z(0, end_kv, rzk[0], (0, 1, 2), vzk)
    for a in range(2):
        tail.column_out(a, ends[a])
        gather_z(a, ends[a], rz[a], (0, 1, 2), vz)
    out_x.wait()
    tail.finish()
    tail_kv.finish()
    for cp in along:
        cp.wait_send()
    work.finish()
    for k in range(1, 8):
        remote(*full(k)).wait_send()
    for b in range(8):
        sent_unless(b == t, stage.at[b], gj.at[0, hf], s_q.at[b], r_q.at[hf], (b, m))
        sent_unless(b == t, stage_kv.at[b], gj.at[pl.ds(1, 2), hf], s_kv.at[b], r_kv.at[hf], (b, m))
    for n in range(2):
        task = role if n == 0 else 3 - role
        for h in range(2):
            b, u = 2 * task + h, 8 + 2 * n + h
            sent_unless((b == t) & own, stage.at[u], gj.at[0, hs], s_q.at[u], r_q.at[hs], (b, owner_m))

    @pl.when(own)
    def _():
        for k in range(8):
            forward(k).wait_send()
        for k in range(1, 8):
            remote(*shared_kv(k)).wait_send()

    @pl.when(jnp.logical_not(own))
    def _():
        for k in range(8):
            part(k).wait_send()


def attend_back(grad_mix, heads, out_full, log_sum, tokens, begins, flat, vec, bias, full_qkv, grads, cid):
    n = len(grads)
    rows, width = tokens.shape
    head = (HD, BLK)
    S, V = jax.ShapeDtypeStruct, pltpu.VMEM
    shards = [(g.shape[1:], BF) for g in grads]
    last = [((width // 32, width), BF), ((SMALL_ROWS, 128), F32)]
    keyed = [((width // 32, 2 * width), BF)]
    ends = [(width // 32, 3 * width), (SMALL_ROWS, 128)] + [s for s, d in shards]
    return pl.pallas_call(
        attend_back_kernel,
        out_shape=(S((rows, width), F32),) + tuple(S(s, F32) for s in ends),
        in_specs=[ANYS] * 3 + [VMEMS] * 6 + [ANYS] + [ANYS] * n,
        out_specs=(ANYS,) + (VMEMS,) * (2 + n),
        scratch_shapes=sums_scratch(shards, True)
        + [V((32,) + s, d) for s, d in last + keyed]
        + [V((3, 12) + head, BF), V((width, 3 * width), BF), V((width, rows), BF)]
        + [V((3,) + s, d) for s, d in shards]
        + sums_scratch(last, False)
        + [V((3,) + s, d) for s, d in last]
        + sums_scratch(keyed, False)
        + [V((3,) + s, d) for s, d in keyed]
        + [
            V((2, 8, 2) + head, BF),
            V((2, 8) + head, BF),
            V((2, 8, BLK, HD), BF),
            V((2, 8, BLK, HD), BF),
            V((10, 2) + head, F32),
            V((12,) + head, F32),
            V((2, 8, 1, BLK), F32),
            V((2, 8, 1, BLK), F32),
            V((12,) + head, BF),
            V((8, 2) + head, BF),
            V((8, 2) + head, F32),
            V((8, 2) + head, BF),
            V((4,) + head, F32),
            V((256, width), F32),
        ]
        + [DMA((8,)), DMA((8,)), DMA((4,)), DMA((8,)), DMA((8,)), DMA((8,)), DMA((12,)), DMA((12,))]
        + [DMA((8,)), DMA((12,)), DMA((8,)), DMA((8,)), DMA((8,))]
        + [DMA((4, n)), DMA((4, n)), DMA((4, 2)), DMA((4, 2)), DMA((4, 1)), DMA((4, 1)), DMA((7,))],
        name="attend_back",
        compiler_params=pltpu.CompilerParams(collective_id=cid, has_side_effects=True, vmem_limit_bytes=62 << 20),
    )(grad_mix, heads, out_full, log_sum, tokens, begins, flat, vec, bias, full_qkv, *grads)


def by_heads(
    tokens,
    cotangent,
    starts,
    w_qkv,
    b_query,
    b_value,
    w_out,
    b_out,
    gain_one,
    shift_one,
    gain_two,
    shift_two,
    w_expand,
    b_expand,
    w_shrink,
    b_shrink,
):
    rows, width = tokens.shape[1:]
    hidden = b_expand.shape[0] * 32
    vectors = [b_query, b_value, b_out, gain_one, shift_one, gain_two, shift_two, b_shrink, b_expand]
    full_qkv, smalls, rest, (heads, out_full, log_sum, attention, begins) = attend(
        tokens[0], starts, [w_qkv, w_out, w_expand, w_shrink], [v.reshape(1, -1) for v in vectors], 1
    )
    full_out, full_expand, full_shrink = (w.reshape(-1, w.shape[-1]) for w in rest)
    attention = attention.reshape(width, rows)
    step = width // 32
    layer_out, grad_hidden, grad_mix, dw_out, dw_expand, dw_shrink, flat, sums, db_expand = middle(
        tokens[0], cotangent[0], attention, smalls, full_out, full_expand, full_shrink
    )
    bias = jnp.pad(db_expand.reshape(32, 4, step), [(0, 0), (0, 0), (0, 128 - step)])
    shards = lambda w: w.reshape((32, -1) + w.shape[1:])
    dtokens, dw_qkv, smalls, dw_out, dw_expand, dw_shrink = attend_back(
        grad_mix.reshape(12, HD, rows),
        heads,
        out_full,
        log_sum,
        tokens[0],
        begins,
        flat,
        sums,
        bias,
        full_qkv,
        [shards(dw_out), shards(dw_expand), shards(dw_shrink)],
        2,
    )
    step = width // 32
    vecs = [smalls[i, :step] for i in range(8)]
    db_query, db_value, db_out, dgain_one, dshift_one, dgain_two, dshift_two, db_shrink = vecs
    db_expand = smalls[8:12, :step].reshape(-1)
    return (
        layer_out.reshape(1, rows, width),
        (grad_hidden + dtokens).reshape(1, rows, width),
        dw_qkv,
        db_query,
        db_value,
        dw_out,
        db_out,
        dgain_one,
        dshift_one,
        dgain_two,
        dshift_two,
        dw_expand,
        db_expand,
        dw_shrink,
        db_shrink,
    )


def solution(mesh):
    rows, vector, seq = P(("tok", "mdl"), None), P(("tok", "mdl")), P("mdl", "tok", None)
    by_name = dict(m=rows, v=vector, s=seq)
    fits = mesh.shape["tok"] == 8 and mesh.shape["mdl"] == 4
    return jax.shard_map(
        by_heads if fits else general,
        mesh=mesh,
        in_specs=(seq, seq, P("mdl", None)) + tuple(by_name[k] for k in "mvvmvvvvvmvmv"),
        out_specs=tuple(by_name[k] for k in "ssmvvmvvvvvmvmv"),
        check_vma=False,
    )
```
